256 devices in a mesh: gx: 2 (over z_hi), gy: 64 (over z_lo, y, x), gz: 2 (over core).
Axes of the slice: x: 4, y: 4, z: 8 (z_hi: 2, z_lo: 4; z = z_hi * 4 + z_lo), core: 2. Of those that a mesh axis runs over, the one named last changes fastest.
Arguments:
- estimate: float32 [256, 64, 4096], P(('gx', 'gy', 'gz')), may hold values from 0.5 to 4
- views_data: bfloat16 [4, 256, 64, 4096], P(None, ('gx', 'gy', 'gz')), may hold values from 0.099609375 to 10
- point_spread: float32 [4, 2, 3, 23], replicated, as said below
- block_owner: int32 [2, 64, 4], replicated, may hold values from -1 to 1, as said below
Outputs:
- updated: float32 [256, 64, 4096], P(('gx', 'gy', 'gz'))
The draws below stay inside these ranges and needn't reach their ends.
Inputs may be any that keep to these rules, and one draw needn't show every extreme that they name: `block_owner`: entry g + s names slot s of the device at position g along gz in the same column (the first two indices are the positions along gx and gy); -1 marks background. Each code appears at most once in a column, the named blocks of a column are consecutive along the third index, and in some column every code from 0 to 1 × (size of gz) − 1 appears. Slots that no entry names are empty and their rows of estimate and views_data are not used. `point_spread`: taps of term 0 are positive.
All inputs are finite; a program needn't handle non-finite values.
Results may differ from the reference program's by a relative error of at most 0.00095.
Values may be sent and summed in bfloat16 or wider, within the bound.
A program may use at most 128 MiB of HBM per device.

```python
import math
import jax
import jax.numpy as jnp
from jax import lax

BLOCK = 64
TAPS = 23
HALO = 11
RANK = 2
VIEWS = 4
SLOTS = 1
PILLAR = 4
SLOT_ROWS = 256
N_GX = 2
N_GY = 64
N_GZ = 2


def draw_point_spread(key, part):
    key_rough, key_sign, key_shift, key_turn = jax.random.split(key, 4)
    array_shape = (VIEWS, RANK, 3, TAPS)
    factor_shape = (VIEWS, RANK, 3, 1)
    rank_index = lax.broadcasted_iota(jnp.int32, array_shape, 1)
    dim_index = lax.broadcasted_iota(jnp.int32, factor_shape, 2)
    tap_index = lax.broadcasted_iota(jnp.int32, array_shape, 3).astype(jnp.float32)
    centre = (TAPS - 1) / 2.0
    lump_width = (TAPS + 9) / 25.0
    lump_mass = lump_width * math.sqrt(2.0 * math.pi)
    rough = jnp.exp(jax.random.uniform(key_rough, array_shape, jnp.float32, math.log(0.5), math.log(2.0)))
    leading_shape = jnp.exp(-jnp.square(tap_index - centre) / (2.0 * lump_width * lump_width)) + 0.04
    leading = 0.75 / (lump_mass + 0.04 * TAPS) * leading_shape * rough
    shift_size = jax.random.uniform(key_shift, factor_shape, jnp.float32, (TAPS + 3) / 10.0, (TAPS + 3) / 4.0)
    shift_sign = (2 * jax.random.randint(key_turn, factor_shape, 0, 2) - 1).astype(jnp.float32)
    offset = shift_size * shift_sign
    sign_draw = (2 * jax.random.randint(key_sign, factor_shape, 0, 2) - 1).astype(jnp.float32)
    paired_sign = sign_draw[:, :, 0:1] * sign_draw[:, :, 1:2]
    factor_sign = jnp.where(dim_index == 2, paired_sign, sign_draw)
    side_shape = jnp.exp(-jnp.square(tap_index - centre - offset) / (2.0 * lump_width * lump_width))
    side = factor_sign * (0.45 / lump_mass) * side_shape * rough
    return jnp.where(rank_index == 0, leading, side)


def draw_block_owner(key, part):
    key_count, key_start, key_order, key_full = jax.random.split(key, 4)
    capacity = SLOTS * N_GZ
    pillars = N_GX * N_GY
    counts = jax.random.randint(key_count, (pillars,), 1, capacity + 1)
    fullest = jax.random.randint(key_full, (), 0, pillars)
    counts = jnp.where(jnp.arange(pillars) == fullest, capacity, counts)
    starts = jax.random.randint(key_start, (pillars,), 0, PILLAR - counts + 1)
    orders = jax.vmap(lambda subkey: jax.random.permutation(subkey, capacity))(jax.random.split(key_order, pillars))
    relative = jnp.arange(PILLAR)[None, :] - starts[:, None]
    tissue = (relative >= 0) & (relative < counts[:, None])
    codes = jnp.take_along_axis(orders, jnp.clip(relative, 0, capacity - 1), axis=1)
    return jnp.where(tissue, codes, -1).reshape(N_GX, N_GY, PILLAR).astype(jnp.int32)


def shard_levels(rng, dims, pieces, least, high):
    level = 1.0
    for dim, parts in pieces:
        steps = jax.random.uniform(jax.random.fold_in(jax.random.fold_in(rng, 6), dim), (parts,), jnp.float32, least / len(pieces), high / len(pieces))
        level = level * jnp.repeat(jnp.exp(steps), dims[dim] // parts).reshape((-1,) + (1,) * (len(dims) - 1 - dim))
    return level


def setup_inputs(seed: int = 0) -> dict:
    keys = jax.random.split(jax.random.key(seed), 5)
    return {
        "estimate": jnp.clip(jnp.exp(math.log(4.0) - 2.0794415 * jax.random.uniform(keys[0], (SLOT_ROWS, BLOCK, BLOCK * BLOCK), jnp.float32) ** shard_levels(keys[0], (SLOT_ROWS, BLOCK, BLOCK * BLOCK), ((0, 256),), -0.2, 0.2)), 0.5, 4.0),
        "views_data": jnp.clip(jnp.exp(math.log(10.0) - 4.609084 * jax.random.uniform(keys[1], (VIEWS, SLOT_ROWS, BLOCK, BLOCK * BLOCK), jnp.float32) ** shard_levels(keys[1], (VIEWS, SLOT_ROWS, BLOCK, BLOCK * BLOCK), ((1, 256),), -0.2, 0.2)), 0.099609375, 10.0).astype(jnp.bfloat16),
        "point_spread": draw_point_spread(jax.random.fold_in(keys[4], 71), 0),
        "block_owner": draw_block_owner(jax.random.fold_in(keys[4], 71), 0),
    }


BLUR_FLOOR = 0.5
HIGHEST_PRECISION = lax.Precision.HIGHEST


def band_matrices(rounded_taps, width, span):
    row_index = lax.broadcasted_iota(jnp.int32, (width, span), 0)
    col_index = lax.broadcasted_iota(jnp.int32, (width, span), 1)
    tap_count = rounded_taps.shape[-1]
    onehot = ((col_index - row_index)[:, :, None] == jnp.arange(tap_count, dtype=jnp.int32)[None, None, :]).astype(jnp.float32)
    matrices = jnp.einsum("vrak,pqk->vrapq", rounded_taps.astype(jnp.float32), onehot, precision=HIGHEST_PRECISION)
    return matrices.astype(jnp.bfloat16)


def forward_blur(extended, matrices):
    first_band = matrices[:, :, 0].astype(jnp.float32)
    second_band = matrices[:, :, 1].astype(jnp.float32)
    third_band = matrices[:, :, 2].astype(jnp.float32)
    first_pass = jnp.einsum("vrpq,qyz->vrpyz", first_band, extended.astype(jnp.float32), precision=HIGHEST_PRECISION).astype(jnp.bfloat16)
    second_pass = jnp.einsum("vrsq,vrpqz->vrpsz", second_band, first_pass.astype(jnp.float32), precision=HIGHEST_PRECISION).astype(jnp.bfloat16)
    return jnp.einsum("vrtq,vrpsq->vpst", third_band, second_pass.astype(jnp.float32), precision=HIGHEST_PRECISION)


def adjoint_blur(ratio_bf, matrices):
    first_band = matrices[:, :, 0].astype(jnp.float32)
    second_band = matrices[:, :, 1].astype(jnp.float32)
    third_band = matrices[:, :, 2].astype(jnp.float32)
    first_pass = jnp.einsum("vrtq,vpst->vrpsq", third_band, ratio_bf.astype(jnp.float32), precision=HIGHEST_PRECISION).astype(jnp.bfloat16)
    second_pass = jnp.einsum("vrsq,vrpsz->vrpqz", second_band, first_pass.astype(jnp.float32), precision=HIGHEST_PRECISION).astype(jnp.bfloat16)
    return jnp.einsum("vrpq,vrpyz->qyz", first_band, second_pass.astype(jnp.float32), precision=HIGHEST_PRECISION)


def source_range(step_value):
    if step_value < 0:
        return 0, HALO
    if step_value == 0:
        return HALO, HALO + BLOCK
    return HALO + BLOCK, 2 * HALO + BLOCK


def target_range(step_value):
    if step_value < 0:
        return BLOCK - HALO, BLOCK
    if step_value == 0:
        return 0, BLOCK
    return 0, HALO


def reference(estimate, views_data, point_spread, block_owner):
    estimate = estimate.reshape(SLOT_ROWS, BLOCK, BLOCK, BLOCK)
    views_data = views_data.reshape(VIEWS, SLOT_ROWS, BLOCK, BLOCK, BLOCK)
    row_count = SLOT_ROWS
    row_index = jnp.arange(row_count, dtype=jnp.int32)
    device_index = row_index // SLOTS
    slot_index = row_index % SLOTS
    plane_x = (device_index // (N_GY * N_GZ)).astype(jnp.int32)
    plane_y = ((device_index // N_GZ) % N_GY).astype(jnp.int32)
    layer_z = device_index % N_GZ
    row_code = layer_z * SLOTS + slot_index
    columns = block_owner[plane_x, plane_y]
    matches = columns == row_code[:, None]
    valid = jnp.any(matches, axis=1)
    depth_index = jnp.arange(PILLAR, dtype=jnp.int32)
    block_height = jnp.sum(jnp.where(matches, depth_index[None, :], 0), axis=1).astype(jnp.int32)
    grid_x = lax.broadcasted_iota(jnp.int32, block_owner.shape, 0)
    grid_y = lax.broadcasted_iota(jnp.int32, block_owner.shape, 1)
    owner_code = jnp.maximum(block_owner, 0)
    row_of_block = jnp.where(block_owner >= 0, ((grid_x * N_GY + grid_y) * N_GZ + owner_code // SLOTS) * SLOTS + owner_code % SLOTS, -1).astype(jnp.int32)
    row_padded = jnp.pad(row_of_block, 1, constant_values=-1)
    field_bf = jnp.where(valid[:, None, None, None], estimate, 0.0).astype(jnp.bfloat16)
    matrices = band_matrices(point_spread.astype(jnp.bfloat16), BLOCK, BLOCK + 2 * HALO)

    def neighbour_rows(number):
        return lax.dynamic_slice(row_padded, (plane_x[number], plane_y[number], block_height[number]), (3, 3, 3))

    def ratio_of_row(number):
        nearby = neighbour_rows(number)
        blocks = field_bf[jnp.clip(nearby, 0, row_count - 1)]
        blocks = jnp.where((nearby >= 0)[:, :, :, None, None, None], blocks, jnp.zeros((), jnp.bfloat16))
        whole = blocks.transpose(0, 3, 1, 4, 2, 5).reshape(3 * BLOCK, 3 * BLOCK, 3 * BLOCK)
        low_edge = BLOCK - HALO
        high_edge = 2 * BLOCK + HALO
        extended = whole[low_edge:high_edge, low_edge:high_edge, low_edge:high_edge]
        blurred = forward_blur(extended, matrices)
        observed = lax.dynamic_index_in_dim(views_data, number, 1, keepdims=False).astype(jnp.float32)
        ratio_value = observed / jnp.maximum(blurred, BLUR_FLOOR)
        return jnp.where(valid[number], ratio_value, 0.0).astype(jnp.bfloat16)

    ratios = lax.map(ratio_of_row, row_index)

    def add_spread(accumulated, number):
        spread_full = adjoint_blur(ratios[number], matrices)
        nearby = neighbour_rows(number)
        for first_step in (-1, 0, 1):
            for second_step in (-1, 0, 1):
                for third_step in (-1, 0, 1):
                    target_row = nearby[first_step + 1, second_step + 1, third_step + 1]
                    source_x = source_range(first_step)
                    source_y = source_range(second_step)
                    source_z = source_range(third_step)
                    target_x = target_range(first_step)
                    target_y = target_range(second_step)
                    target_z = target_range(third_step)
                    portion = spread_full[source_x[0]:source_x[1], source_y[0]:source_y[1], source_z[0]:source_z[1]]
                    portion = jnp.where(target_row >= 0, portion, 0.0)
                    accumulated = accumulated.at[jnp.maximum(target_row, 0), target_x[0]:target_x[1], target_y[0]:target_y[1], target_z[0]:target_z[1]].add(portion)
        return accumulated, None

    accumulated = jnp.zeros((row_count, BLOCK, BLOCK, BLOCK), jnp.float32)
    accumulated = lax.scan(add_spread, accumulated, row_index)[0]
    result = jnp.where(valid[:, None, None, None], estimate * accumulated / VIEWS, 0.0)
    return result.reshape(SLOT_ROWS, BLOCK, BLOCK * BLOCK)
```

```python
import functools

import jax
import jax.numpy as jnp
from jax import lax
from jax.experimental import pallas as pl
from jax.experimental.pallas import tpu as pltpu
from jax.sharding import PartitionSpec as P

MESH = pl.DeviceIdType.MESH
F32, BF16, I32 = jnp.float32, jnp.bfloat16, jnp.int32
BLOCK, TAPS, HALO, RANK, VIEWS, PILLAR = 64, 23, 11, 2, 4, 4
FLOOR = 0.5
SPAN_A = 80
PAIRS = 48
STEP_F, STEP_T, STEP_V = 56, 168, 520
LANES = 128
WIDTH = 768
FACE = 3328


def iota(shape, dim):
    return lax.broadcasted_iota(I32, shape, dim)


def band(distance, tap):
    total = jnp.zeros(distance.shape, F32)
    for t in range(TAPS):
        total = jnp.where(distance == t, tap(t), total)
    return total


def ext_c(lane):
    return jnp.where(lane < 96, lane, lane - LANES)


def parity_b(row):
    return jnp.where(row < 32, 2 * row, 2 * row - 63)


def ext_b(row):
    odd = (row >= PAIRS).astype(I32)
    pair = row - PAIRS * odd
    value = 2 * pair + odd - 88 * (pair >= 38).astype(I32)
    return jnp.where(pair >= 44, 1000, value)


def build_weights(ps, mesh_row, wb, wbt, wc, wct, wa, wat):
    def tap(number, axis):
        return lambda t: ps[(number * 3 + axis) * TAPS + t]

    d_b = ext_b(iota((64, 96), 1)) - parity_b(iota((64, 96), 0)) + HALO
    lane = iota((LANES, LANES), 1)
    d_c = ext_c(iota((LANES, LANES), 0)) - jnp.where(lane >= 64, lane - 64, lane) + HALO
    d_ct = ext_c(iota((64, LANES), 1)) - iota((64, LANES), 0) + HALO
    wct[...] = jnp.zeros_like(wct)

    @pl.loop(0, VIEWS * RANK)
    def _(number):
        start = pl.multiple_of(number * 64, 64)
        wb[pl.ds(start, 64), :] = band(d_b, tap(number, 1)).astype(BF16)
        base = band(d_c, tap(number, 2))
        wc[number, 0:128, :] = jnp.where(lane < 64, base, 0.0).astype(BF16)
        wc[number, 128:256, :] = jnp.where(lane >= 64, base, 0.0).astype(BF16)
        base = band(d_ct, tap(number, 2)).astype(BF16)
        wct[number, 0:64, 0:128] = base
        wct[number, 64:128, 128:256] = base

    col = iota((96, LANES), 1)
    high = col >= 64
    d_bt = ext_b(iota((96, LANES), 0)) - parity_b(jnp.where(high, col - 64, col)) + HALO
    for pair in range(VIEWS * RANK // 2):
        low_tap, high_tap = tap(2 * pair, 1), tap(2 * pair + 1, 1)
        wbt[:, pair * LANES : (pair + 1) * LANES] = band(
            d_bt, lambda t: jnp.where(high, high_tap(t), low_tap(t))
        ).astype(BF16)

    def ext_a(place):
        return place - SPAN_A * (place >= 64).astype(I32) * mesh_row

    second = iota((64, 2 * SPAN_A), 1) >= SPAN_A
    place = iota((64, 2 * SPAN_A), 1) - SPAN_A * second.astype(I32)
    d_a = ext_a(place) - iota((64, 2 * SPAN_A), 0) + HALO
    d_at = ext_a(iota((SPAN_A, 64), 0)) - iota((SPAN_A, 64), 1) + HALO

    @pl.loop(0, VIEWS)
    def _(view):
        first_tap, second_tap = tap(2 * view, 0), tap(2 * view + 1, 0)
        wa[view] = band(d_a, lambda t: jnp.where(second, second_tap(t), first_tap(t))).astype(BF16)
        wat[view, 0:SPAN_A, :] = band(d_at, first_tap).astype(BF16)
        wat[view, SPAN_A : 2 * SPAN_A, :] = band(d_at, second_tap).astype(BF16)


def kernel(
    n_gy,
    est_hbm,
    data_hbm,
    ps,
    owner,
    out,
    est,
    data,
    own,
    sib,
    gx_in,
    gy_in,
    co_in,
    mid_f,
    mix_f,
    rows_t,
    t2,
    v2,
    wb,
    wbt,
    wc,
    wct,
    wa,
    wat,
    keep_gx,
    keep_gy,
    keep_co,
    give_own,
    give_gx,
    give_gy,
    give_co,
    take_own,
    take_gx,
    take_gy,
    take_co,
    put_gx,
    put_gy,
    put_co,
    get_gx,
    get_gy,
    get_co,
    load_sem,
    send_sem,
    recv_sem,
):
    i, j, g = lax.axis_index("gx"), lax.axis_index("gy"), lax.axis_index("gz")
    sibling = (i, j, 1 - g)
    across = (1 - i, j, g)
    beside = ((i, j - 1, g), (i, j + 1, g))
    corner = ((1 - i, j - 1, g), (1 - i, j + 1, g))
    exists = (j > 0, j < n_gy - 1)

    load_est = pltpu.make_async_copy(est_hbm.at[0], est, load_sem.at[0])
    load_data = pltpu.make_async_copy(data_hbm.at[:, 0], data, load_sem.at[1])
    load_est.start()
    load_data.start()

    def copy(number, src, dst, target):
        return pltpu.make_async_remote_copy(
            src_ref=src,
            dst_ref=dst,
            send_sem=send_sem.at[number],
            recv_sem=recv_sem.at[number],
            device_id=target,
            device_id_type=MESH,
        )

    def both_sides(action):
        for side in range(2):

            @pl.when(exists[side])
            def _(side=side):
                action(side)

    barrier = pltpu.get_barrier_semaphore()
    for target in (sibling, across):
        pl.semaphore_signal(barrier, inc=1, device_id=target, device_id_type=MESH)

    def greet(side):
        pl.semaphore_signal(barrier, inc=1, device_id=beside[side], device_id_type=MESH)
        pl.semaphore_signal(barrier, inc=1, device_id=corner[side], device_id_type=MESH)

    both_sides(greet)
    load_est.wait()
    own[...] = est[...].astype(BF16)
    waits = 2 + 2 * exists[0].astype(I32) + 2 * exists[1].astype(I32)
    pl.semaphore_wait(barrier, waits)

    edge = pl.multiple_of(48 * (1 - i), 16)
    my_edge = own.at[pl.ds(edge, 16), :]
    toward = (pl.ds(0, WIDTH), pl.ds(FACE, WIDTH))
    send_sib = copy(0, own, sib, sibling)
    send_gx = copy(1, my_edge, gx_in.at[0], across)
    send_gy = [copy(2 + s, own.at[:, toward[s]], gy_in.at[1 - s, 0], beside[s]) for s in range(2)]
    send_co = [
        copy(4 + s, own.at[pl.ds(edge, 16), toward[s]], co_in.at[1 - s, 0], corner[s])
        for s in range(2)
    ]
    pass_gx = copy(6, gx_in.at[0], gx_in.at[1], sibling)
    pass_gy = [copy(7 + s, gy_in.at[s, 0], gy_in.at[s, 1], sibling) for s in range(2)]
    pass_co = [copy(9 + s, co_in.at[s, 0], co_in.at[s, 1], sibling) for s in range(2)]

    def arrived(number, dst):
        copy(number, dst, dst, sibling).wait_recv()

    send_gx.start()
    both_sides(lambda s: send_co[s].start())
    both_sides(lambda s: send_gy[s].start())
    send_sib.start()

    for side in range(2):

        @pl.when(jnp.logical_not(exists[side]))
        def _(side=side):
            gy_in[side] = jnp.zeros(gy_in.shape[1:], BF16)
            co_in[side] = jnp.zeros(co_in.shape[1:], BF16)

    def column(row, col):
        col = jnp.minimum(jnp.maximum(col, 0), n_gy - 1)
        base = (row * n_gy + col) * PILLAR
        codes = [owner[base + k] for k in range(PILLAR)]
        found = []
        for code in (g, 1 - g):
            hits = [(codes[k] == code).astype(I32) for k in range(PILLAR)]
            found.append((sum(hits), sum(k * hits[k] for k in range(PILLAR))))
        return found

    home = column(i, j)
    valid, height = home[0]

    def factors(entry, there=None):
        present, level = entry
        live = present * valid
        if there is not None:
            live = live * there.astype(I32)
        at = [(live * (level - height == d).astype(I32)).astype(F32) for d in (0, 1, -1)]
        lane_low = (iota((1, LANES), 1) & 63) < 32
        return at[0], jnp.where(lane_low, at[1], at[2])

    f_sib = factors(home[1])
    f_gx = [factors(e) for e in column(1 - i, j)]
    f_gy = [[factors(e, exists[s]) for e in column(i, j + 2 * s - 1)] for s in range(2)]
    f_co = [[factors(e, exists[s]) for e in column(1 - i, j + 2 * s - 1)] for s in range(2)]
    live = valid.astype(F32)

    build_weights(ps, i, wb, wbt, wc, wct, wa, wat)

    def place(first_row, count, pair, mid, mix):
        mid_f[pl.ds(first_row * STEP_F + pair, count, stride=STEP_F), :] = mid
        mix_f[pl.ds(first_row * STEP_F + pair, count, stride=STEP_F), :] = mix

    def tile(number):
        return pl.ds(pl.multiple_of(number * LANES, LANES), LANES)

    def blend(pieces, factor):
        first, second = pieces[0].astype(F32), pieces[1].astype(F32)
        return (
            first * factor[0][0] + second * factor[1][0],
            first * factor[0][1] + second * factor[1][1],
        )

    for pair in range(44, PAIRS):
        place(0, SPAN_A, pair, jnp.zeros((SPAN_A, LANES), F32), jnp.zeros((SPAN_A, LANES), F32))

    first_pair = (38, 32)

    for side in range(2):

        @pl.when(exists[side])
        def _(side=side):
            arrived(3 - side, gy_in.at[side, 0])
            pass_gy[side].start()

    send_sib.wait_recv()

    @pl.loop(0, 32)
    def _(pair):
        place(0, 64, pair, own[:, tile(pair)].astype(F32), sib[:, tile(pair)].astype(F32) * f_sib[1])

    both_sides(lambda s: pass_gy[s].wait_recv())
    for side in range(2):
        for pair in range(6):
            lanes = pl.ds(pair * LANES, LANES)
            mid, mix = blend([gy_in[side, k, :, lanes] for k in range(2)], f_gy[side])
            place(0, 64, first_pair[side] + pair, mid, mix)

    low = iota((PAIRS, LANES), 1) < 64

    def forward_chunk(chunk):
        for two in range(4):
            parts = []
            for one in range(2):
                start = pl.multiple_of((chunk * 8 + two * 2 + one) * STEP_F, 8)
                mid, mix = mid_f[pl.ds(start, PAIRS), :], mix_f[pl.ds(start, PAIRS), :]
                even = jnp.where(low, mid, pltpu.roll(mix, 64, 1))
                odd = jnp.where(low, pltpu.roll(mid, 64, 1), mix)
                parts.append(jnp.concatenate([even, odd], axis=0).astype(BF16))
            first = jnp.dot(wb[...], jnp.concatenate(parts, axis=1), preferred_element_type=F32)
            rows_t[:, two * 256 : two * 256 + 256] = first.astype(BF16)
        for number in range(VIEWS * RANK):
            view, term = number // RANK, number % RANK
            block = jnp.concatenate(
                [
                    jnp.concatenate(
                        [
                            rows_t[number * 64 : number * 64 + 32, a * LANES : (a + 1) * LANES],
                            rows_t[number * 64 + 32 : number * 64 + 64, a * LANES : (a + 1) * LANES],
                        ],
                        axis=1,
                    )
                    for a in range(8)
                ],
                axis=0,
            )
            second = jnp.dot(block, wc[number], preferred_element_type=F32)
            for a in range(8):
                start = view * 32 * STEP_T + term * SPAN_A + chunk * 8 + a
                t2[pl.ds(start, 32, stride=STEP_T), :] = second[a * 32 : a * 32 + 32, :]

    pl.loop(0, 8)(forward_chunk)

    arrived(1, gx_in.at[0])
    pass_gx.start()
    for side in range(2):

        @pl.when(exists[side])
        def _(side=side):
            arrived(5 - side, co_in.at[side, 0])
            pass_co[side].start()

    pass_gx.wait_recv()
    both_sides(lambda s: pass_co[s].wait_recv())

    @pl.loop(0, 32)
    def _(pair):
        mid, mix = blend([gx_in[k, :, tile(pair)] for k in range(2)], f_gx)
        place(64, 16, pair, mid, mix)

    for side in range(2):
        for pair in range(6):
            lanes = pl.ds(pair * LANES, LANES)
            mid, mix = blend([co_in[side, k, :, lanes] for k in range(2)], f_co[side])
            place(64, 16, first_pair[side] + pair, mid, mix)

    pl.loop(8, 10)(forward_chunk)
    load_data.wait()

    def turn(step):
        view, two = step // 16, step % 16
        start = pl.multiple_of((view * 32 + two * 2) * STEP_T, 8)
        fields = jnp.concatenate(
            [t2[pl.ds(start + k * STEP_T, 2 * SPAN_A), :].astype(BF16) for k in range(2)], axis=1
        )
        blurred = jnp.dot(wa[view], fields, preferred_element_type=F32)
        observed = data[view, :, pl.ds(pl.multiple_of(two * 256, 256), 256)].astype(F32)
        ratio = (observed / jnp.maximum(blurred, FLOOR) * live).astype(BF16)
        back = jnp.dot(wat[view], ratio, preferred_element_type=F32).astype(BF16)
        for term in range(RANK):
            rows = back[term * SPAN_A : (term + 1) * SPAN_A]
            block = jnp.concatenate([rows[:, :LANES], rows[:, LANES:]], axis=0)
            wide = jnp.dot(block, wct[view * RANK + term], preferred_element_type=F32)
            for k in range(2):
                for odd in range(2):
                    at = (view * RANK + term) * 64 + odd * 32 + two * 2 + k
                    v2[pl.ds(at, SPAN_A, stride=STEP_V), :] = wide[
                        k * SPAN_A : (k + 1) * SPAN_A, odd * LANES : (odd + 1) * LANES
                    ]

    pl.loop(0, 64)(turn)

    def adjoint_pair(step):
        start = pl.multiple_of(step * 2 * STEP_V, 8)
        fields = jnp.concatenate(
            [v2[pl.ds(start + k * STEP_V, 512), :].astype(BF16) for k in range(2)], axis=1
        )
        spread = jnp.dot(wbt[...], fields, preferred_element_type=F32)
        for k in range(2):
            even = spread[0:PAIRS, k * LANES : (k + 1) * LANES]
            odd = spread[PAIRS : 2 * PAIRS, k * LANES : (k + 1) * LANES]
            at = pl.multiple_of((step * 2 + k) * STEP_F, 8)
            mid_f[pl.ds(at, PAIRS), :] = jnp.where(low, even, pltpu.roll(odd, 64, 1))
            mix_f[pl.ds(at, PAIRS), :] = jnp.where(low, pltpu.roll(even, 64, 1), odd)

    def fetch(first_row, count, pair):
        at = pl.ds(first_row * STEP_F + pair, count, stride=STEP_F)
        return mid_f[at, :], mix_f[at, :]

    pl.loop(32, 40)(adjoint_pair)

    @pl.loop(0, 32)
    def _(pair):
        mid, mix = fetch(64, 16, pair)
        keep_gx[:, tile(pair)] = mid * f_gx[0][0] + mix * f_gx[0][1]
        give_gx[:, tile(pair)] = (mid * f_gx[1][0] + mix * f_gx[1][1]).astype(BF16)

    for side in range(2):
        for pair in range(6):
            lanes = pl.ds(pair * LANES, LANES)
            mid, mix = fetch(64, 16, first_pair[side] + pair)
            one, two = f_co[side]
            keep_co[side, :, lanes] = mid * one[0] + mix * one[1]
            give_co[side, :, lanes] = (mid * two[0] + mix * two[1]).astype(BF16)

    share_gx = copy(11, give_gx, take_gx, sibling)
    share_co = copy(12, give_co, take_co, sibling)
    share_gx.start()
    share_co.start()
    pl.loop(0, 8)(adjoint_pair)
    share_gx.wait_recv()
    share_co.wait_recv()
    put_gx[...] = (keep_gx[...] + take_gx[...].astype(F32)).astype(BF16)
    put_co[...] = (keep_co[...] + take_co[...].astype(F32)).astype(BF16)
    final_gx = copy(13, put_gx, get_gx, across)
    final_co = [copy(14 + s, put_co.at[s], get_co.at[1 - s], corner[s]) for s in range(2)]
    final_gx.start()
    both_sides(lambda s: final_co[s].start())
    pl.loop(8, 32)(adjoint_pair)

    for side in range(2):
        for pair in range(6):
            lanes = pl.ds(pair * LANES, LANES)
            mid, mix = fetch(0, 64, first_pair[side] + pair)
            one, two = f_gy[side]
            keep_gy[side, :, lanes] = mid * one[0] + mix * one[1]
            give_gy[side, :, lanes] = (mid * two[0] + mix * two[1]).astype(BF16)

    share_gy = copy(16, give_gy, take_gy, sibling)
    share_gy.start()

    @pl.loop(0, 32)
    def _(pair):
        mid, mix = fetch(0, 64, pair)
        out[0, :, tile(pair)] = mid
        give_own[:, tile(pair)] = (mix * f_sib[1]).astype(BF16)

    share_own = copy(17, give_own, take_own, sibling)
    share_own.start()
    share_gy.wait_recv()
    put_gy[...] = (keep_gy[...] + take_gy[...].astype(F32)).astype(BF16)
    final_gy = [copy(18 + s, put_gy.at[s], get_gy.at[1 - s], beside[s]) for s in range(2)]
    both_sides(lambda s: final_gy[s].start())

    share_own.wait_recv()
    out[0] = out[0] + take_own[...].astype(F32)
    final_gx.wait_recv()
    out[0, pl.ds(edge, 16), :] = out[0, pl.ds(edge, 16), :] + get_gx[...].astype(F32)
    for side in range(2):

        @pl.when(exists[side])
        def _(side=side):
            arrived(15 - side, get_co.at[side])
            arrived(19 - side, get_gy.at[side])
            out[0, :, toward[side]] = out[0, :, toward[side]] + get_gy[side].astype(F32)
            out[0, pl.ds(edge, 16), toward[side]] = out[0, pl.ds(edge, 16), toward[side]] + get_co[
                side
            ].astype(F32)

    out[0] = est[...] * out[0] * (live / VIEWS)

    for item in (send_sib, send_gx, pass_gx, share_gx, share_co, final_gx, share_gy, share_own):
        item.wait_send()

    def drain(side):
        for group in (send_gy, send_co, pass_gy, pass_co, final_co, final_gy):
            group[side].wait_send()

    both_sides(drain)


def solution(mesh):
    n_gy = mesh.shape["gy"]

    def body(estimate, views_data, point_spread, block_owner):
        slab, side, small = (16, 4096), (2, 64, WIDTH), (2, 16, WIDTH)
        scratch = [
            ((64, 4096), F32),
            ((VIEWS, 64, 4096), BF16),
            ((64, 4096), BF16),
            ((64, 4096), BF16),
            ((2, 16, 4096), BF16),
            ((2, 2, 64, WIDTH), BF16),
            ((2, 2, 16, WIDTH), BF16),
            ((SPAN_A * STEP_F, LANES), F32),
            ((SPAN_A * STEP_F, LANES), F32),
            ((512, 1024), BF16),
            ((VIEWS * 32 * STEP_T, LANES), F32),
            ((SPAN_A * STEP_V, LANES), F32),
            ((512, 96), BF16),
            ((96, 512), BF16),
            ((8, 256, 128), BF16),
            ((8, 128, 256), BF16),
            ((VIEWS, 64, 2 * SPAN_A), BF16),
            ((VIEWS, 2 * SPAN_A, 64), BF16),
            (slab, F32),
            (side, F32),
            (small, F32),
            ((64, 4096), BF16),
            (slab, BF16),
            (side, BF16),
            (small, BF16),
            ((64, 4096), BF16),
            (slab, BF16),
            (side, BF16),
            (small, BF16),
            (slab, BF16),
            (side, BF16),
            (small, BF16),
            (slab, BF16),
            (side, BF16),
            (small, BF16),
        ]
        any_spec = pl.BlockSpec(memory_space=pl.ANY)
        smem = pl.BlockSpec(memory_space=pltpu.SMEM)
        return pl.pallas_call(
            functools.partial(kernel, n_gy),
            out_shape=jax.ShapeDtypeStruct((1, 64, 4096), F32),
            in_specs=[any_spec, any_spec, smem, smem],
            out_specs=pl.BlockSpec(memory_space=pltpu.VMEM),
            scratch_shapes=[pltpu.VMEM(shape, kind) for shape, kind in scratch]
            + [
                pltpu.SemaphoreType.DMA((2,)),
                pltpu.SemaphoreType.DMA((20,)),
                pltpu.SemaphoreType.DMA((20,)),
            ],
            compiler_params=pltpu.CompilerParams(
                collective_id=0, has_side_effects=True, vmem_limit_bytes=60 * 2**20
            ),
        )(estimate, views_data, point_spread.reshape(-1), block_owner.reshape(-1))

    placed = (P(("gx", "gy", "gz"), None, None), P(None, ("gx", "gy", "gz"), None, None), P(), P())
    return jax.shard_map(
        body,
        mesh=mesh,
        in_specs=placed,
        out_specs=P(("gx", "gy", "gz"), None, None),
        check_vma=False,
    )
```

```python
import functools

import jax
import jax.numpy as jnp
from jax import lax
from jax.experimental import pallas as pl
from jax.experimental.pallas import tpu as pltpu
from jax.sharding import PartitionSpec as P

MESH = pl.DeviceIdType.MESH
F32, BF16, I32 = jnp.float32, jnp.bfloat16, jnp.int32
BLOCK, TAPS, HALO, RANK, VIEWS, PILLAR = 64, 23, 11, 2, 4, 4
FLOOR = 0.5
SPAN_A = 80
PAIRS = 48
STEP_F, STEP_T, STEP_V = 56, 168, 520
LANES = 128
WIDTH = 768
FACE = 3328
TURN = 32
CHUNK = 16
DUO = 16


def iota(shape, dim):
    return lax.broadcasted_iota(I32, shape, dim)


def band(distance, tap):
    total = jnp.zeros(distance.shape, F32)
    for t in range(TAPS):
        total = jnp.where(distance == t, tap(t), total)
    return total


def ext_c(lane):
    return jnp.where(lane < 96, lane, lane - LANES)


def parity_b(row):
    return jnp.where(row < 32, 2 * row, 2 * row - 63)


def ext_b(row):
    odd = (row >= PAIRS).astype(I32)
    pair = row - PAIRS * odd
    value = 2 * pair + odd - 88 * (pair >= 38).astype(I32)
    return jnp.where(pair >= 44, 1000, value)


def build_weights(ps, mesh_row, wb, wbt, wc, wct, wa, wat):
    def tap(number, axis):
        return lambda t: ps[number // RANK, axis, number % RANK, t]

    d_b = ext_b(iota((64, 96), 1)) - parity_b(iota((64, 96), 0)) + HALO
    lane = iota((LANES, LANES), 1)
    d_c = ext_c(iota((LANES, LANES), 0)) - jnp.where(lane >= 64, lane - 64, lane) + HALO
    d_ct = ext_c(iota((64, LANES), 1)) - iota((64, LANES), 0) + HALO
    wct[...] = jnp.zeros_like(wct)

    @pl.loop(0, VIEWS * RANK)
    def _(number):
        start = pl.multiple_of(number * 64, 64)
        wb[pl.ds(start, 64), :] = band(d_b, tap(number, 1)).astype(BF16)
        base = band(d_c, tap(number, 2))
        wc[number, 0:128, :] = jnp.where(lane < 64, base, 0.0).astype(BF16)
        wc[number, 128:256, :] = jnp.where(lane >= 64, base, 0.0).astype(BF16)
        base = band(d_ct, tap(number, 2)).astype(BF16)
        wct[number, 0:64, 0:128] = base
        wct[number, 64:128, 128:256] = base

    col = iota((96, LANES), 1)
    high = col >= 64
    d_bt = ext_b(iota((96, LANES), 0)) - parity_b(jnp.where(high, col - 64, col)) + HALO
    for pair in range(VIEWS * RANK // 2):
        low_tap, high_tap = tap(2 * pair, 1), tap(2 * pair + 1, 1)
        wbt[:, pair * LANES : (pair + 1) * LANES] = band(
            d_bt, lambda t: jnp.where(high, high_tap(t), low_tap(t))
        ).astype(BF16)

    def ext_a(place):
        return place - SPAN_A * (place >= 64).astype(I32) * mesh_row

    second = iota((64, 2 * SPAN_A), 1) >= SPAN_A
    place = iota((64, 2 * SPAN_A), 1) - SPAN_A * second.astype(I32)
    d_a = ext_a(place) - iota((64, 2 * SPAN_A), 0) + HALO
    d_at = ext_a(iota((SPAN_A, 64), 0)) - iota((SPAN_A, 64), 1) + HALO

    @pl.loop(0, VIEWS)
    def _(view):
        first_tap, second_tap = tap(2 * view, 0), tap(2 * view + 1, 0)
        wa[view] = band(d_a, lambda t: jnp.where(second, second_tap(t), first_tap(t))).astype(BF16)
        wat[view, 0:SPAN_A, :] = band(d_at, first_tap).astype(BF16)
        wat[view, SPAN_A : 2 * SPAN_A, :] = band(d_at, second_tap).astype(BF16)


def kernel(
    n_gy,
    est_hbm,
    data_hbm,
    ps,
    owner,
    out,
    est,
    data,
    own,
    sib,
    gx_in,
    gy_in,
    co_in,
    mid_f,
    mix_f,
    rows_t,
    t2,
    v2,
    wb,
    wbt,
    wc,
    wct,
    wa,
    wat,
    keep_gx,
    keep_gy,
    keep_co,
    give_own,
    give_gx,
    give_gy,
    give_co,
    take_own,
    take_gx,
    take_gy,
    take_co,
    put_gx,
    put_gy,
    put_co,
    get_gx,
    get_gy,
    get_co,
    load_sem,
    send_sem,
    recv_sem,
):
    i, j, g = lax.axis_index("gx"), lax.axis_index("gy"), lax.axis_index("gz")
    sibling = (i, j, 1 - g)
    across = (1 - i, j, g)
    beside = ((i, j - 1, g), (i, j + 1, g))
    corner = ((1 - i, j - 1, g), (1 - i, j + 1, g))
    exists = (j > 0, j < n_gy - 1)

    load_est = pltpu.make_async_copy(est_hbm.at[0], est, load_sem.at[0])
    load_data = pltpu.make_async_copy(data_hbm.at[:, 0], data, load_sem.at[1])
    load_est.start()
    load_data.start()

    def copy(number, src, dst, target):
        return pltpu.make_async_remote_copy(
            src_ref=src,
            dst_ref=dst,
            send_sem=send_sem.at[number],
            recv_sem=recv_sem.at[number],
            device_id=target,
            device_id_type=MESH,
        )

    def both_sides(action):
        for side in range(2):

            @pl.when(exists[side])
            def _(side=side):
                action(side)

    barrier = pltpu.get_barrier_semaphore()
    for target in (sibling, across):
        pl.semaphore_signal(barrier, inc=1, device_id=target, device_id_type=MESH)

    def greet(side):
        pl.semaphore_signal(barrier, inc=1, device_id=beside[side], device_id_type=MESH)
        pl.semaphore_signal(barrier, inc=1, device_id=corner[side], device_id_type=MESH)

    both_sides(greet)
    load_est.wait()
    own[...] = est[...].astype(BF16)
    waits = 2 + 2 * exists[0].astype(I32) + 2 * exists[1].astype(I32)
    pl.semaphore_wait(barrier, waits)

    edge = pl.multiple_of(48 * (1 - i), 16)
    my_edge = own.at[pl.ds(edge, 16), :]
    toward = (pl.ds(0, WIDTH), pl.ds(FACE, WIDTH))
    send_sib = copy(0, own, sib, sibling)
    send_gx = copy(1, my_edge, gx_in.at[0], across)
    send_gy = [copy(2 + s, own.at[:, toward[s]], gy_in.at[1 - s, 0], beside[s]) for s in range(2)]
    send_co = [
        copy(4 + s, own.at[pl.ds(edge, 16), toward[s]], co_in.at[1 - s, 0], corner[s])
        for s in range(2)
    ]
    pass_gx = copy(6, gx_in.at[0], gx_in.at[1], sibling)
    pass_gy = [copy(7 + s, gy_in.at[s, 0], gy_in.at[s, 1], sibling) for s in range(2)]
    pass_co = [copy(9 + s, co_in.at[s, 0], co_in.at[s, 1], sibling) for s in range(2)]

    def arrived(number, dst):
        copy(number, dst, dst, sibling).wait_recv()

    send_gx.start()
    both_sides(lambda s: send_co[s].start())
    both_sides(lambda s: send_gy[s].start())
    send_sib.start()

    for side in range(2):

        @pl.when(jnp.logical_not(exists[side]))
        def _(side=side):
            gy_in[side] = jnp.zeros(gy_in.shape[1:], BF16)
            co_in[side] = jnp.zeros(co_in.shape[1:], BF16)

    def column(row, col):
        col = jnp.minimum(jnp.maximum(col, 0), n_gy - 1)
        codes = [owner[row, k, col] for k in range(PILLAR)]
        found = []
        for code in (g, 1 - g):
            hits = [(codes[k] == code).astype(I32) for k in range(PILLAR)]
            found.append((sum(hits), sum(k * hits[k] for k in range(PILLAR))))
        return found

    home = column(i, j)
    valid, height = home[0]

    def factors(entry, there=None):
        present, level = entry
        live = present * valid
        if there is not None:
            live = live * there.astype(I32)
        at = [(live * (level - height == d).astype(I32)).astype(F32) for d in (0, 1, -1)]
        lane_low = (iota((1, LANES), 1) & 63) < 32
        return at[0], jnp.where(lane_low, at[1], at[2])

    f_sib = factors(home[1])
    f_gx = [factors(e) for e in column(1 - i, j)]
    f_gy = [[factors(e, exists[s]) for e in column(i, j + 2 * s - 1)] for s in range(2)]
    f_co = [[factors(e, exists[s]) for e in column(1 - i, j + 2 * s - 1)] for s in range(2)]
    live = valid.astype(F32)

    build_weights(ps, i, wb, wbt, wc, wct, wa, wat)

    def place(first_row, count, pair, mid, mix):
        mid_f[pl.ds(first_row * STEP_F + pair, count, stride=STEP_F), :] = mid
        mix_f[pl.ds(first_row * STEP_F + pair, count, stride=STEP_F), :] = mix

    def tile(number):
        return pl.ds(pl.multiple_of(number * LANES, LANES), LANES)

    def blend(pieces, factor):
        first, second = pieces[0].astype(F32), pieces[1].astype(F32)
        return (
            first * factor[0][0] + second * factor[1][0],
            first * factor[0][1] + second * factor[1][1],
        )

    for pair in range(44, PAIRS):
        place(0, SPAN_A, pair, jnp.zeros((SPAN_A, LANES), F32), jnp.zeros((SPAN_A, LANES), F32))

    first_pair = (38, 32)

    for side in range(2):

        @pl.when(exists[side])
        def _(side=side):
            arrived(3 - side, gy_in.at[side, 0])
            pass_gy[side].start()

    send_sib.wait_recv()

    @pl.loop(0, 32)
    def _(pair):
        place(0, 64, pair, own[:, tile(pair)].astype(F32), sib[:, tile(pair)].astype(F32) * f_sib[1])

    both_sides(lambda s: pass_gy[s].wait_recv())
    for side in range(2):
        for pair in range(6):
            lanes = pl.ds(pair * LANES, LANES)
            mid, mix = blend([gy_in[side, k, :, lanes] for k in range(2)], f_gy[side])
            place(0, 64, first_pair[side] + pair, mid, mix)

    low = iota((PAIRS, LANES), 1) < 64

    def forward_chunk(chunk):
        for two in range(CHUNK // 2):
            parts = []
            for one in range(2):
                start = pl.multiple_of((chunk * CHUNK + two * 2 + one) * STEP_F, 8)
                mid, mix = mid_f[pl.ds(start, PAIRS), :], mix_f[pl.ds(start, PAIRS), :]
                even = jnp.where(low, mid, pltpu.roll(mix, 64, 1))
                odd = jnp.where(low, pltpu.roll(mid, 64, 1), mix)
                parts.append(jnp.concatenate([even, odd], axis=0).astype(BF16))
            first = jnp.dot(wb[...], jnp.concatenate(parts, axis=1), preferred_element_type=F32)
            rows_t[:, two * 256 : two * 256 + 256] = first.astype(BF16)
        for number in range(VIEWS * RANK):
            view, term = number // RANK, number % RANK
            top = number * 64
            block = jnp.concatenate(
                [
                    jnp.concatenate(
                        [
                            rows_t[top : top + 32, a * LANES : (a + 1) * LANES],
                            rows_t[top + 32 : top + 64, a * LANES : (a + 1) * LANES],
                        ],
                        axis=1,
                    )
                    for a in range(CHUNK)
                ],
                axis=0,
            )
            second = jnp.dot(block, wc[number], preferred_element_type=F32)
            for a in range(CHUNK):
                start = view * 32 * STEP_T + term * SPAN_A + chunk * CHUNK + a
                t2[pl.ds(start, 32, stride=STEP_T), :] = second[a * 32 : a * 32 + 32, :]

    pl.loop(0, 64 // CHUNK)(forward_chunk)

    arrived(1, gx_in.at[0])
    pass_gx.start()
    for side in range(2):

        @pl.when(exists[side])
        def _(side=side):
            arrived(5 - side, co_in.at[side, 0])
            pass_co[side].start()

    pass_gx.wait_recv()
    both_sides(lambda s: pass_co[s].wait_recv())

    @pl.loop(0, 32)
    def _(pair):
        mid, mix = blend([gx_in[k, :, tile(pair)] for k in range(2)], f_gx)
        place(64, 16, pair, mid, mix)

    for side in range(2):
        for pair in range(6):
            lanes = pl.ds(pair * LANES, LANES)
            mid, mix = blend([co_in[side, k, :, lanes] for k in range(2)], f_co[side])
            place(64, 16, first_pair[side] + pair, mid, mix)

    pl.loop(64 // CHUNK, SPAN_A // CHUNK)(forward_chunk)
    load_data.wait()

    def turn(step):
        view, group = step // (32 // TURN), step % (32 // TURN)
        start = pl.multiple_of((view * 32 + group * TURN) * STEP_T, 8)
        fields = jnp.concatenate(
            [t2[pl.ds(start + k * STEP_T, 2 * SPAN_A), :].astype(BF16) for k in range(TURN)], axis=1
        )
        blurred = jnp.dot(wa[view], fields, preferred_element_type=F32)
        lanes = pl.ds(pl.multiple_of(group * (TURN * LANES), TURN * LANES), TURN * LANES)
        ratio = (data[view, :, lanes].astype(F32) / jnp.maximum(blurred, FLOOR) * live).astype(BF16)
        back = jnp.dot(wat[view], ratio, preferred_element_type=F32).astype(BF16)
        for term in range(RANK):
            rows = back[term * SPAN_A : (term + 1) * SPAN_A]
            block = jnp.concatenate(
                [rows[:, k * LANES : (k + 1) * LANES] for k in range(TURN)], axis=0
            )
            wide = jnp.dot(block, wct[view * RANK + term], preferred_element_type=F32)
            for k in range(TURN):
                for odd in range(2):
                    at = (view * RANK + term) * 64 + odd * 32 + group * TURN + k
                    v2[pl.ds(at, SPAN_A, stride=STEP_V), :] = wide[
                        k * SPAN_A : (k + 1) * SPAN_A, odd * LANES : (odd + 1) * LANES
                    ]

    pl.loop(0, VIEWS * 32 // TURN)(turn)

    def adjoint_rows(step):
        start = pl.multiple_of(step * DUO * STEP_V, 8)
        fields = jnp.concatenate(
            [v2[pl.ds(start + k * STEP_V, 512), :].astype(BF16) for k in range(DUO)], axis=1
        )
        spread = jnp.dot(wbt[...], fields, preferred_element_type=F32)
        for k in range(DUO):
            even = spread[0:PAIRS, k * LANES : (k + 1) * LANES]
            odd = spread[PAIRS : 2 * PAIRS, k * LANES : (k + 1) * LANES]
            at = pl.multiple_of((step * DUO + k) * STEP_F, 8)
            mid_f[pl.ds(at, PAIRS), :] = jnp.where(low, even, pltpu.roll(odd, 64, 1))
            mix_f[pl.ds(at, PAIRS), :] = jnp.where(low, pltpu.roll(even, 64, 1), odd)

    def fetch(first_row, count, pair):
        at = pl.ds(first_row * STEP_F + pair, count, stride=STEP_F)
        return mid_f[at, :], mix_f[at, :]

    pl.loop(64 // DUO, SPAN_A // DUO)(adjoint_rows)

    @pl.loop(0, 32)
    def _(pair):
        mid, mix = fetch(64, 16, pair)
        keep_gx[:, tile(pair)] = mid * f_gx[0][0] + mix * f_gx[0][1]
        give_gx[:, tile(pair)] = (mid * f_gx[1][0] + mix * f_gx[1][1]).astype(BF16)

    for side in range(2):
        for pair in range(6):
            lanes = pl.ds(pair * LANES, LANES)
            mid, mix = fetch(64, 16, first_pair[side] + pair)
            one, two = f_co[side]
            keep_co[side, :, lanes] = mid * one[0] + mix * one[1]
            give_co[side, :, lanes] = (mid * two[0] + mix * two[1]).astype(BF16)

    share_gx = copy(11, give_gx, take_gx, sibling)
    share_co = copy(12, give_co, take_co, sibling)
    share_gx.start()
    share_co.start()
    pl.loop(0, 16 // DUO)(adjoint_rows)
    share_gx.wait_recv()
    share_co.wait_recv()
    put_gx[...] = (keep_gx[...] + take_gx[...].astype(F32)).astype(BF16)
    put_co[...] = (keep_co[...] + take_co[...].astype(F32)).astype(BF16)
    final_gx = copy(13, put_gx, get_gx, across)
    final_co = [copy(14 + s, put_co.at[s], get_co.at[1 - s], corner[s]) for s in range(2)]
    final_gx.start()
    both_sides(lambda s: final_co[s].start())
    pl.loop(16 // DUO, 64 // DUO)(adjoint_rows)

    for side in range(2):
        for pair in range(6):
            lanes = pl.ds(pair * LANES, LANES)
            mid, mix = fetch(0, 64, first_pair[side] + pair)
            one, two = f_gy[side]
            keep_gy[side, :, lanes] = mid * one[0] + mix * one[1]
            give_gy[side, :, lanes] = (mid * two[0] + mix * two[1]).astype(BF16)

    share_gy = copy(16, give_gy, take_gy, sibling)
    share_gy.start()

    @pl.loop(0, 32)
    def _(pair):
        mid, mix = fetch(0, 64, pair)
        out[0, :, tile(pair)] = mid
        give_own[:, tile(pair)] = (mix * f_sib[1]).astype(BF16)

    share_own = copy(17, give_own, take_own, sibling)
    share_own.start()
    share_gy.wait_recv()
    put_gy[...] = (keep_gy[...] + take_gy[...].astype(F32)).astype(BF16)
    final_gy = [copy(18 + s, put_gy.at[s], get_gy.at[1 - s], beside[s]) for s in range(2)]
    both_sides(lambda s: final_gy[s].start())

    share_own.wait_recv()
    out[0] = out[0] + take_own[...].astype(F32)
    final_gx.wait_recv()
    out[0, pl.ds(edge, 16), :] = out[0, pl.ds(edge, 16), :] + get_gx[...].astype(F32)
    for side in range(2):

        @pl.when(exists[side])
        def _(side=side):
            arrived(15 - side, get_co.at[side])
            arrived(19 - side, get_gy.at[side])
            out[0, :, toward[side]] = out[0, :, toward[side]] + get_gy[side].astype(F32)
            out[0, pl.ds(edge, 16), toward[side]] = out[0, pl.ds(edge, 16), toward[side]] + get_co[
                side
            ].astype(F32)

    out[0] = est[...] * out[0] * (live / VIEWS)

    for item in (send_sib, send_gx, pass_gx, share_gx, share_co, final_gx, share_gy, share_own):
        item.wait_send()

    def drain(side):
        for group in (send_gy, send_co, pass_gy, pass_co, final_co, final_gy):
            group[side].wait_send()

    both_sides(drain)


def solution(mesh):
    n_gy = mesh.shape["gy"]

    def body(estimate, views_data, point_spread, block_owner):
        slab, side, small = (16, 4096), (2, 64, WIDTH), (2, 16, WIDTH)
        scratch = [
            ((64, 4096), F32),
            ((VIEWS, 64, 4096), BF16),
            ((64, 4096), BF16),
            ((64, 4096), BF16),
            ((2, 16, 4096), BF16),
            ((2, 2, 64, WIDTH), BF16),
            ((2, 2, 16, WIDTH), BF16),
            ((SPAN_A * STEP_F, LANES), F32),
            ((SPAN_A * STEP_F, LANES), F32),
            ((512, CHUNK * LANES), BF16),
            ((VIEWS * 32 * STEP_T, LANES), F32),
            ((SPAN_A * STEP_V, LANES), F32),
            ((512, 96), BF16),
            ((96, 512), BF16),
            ((8, 256, 128), BF16),
            ((8, 128, 256), BF16),
            ((VIEWS, 64, 2 * SPAN_A), BF16),
            ((VIEWS, 2 * SPAN_A, 64), BF16),
            (slab, F32),
            (side, F32),
            (small, F32),
            ((64, 4096), BF16),
            (slab, BF16),
            (side, BF16),
            (small, BF16),
            ((64, 4096), BF16),
            (slab, BF16),
            (side, BF16),
            (small, BF16),
            (slab, BF16),
            (side, BF16),
            (small, BF16),
            (slab, BF16),
            (side, BF16),
            (small, BF16),
        ]
        any_spec = pl.BlockSpec(memory_space=pl.ANY)
        smem = pl.BlockSpec(memory_space=pltpu.SMEM)
        return pl.pallas_call(
            functools.partial(kernel, n_gy),
            out_shape=jax.ShapeDtypeStruct((1, 64, 4096), F32),
            in_specs=[any_spec, any_spec, smem, smem],
            out_specs=pl.BlockSpec(memory_space=pltpu.VMEM),
            scratch_shapes=[pltpu.VMEM(shape, kind) for shape, kind in scratch]
            + [
                pltpu.SemaphoreType.DMA((2,)),
                pltpu.SemaphoreType.DMA((20,)),
                pltpu.SemaphoreType.DMA((20,)),
            ],
            compiler_params=pltpu.CompilerParams(
                collective_id=0, has_side_effects=True, vmem_limit_bytes=60 * 2**20
            ),
        )(
            estimate,
            views_data,
            point_spread.transpose(0, 2, 1, 3),
            block_owner.transpose(0, 2, 1),
        )

    placed = (P(("gx", "gy", "gz"), None, None), P(None, ("gx", "gy", "gz"), None, None), P(), P())
    return jax.shard_map(
        body,
        mesh=mesh,
        in_specs=placed,
        out_specs=P(("gx", "gy", "gz"), None, None),
        check_vma=False,
    )
```

```python
import functools

import jax
import jax.numpy as jnp
from jax import lax
from jax.experimental import pallas as pl
from jax.experimental.pallas import tpu as pltpu
from jax.sharding import PartitionSpec as P

MESH = pl.DeviceIdType.MESH
F32, BF16, I32 = jnp.float32, jnp.bfloat16, jnp.int32
BLOCK, TAPS, HALO, RANK, VIEWS, PILLAR = 64, 23, 11, 2, 4, 4
FLOOR = 0.5
SPAN_A = 80
PAIRS = 48
STEP_F, STEP_T, STEP_V = 56, 168, 520
LANES = 128
WIDTH = 768
FACE = 3328
QUARTER = 1024
TURN = 32
CHUNK = 16
DUO = 16


def iota(shape, dim):
    return lax.broadcasted_iota(I32, shape, dim)


def band(distance, tap):
    total = jnp.zeros(distance.shape, F32)
    for t in range(TAPS):
        total = jnp.where(distance == t, tap(t), total)
    return total


def ext_c(lane):
    return jnp.where(lane < 96, lane, lane - LANES)


def parity_b(row):
    return jnp.where(row < 32, 2 * row, 2 * row - 63)


def ext_b(row):
    odd = (row >= PAIRS).astype(I32)
    pair = row - PAIRS * odd
    value = 2 * pair + odd - 88 * (pair >= 38).astype(I32)
    return jnp.where(pair >= 44, 1000, value)


def tap_of(ps):
    def tap(number, axis):
        return lambda t: ps[number // RANK, axis, number % RANK, t]

    return tap


def build_forward(ps, wb, wc):
    tap = tap_of(ps)
    d_b = ext_b(iota((64, 96), 1)) - parity_b(iota((64, 96), 0)) + HALO
    lane = iota((LANES, LANES), 1)
    d_c = ext_c(iota((LANES, LANES), 0)) - jnp.where(lane >= 64, lane - 64, lane) + HALO

    @pl.loop(0, VIEWS * RANK)
    def _(number):
        start = pl.multiple_of(number * 64, 64)
        wb[pl.ds(start, 64), :] = band(d_b, tap(number, 1)).astype(BF16)
        base = band(d_c, tap(number, 2))
        wc[number, 0:128, :] = jnp.where(lane < 64, base, 0.0).astype(BF16)
        wc[number, 128:256, :] = jnp.where(lane >= 64, base, 0.0).astype(BF16)


def build_rest(ps, mesh_row, wbt, wct, wa, wat):
    tap = tap_of(ps)
    d_ct = ext_c(iota((64, LANES), 1)) - iota((64, LANES), 0) + HALO
    wct[...] = jnp.zeros_like(wct)

    @pl.loop(0, VIEWS * RANK)
    def _(number):
        base = band(d_ct, tap(number, 2)).astype(BF16)
        wct[number, 0:64, 0:128] = base
        wct[number, 64:128, 128:256] = base

    col = iota((96, LANES), 1)
    high = col >= 64
    d_bt = ext_b(iota((96, LANES), 0)) - parity_b(jnp.where(high, col - 64, col)) + HALO
    for pair in range(VIEWS * RANK // 2):
        low_tap, high_tap = tap(2 * pair, 1), tap(2 * pair + 1, 1)
        wbt[:, pair * LANES : (pair + 1) * LANES] = band(
            d_bt, lambda t: jnp.where(high, high_tap(t), low_tap(t))
        ).astype(BF16)

    def ext_a(place):
        inside = place - (64 + HALO) * (place >= 64).astype(I32) * mesh_row
        return jnp.where(place >= 64 + HALO, 1000, inside)

    second = iota((64, 2 * SPAN_A), 1) >= SPAN_A
    place = iota((64, 2 * SPAN_A), 1) - SPAN_A * second.astype(I32)
    d_a = ext_a(place) - iota((64, 2 * SPAN_A), 0) + HALO
    d_at = ext_a(iota((SPAN_A, 64), 0)) - iota((SPAN_A, 64), 1) + HALO

    @pl.loop(0, VIEWS)
    def _(view):
        first_tap, second_tap = tap(2 * view, 0), tap(2 * view + 1, 0)
        wa[view] = band(d_a, lambda t: jnp.where(second, second_tap(t), first_tap(t))).astype(BF16)
        wat[view, 0:SPAN_A, :] = band(d_at, first_tap).astype(BF16)
        wat[view, SPAN_A : 2 * SPAN_A, :] = band(d_at, second_tap).astype(BF16)


def kernel(
    n_gy,
    est_hbm,
    data_hbm,
    ps,
    owner,
    out,
    est,
    data,
    own,
    sib,
    slab,
    gx_in,
    gy_in,
    co_in,
    mid_f,
    mix_f,
    rows_t,
    t2,
    v2,
    wb,
    wbt,
    wc,
    wct,
    wa,
    wat,
    keep_gx,
    part_gx,
    keep_gy,
    give_own,
    give_gx,
    give_gy,
    give_co,
    take_own,
    take_gx,
    take_gy,
    take_co,
    put_gx,
    put_gy,
    get_gx,
    get_gy,
    load_sem,
    send_sem,
    recv_sem,
):
    i, j, g = lax.axis_index("gx"), lax.axis_index("gy"), lax.axis_index("gz")
    sibling = (i, j, 1 - g)
    across = (1 - i, j, g)
    beside = [[(i, j + 2 * s - 1, g), (i, j + 2 * s - 1, 1 - g)] for s in range(2)]
    exists = (j > 0, j < n_gy - 1)

    load_est = pltpu.make_async_copy(est_hbm.at[0], est, load_sem.at[0])
    load_data = pltpu.make_async_copy(data_hbm.at[:, 0], data, load_sem.at[1])
    load_est.start()
    load_data.start()

    def copy(number, src, dst, target):
        return pltpu.make_async_remote_copy(
            src_ref=src,
            dst_ref=dst,
            send_sem=send_sem.at[number],
            recv_sem=recv_sem.at[number],
            device_id=target,
            device_id_type=MESH,
        )

    def both_sides(action):
        for side in range(2):

            @pl.when(exists[side])
            def _(side=side):
                action(side)

    barrier = pltpu.get_barrier_semaphore()
    for target in (sibling, across):
        pl.semaphore_signal(barrier, inc=1, device_id=target, device_id_type=MESH)

    def greet(side):
        for core in range(2):
            pl.semaphore_signal(
                barrier, inc=1, device_id=beside[side][core], device_id_type=MESH
            )

    both_sides(greet)
    load_est.wait()
    own[...] = est[...].astype(BF16)

    row = i.astype(F32)
    edge = est[53:64, :] * (1.0 - row) + est[0:HALO, :] * row
    slab[...] = jnp.concatenate(
        [edge[:, q * QUARTER : (q + 1) * QUARTER] for q in range(4)] + [jnp.zeros((4, QUARTER), F32)],
        axis=0,
    ).astype(BF16)
    waits = 2 + 2 * exists[0].astype(I32) + 2 * exists[1].astype(I32)
    pl.semaphore_wait(barrier, waits)

    toward = (pl.ds(0, WIDTH), pl.ds(FACE, WIDTH))
    inside = ((pl.ds(0, 16), pl.ds(0, WIDTH)), (pl.ds(32, 16), pl.ds(256, WIDTH)))
    send_sib = copy(0, own, sib, sibling)
    send_gx = copy(1, slab, gx_in.at[0], across)
    send_gy = [copy(2 + s, own.at[:, toward[s]], gy_in.at[1 - s, 0], beside[s][0]) for s in range(2)]
    pass_gx = copy(4, gx_in.at[0], gx_in.at[1], sibling)
    pass_gy = [copy(5 + s, gy_in.at[s, 0], gy_in.at[s, 1], sibling) for s in range(2)]
    pass_co = [
        [
            copy(7 + 2 * s + c, gx_in.at[0, *inside[s]], co_in.at[1 - s, c], beside[s][c])
            for c in range(2)
        ]
        for s in range(2)
    ]

    def arrived(number, dst):
        copy(number, dst, dst, sibling).wait_recv()

    both_sides(lambda s: send_gy[s].start())
    send_gx.start()
    send_sib.start()

    for side in range(2):

        @pl.when(jnp.logical_not(exists[side]))
        def _(side=side):
            gy_in[side] = jnp.zeros(gy_in.shape[1:], BF16)
            co_in[side] = jnp.zeros(co_in.shape[1:], BF16)
            take_co[side] = jnp.zeros(take_co.shape[1:], BF16)

    def column(row, col):
        col = jnp.minimum(jnp.maximum(col, 0), n_gy - 1)
        codes = [owner[row, k, col] for k in range(PILLAR)]
        found = []
        for code in (g, 1 - g):
            hits = [(codes[k] == code).astype(I32) for k in range(PILLAR)]
            found.append((sum(hits), sum(k * hits[k] for k in range(PILLAR))))
        return found

    home = column(i, j)
    valid, height = home[0]

    def factors(entry, there=None):
        present, level = entry
        live = present * valid
        if there is not None:
            live = live * there.astype(I32)
        at = [(live * (level - height == d).astype(I32)).astype(F32) for d in (0, 1, -1)]
        lane_low = (iota((1, LANES), 1) & 63) < 32
        return at[0], jnp.where(lane_low, at[1], at[2])

    f_sib = factors(home[1])
    f_gx = [factors(e) for e in column(1 - i, j)]
    f_gy = [[factors(e, exists[s]) for e in column(i, j + 2 * s - 1)] for s in range(2)]
    f_co = [[factors(e, exists[s]) for e in column(1 - i, j + 2 * s - 1)] for s in range(2)]
    live = valid.astype(F32)

    build_forward(ps, wb, wc)

    def place(first_row, count, pair, mid, mix):
        mid_f[pl.ds(first_row * STEP_F + pair, count, stride=STEP_F), :] = mid
        mix_f[pl.ds(first_row * STEP_F + pair, count, stride=STEP_F), :] = mix

    def tile(number):
        return pl.ds(pl.multiple_of(number * LANES, LANES), LANES)

    def blend(pieces, factor):
        first, second = pieces[0].astype(F32), pieces[1].astype(F32)
        return (
            first * factor[0][0] + second * factor[1][0],
            first * factor[0][1] + second * factor[1][1],
        )

    for pair in range(44, PAIRS):
        place(0, SPAN_A, pair, jnp.zeros((SPAN_A, LANES), F32), jnp.zeros((SPAN_A, LANES), F32))

    first_pair = (38, 32)

    for side in range(2):

        @pl.when(exists[side])
        def _(side=side):
            arrived(3 - side, gy_in.at[side, 0])
            pass_gy[side].start()

    build_rest(ps, i, wbt, wct, wa, wat)
    send_sib.wait_recv()

    @pl.loop(0, 32)
    def _(pair):
        place(0, 64, pair, own[:, tile(pair)].astype(F32), sib[:, tile(pair)].astype(F32) * f_sib[1])

    both_sides(lambda s: pass_gy[s].wait_recv())
    for side in range(2):
        for pair in range(6):
            lanes = pl.ds(pair * LANES, LANES)
            mid, mix = blend([gy_in[side, k, :, lanes] for k in range(2)], f_gy[side])
            place(0, 64, first_pair[side] + pair, mid, mix)

    low = iota((PAIRS, LANES), 1) < 64

    def forward_chunk(chunk):
        for two in range(CHUNK // 2):
            parts = []
            for one in range(2):
                start = pl.multiple_of((chunk * CHUNK + two * 2 + one) * STEP_F, 8)
                mid, mix = mid_f[pl.ds(start, PAIRS), :], mix_f[pl.ds(start, PAIRS), :]
                even = jnp.where(low, mid, pltpu.roll(mix, 64, 1))
                odd = jnp.where(low, pltpu.roll(mid, 64, 1), mix)
                parts.append(jnp.concatenate([even, odd], axis=0).astype(BF16))
            first = jnp.dot(wb[...], jnp.concatenate(parts, axis=1), preferred_element_type=F32)
            rows_t[:, two * 256 : two * 256 + 256] = first.astype(BF16)
        for number in range(VIEWS * RANK):
            view, term = number // RANK, number % RANK
            top = number * 64
            block = jnp.concatenate(
                [
                    jnp.concatenate(
                        [
                            rows_t[top : top + 32, a * LANES : (a + 1) * LANES],
                            rows_t[top + 32 : top + 64, a * LANES : (a + 1) * LANES],
                        ],
                        axis=1,
                    )
                    for a in range(CHUNK)
                ],
                axis=0,
            )
            second = jnp.dot(block, wc[number], preferred_element_type=F32)
            for a in range(CHUNK):
                start = view * 32 * STEP_T + term * SPAN_A + chunk * CHUNK + a
                t2[pl.ds(start, 32, stride=STEP_T), :] = second[a * 32 : a * 32 + 32, :]

    pl.loop(0, 2)(forward_chunk)

    arrived(1, gx_in.at[0])
    pass_gx.start()

    def pass_ends(side):
        for core in range(2):
            pass_co[side][core].start()

    both_sides(pass_ends)
    pl.loop(2, 64 // CHUNK)(forward_chunk)

    pass_gx.wait_recv()
    for side in range(2):

        @pl.when(exists[side])
        def _(side=side):
            for core in range(2):
                arrived(7 + 2 * (1 - side) + core, co_in.at[side, core])

    def lengthen(rows):
        return jnp.concatenate([rows, jnp.zeros((16 - HALO, rows.shape[1]), F32)], axis=0)

    for q in range(4):
        rows = [gx_in[k].astype(F32)[HALO * q : HALO * q + HALO] for k in range(2)]
        for number in range(8):
            lanes = slice(number * LANES, (number + 1) * LANES)
            mid, mix = blend([lengthen(rows[k][:, lanes]) for k in range(2)], f_gx)
            place(64, 16, q * 8 + number, mid, mix)

    for side in range(2):
        down = 1 - side
        for pair in range(6):
            lanes = slice(pair * LANES, (pair + 1) * LANES)
            rows = [co_in[side, k, :, lanes].astype(F32)[down : down + HALO] for k in range(2)]
            mid, mix = blend([lengthen(r) for r in rows], f_co[side])
            place(64, 16, first_pair[side] + pair, mid, mix)

    forward_chunk(64 // CHUNK)
    load_data.wait()

    def turn(step):
        view, group = step // (32 // TURN), step % (32 // TURN)
        start = pl.multiple_of((view * 32 + group * TURN) * STEP_T, 8)
        fields = jnp.concatenate(
            [t2[pl.ds(start + k * STEP_T, 2 * SPAN_A), :].astype(BF16) for k in range(TURN)], axis=1
        )
        blurred = jnp.dot(wa[view], fields, preferred_element_type=F32)
        lanes = pl.ds(pl.multiple_of(group * (TURN * LANES), TURN * LANES), TURN * LANES)
        ratio = (data[view, :, lanes].astype(F32) / jnp.maximum(blurred, FLOOR) * live).astype(BF16)
        back = jnp.dot(wat[view], ratio, preferred_element_type=F32).astype(BF16)
        for term in range(RANK):
            rows = back[term * SPAN_A : (term + 1) * SPAN_A]
            block = jnp.concatenate(
                [rows[:, k * LANES : (k + 1) * LANES] for k in range(TURN)], axis=0
            )
            wide = jnp.dot(block, wct[view * RANK + term], preferred_element_type=F32)
            for k in range(TURN):
                for odd in range(2):
                    at = (view * RANK + term) * 64 + odd * 32 + group * TURN + k
                    v2[pl.ds(at, SPAN_A, stride=STEP_V), :] = wide[
                        k * SPAN_A : (k + 1) * SPAN_A, odd * LANES : (odd + 1) * LANES
                    ]

    pl.loop(0, VIEWS * 32 // TURN)(turn)

    def adjoint_rows(step):
        start = pl.multiple_of(step * DUO * STEP_V, 8)
        fields = jnp.concatenate(
            [v2[pl.ds(start + k * STEP_V, 512), :].astype(BF16) for k in range(DUO)], axis=1
        )
        spread = jnp.dot(wbt[...], fields, preferred_element_type=F32)
        for k in range(DUO):
            even = spread[0:PAIRS, k * LANES : (k + 1) * LANES]
            odd = spread[PAIRS : 2 * PAIRS, k * LANES : (k + 1) * LANES]
            at = pl.multiple_of((step * DUO + k) * STEP_F, 8)
            mid_f[pl.ds(at, PAIRS), :] = jnp.where(low, even, pltpu.roll(odd, 64, 1))
            mix_f[pl.ds(at, PAIRS), :] = jnp.where(low, pltpu.roll(even, 64, 1), odd)

    def fetch(first_row, count, pair):
        at = pl.ds(first_row * STEP_F + pair, count, stride=STEP_F)
        return mid_f[at, :], mix_f[at, :]

    adjoint_rows(64 // DUO)
    for q in range(4):
        for number in range(8):
            lanes = slice(number * LANES, (number + 1) * LANES)
            mid, mix = fetch(64, 16, q * 8 + number)
            mid, mix = mid[:HALO], mix[:HALO]
            keep_gx[HALO * q : HALO * q + HALO, lanes] = mid * f_gx[0][0] + mix * f_gx[0][1]
            part_gx[HALO * q : HALO * q + HALO, lanes] = mid * f_gx[1][0] + mix * f_gx[1][1]
    keep_gx[44:48, :] = jnp.zeros((4, QUARTER), F32)
    part_gx[44:48, :] = jnp.zeros((4, QUARTER), F32)
    give_gx[...] = part_gx[...].astype(BF16)
    share_gx = copy(11, give_gx, take_gx, sibling)
    share_gx.start()

    for side in range(2):
        down = 1 - side
        for pair in range(6):
            lanes = slice(pair * LANES, (pair + 1) * LANES)
            mid, mix = fetch(64, 16, first_pair[side] + pair)
            for core in range(2):
                factor = f_co[side][core]
                rows = (mid * factor[0] + mix * factor[1])[:HALO]
                parts = [jnp.zeros((down, LANES), F32)] if down else []
                parts += [rows, jnp.zeros((16 - HALO - down, LANES), F32)]
                give_co[side, core, :, lanes] = jnp.concatenate(parts, axis=0).astype(BF16)

    send_co = [
        [
            copy(12 + 2 * s + c, give_co.at[s, c], take_co.at[1 - s, c], beside[s][c])
            for c in range(2)
        ]
        for s in range(2)
    ]

    def send_ends(side):
        for core in range(2):
            send_co[side][core].start()

    both_sides(send_ends)
    final_gx = copy(16, put_gx, get_gx, across)

    def finish_gx():
        share_gx.wait_recv()
        keep_gx[...] = keep_gx[...] + take_gx[...].astype(F32)
        for side in range(2):

            @pl.when(exists[side])
            def _(side=side):
                for core in range(2):
                    arrived(12 + 2 * (1 - side) + core, take_co.at[side, core])

        for side in range(2):
            ends = take_co[side, 0].astype(F32) + take_co[side, 1].astype(F32)
            keep_gx[inside[side]] = keep_gx[inside[side]] + ends
        put_gx[...] = keep_gx[...].astype(BF16)
        final_gx.start()

    share_gy = [copy(17 + k, give_gy.at[k], take_gy.at[k], sibling) for k in range(4)]
    final_gy = [
        [
            copy(21 + 2 * k + s, put_gy.at[k, s], get_gy.at[k, 1 - s], beside[s][0])
            for s in range(2)
        ]
        for k in range(4)
    ]
    share_own = [
        copy(29 + k, give_own.at[pl.ds(16 * k, 16)], take_own.at[pl.ds(16 * k, 16)], sibling)
        for k in range(4)
    ]

    def own_rows(k):
        adjoint_rows(k)
        for side in range(2):
            for pair in range(6):
                lanes = pl.ds(pair * LANES, LANES)
                mid, mix = fetch(16 * k, 16, first_pair[side] + pair)
                one, two = f_gy[side]
                keep_gy[k, side, :, lanes] = mid * one[0] + mix * one[1]
                give_gy[k, side, :, lanes] = (mid * two[0] + mix * two[1]).astype(BF16)
        share_gy[k].start()
        for pair in range(32):
            lanes = pl.ds(pair * LANES, LANES)
            mid, mix = fetch(16 * k, 16, pair)
            out[0, 16 * k : 16 * k + 16, lanes] = mid
            give_own[16 * k : 16 * k + 16, lanes] = (mix * f_sib[1]).astype(BF16)
        share_own[k].start()

    def finish_gy(k):
        share_gy[k].wait_recv()
        put_gy[k] = (keep_gy[k] + take_gy[k].astype(F32)).astype(BF16)
        both_sides(lambda s: final_gy[k][s].start())

    own_rows(0)
    finish_gx()
    for k in range(1, 4):
        own_rows(k)
        finish_gy(k - 1)
    finish_gy(3)

    for k in range(4):
        share_own[k].wait_recv()
    out[0] = out[0] + take_own[...].astype(F32)
    final_gx.wait_recv()
    for q in range(4):
        rows = get_gx[...].astype(F32)[HALO * q : HALO * q + HALO]
        gap = jnp.zeros((16 - HALO, QUARTER), F32)
        lanes = pl.ds(q * QUARTER, QUARTER)
        out[0, 0:16, lanes] = out[0, 0:16, lanes] + jnp.concatenate([rows, gap], axis=0) * row
        out[0, 48:64, lanes] = out[0, 48:64, lanes] + jnp.concatenate([gap, rows], axis=0) * (
            1.0 - row
        )
    for side in range(2):

        @pl.when(exists[side])
        def _(side=side):
            for k in range(4):
                arrived(21 + 2 * k + 1 - side, get_gy.at[k, side])
                rows = slice(16 * k, 16 * k + 16)
                out[0, rows, toward[side]] = out[0, rows, toward[side]] + get_gy[k, side].astype(F32)

    out[0] = est[...] * out[0] * (live / VIEWS)

    for item in [send_sib, send_gx, pass_gx, share_gx, final_gx] + share_gy + share_own:
        item.wait_send()

    def drain(side):
        items = [send_gy[side], pass_gy[side], *pass_co[side], *send_co[side]]
        for item in items + [final_gy[k][side] for k in range(4)]:
            item.wait_send()

    both_sides(drain)


def solution(mesh):
    n_gy = mesh.shape["gy"]

    def body(estimate, views_data, point_spread, block_owner):
        slab, ends = (48, QUARTER), (2, 2, 16, WIDTH)
        sides = (4, 2, 16, WIDTH)
        scratch = [
            ((64, 4096), F32),
            ((VIEWS, 64, 4096), BF16),
            ((64, 4096), BF16),
            ((64, 4096), BF16),
            (slab, BF16),
            ((2, *slab), BF16),
            ((2, 2, 64, WIDTH), BF16),
            (ends, BF16),
            ((SPAN_A * STEP_F, LANES), F32),
            ((SPAN_A * STEP_F, LANES), F32),
            ((512, CHUNK * LANES), BF16),
            ((VIEWS * 32 * STEP_T, LANES), F32),
            ((SPAN_A * STEP_V, LANES), F32),
            ((512, 96), BF16),
            ((96, 512), BF16),
            ((8, 256, 128), BF16),
            ((8, 128, 256), BF16),
            ((VIEWS, 64, 2 * SPAN_A), BF16),
            ((VIEWS, 2 * SPAN_A, 64), BF16),
            (slab, F32),
            (slab, F32),
            (sides, F32),
            ((64, 4096), BF16),
            (slab, BF16),
            (sides, BF16),
            (ends, BF16),
            ((64, 4096), BF16),
            (slab, BF16),
            (sides, BF16),
            (ends, BF16),
            (slab, BF16),
            (sides, BF16),
            (slab, BF16),
            (sides, BF16),
        ]
        any_spec = pl.BlockSpec(memory_space=pl.ANY)
        smem = pl.BlockSpec(memory_space=pltpu.SMEM)
        return pl.pallas_call(
            functools.partial(kernel, n_gy),
            out_shape=jax.ShapeDtypeStruct((1, 64, 4096), F32),
            in_specs=[any_spec, any_spec, smem, smem],
            out_specs=pl.BlockSpec(memory_space=pltpu.VMEM),
            scratch_shapes=[pltpu.VMEM(shape, kind) for shape, kind in scratch]
            + [
                pltpu.SemaphoreType.DMA((2,)),
                pltpu.SemaphoreType.DMA((33,)),
                pltpu.SemaphoreType.DMA((33,)),
            ],
            compiler_params=pltpu.CompilerParams(
                collective_id=0, has_side_effects=True, vmem_limit_bytes=60 * 2**20
            ),
        )(
            estimate,
            views_data,
            point_spread.transpose(0, 2, 1, 3),
            block_owner.transpose(0, 2, 1),
        )

    placed = (P(("gx", "gy", "gz"), None, None), P(None, ("gx", "gy", "gz"), None, None), P(), P())
    return jax.shard_map(
        body,
        mesh=mesh,
        in_specs=placed,
        out_specs=P(("gx", "gy", "gz"), None, None),
        check_vma=False,
    )
```

```python
import functools

import jax
import jax.numpy as jnp
from jax import lax
from jax.experimental import pallas as pl
from jax.experimental.pallas import tpu as pltpu
from jax.sharding import PartitionSpec as P

MESH = pl.DeviceIdType.MESH
F32, BF16, I32 = jnp.float32, jnp.bfloat16, jnp.int32
BLOCK, TAPS, HALO, RANK, VIEWS, PILLAR = 64, 23, 11, 2, 4, 4
FLOOR = 0.5
SPAN_A = 80
PAIRS = 48
STEP_F, STEP_T, STEP_V = 56, 168, 520
LANES = 128
WIDTH = 768
FACE = 3328
QUARTER = 1024
CHUNK = 16
DUO = 16


def iota(shape, dim):
    return lax.broadcasted_iota(I32, shape, dim)


def band(distance, tap):
    total = jnp.zeros(distance.shape, F32)
    for t in range(TAPS):
        total = jnp.where(distance == t, tap(t), total)
    return total


def ext_c(lane):
    return jnp.where(lane < 96, lane, lane - LANES)


def parity_b(row):
    return jnp.where(row < 32, 2 * row, 2 * row - 63)


def ext_b(row):
    odd = (row >= PAIRS).astype(I32)
    pair = row - PAIRS * odd
    value = 2 * pair + odd - 88 * (pair >= 38).astype(I32)
    return jnp.where(pair >= 44, 1000, value)


def tap_of(ps):
    def tap(number, axis):
        return lambda t: ps[number // RANK, axis, number % RANK, t]

    return tap


def build_forward(ps, wb, wc):
    tap = tap_of(ps)
    d_b = ext_b(iota((64, 96), 1)) - parity_b(iota((64, 96), 0)) + HALO
    lane = iota((LANES, LANES), 1)
    d_c = ext_c(iota((LANES, LANES), 0)) - jnp.where(lane >= 64, lane - 64, lane) + HALO

    @pl.loop(0, VIEWS * RANK)
    def _(number):
        start = pl.multiple_of(number * 64, 64)
        wb[pl.ds(start, 64), :] = band(d_b, tap(number, 1)).astype(BF16)
        base = band(d_c, tap(number, 2))
        wc[number, 0:128, :] = jnp.where(lane < 64, base, 0.0).astype(BF16)
        wc[number, 128:256, :] = jnp.where(lane >= 64, base, 0.0).astype(BF16)


def build_rest(ps, mesh_row, wbt, wct, wa, wat_own, wat_far):
    tap = tap_of(ps)
    d_ct = ext_c(iota((64, LANES), 1)) - iota((64, LANES), 0) + HALO
    wct[...] = jnp.zeros_like(wct)

    @pl.loop(0, VIEWS * RANK)
    def _(number):
        base = band(d_ct, tap(number, 2)).astype(BF16)
        wct[number, 0:64, 0:128] = base
        wct[number, 64:128, 128:256] = base

    col = iota((96, LANES), 1)
    high = col >= 64
    d_bt = ext_b(iota((96, LANES), 0)) - parity_b(jnp.where(high, col - 64, col)) + HALO
    for pair in range(VIEWS * RANK // 2):
        low_tap, high_tap = tap(2 * pair, 1), tap(2 * pair + 1, 1)
        wbt[:, pair * LANES : (pair + 1) * LANES] = band(
            d_bt, lambda t: jnp.where(high, high_tap(t), low_tap(t))
        ).astype(BF16)

    def ext_a(place):
        inside = place - (64 + HALO) * (place >= 64).astype(I32) * mesh_row
        return jnp.where(place >= 64 + HALO, 1000, inside)

    second = iota((64, 2 * SPAN_A), 1) >= SPAN_A
    place = iota((64, 2 * SPAN_A), 1) - SPAN_A * second.astype(I32)
    d_a = ext_a(place) - iota((64, 2 * SPAN_A), 0) + HALO
    d_at = ext_a(iota((SPAN_A, 64), 0)) - iota((SPAN_A, 64), 1) + HALO

    @pl.loop(0, VIEWS)
    def _(view):
        first_tap, second_tap = tap(2 * view, 0), tap(2 * view + 1, 0)
        wa[view] = band(d_a, lambda t: jnp.where(second, second_tap(t), first_tap(t))).astype(BF16)
        for term, taps in enumerate((first_tap, second_tap)):
            base = band(d_at, taps).astype(BF16)
            wat_own[view, term * 64 : term * 64 + 64, :] = base[:64]
            wat_far[view, term * 16 : term * 16 + 16, :] = base[64:]


def kernel(
    n_gy,
    est_hbm,
    data_hbm,
    ps,
    owner,
    out,
    est,
    data,
    own,
    sib,
    slab,
    gx_in,
    gy_in,
    co_in,
    mid_f,
    mix_f,
    rows_t,
    t2,
    v2,
    wb,
    wbt,
    wc,
    wct,
    wa,
    wat_own,
    wat_far,
    keep_gx,
    part_gx,
    give_own,
    give_gx,
    give_gy,
    give_co,
    take_own,
    take_gx,
    take_gy,
    take_co,
    put_gx,
    get_gx,
    load_sem,
    send_sem,
    recv_sem,
):
    i, j, g = lax.axis_index("gx"), lax.axis_index("gy"), lax.axis_index("gz")
    sibling = (i, j, 1 - g)
    across = (1 - i, j, g)
    beside = [[(i, j + 2 * s - 1, g), (i, j + 2 * s - 1, 1 - g)] for s in range(2)]
    exists = (j > 0, j < n_gy - 1)

    toward = (pl.ds(0, WIDTH), pl.ds(FACE, WIDTH))
    parts = (*toward, pl.ds(WIDTH, FACE - WIDTH))
    load_est = [
        pltpu.make_async_copy(est_hbm.at[0, :, p], est.at[:, p], load_sem.at[n])
        for n, p in enumerate(parts)
    ]
    load_data = pltpu.make_async_copy(data_hbm.at[:, 0], data, load_sem.at[3])
    for item in load_est:
        item.start()
    load_data.start()

    def copy(number, src, dst, target):
        return pltpu.make_async_remote_copy(
            src_ref=src,
            dst_ref=dst,
            send_sem=send_sem.at[number],
            recv_sem=recv_sem.at[number],
            device_id=target,
            device_id_type=MESH,
        )

    def both_sides(action):
        for side in range(2):

            @pl.when(exists[side])
            def _(side=side):
                action(side)

    barrier = pltpu.get_barrier_semaphore()
    for target in (sibling, across):
        pl.semaphore_signal(barrier, inc=1, device_id=target, device_id_type=MESH)

    def greet(side):
        for core in range(2):
            pl.semaphore_signal(
                barrier, inc=1, device_id=beside[side][core], device_id_type=MESH
            )

    both_sides(greet)
    for item, lanes in zip(load_est[:2], toward):
        item.wait()
        own[:, lanes] = est[:, lanes].astype(BF16)
    waits = 2 + 2 * exists[0].astype(I32) + 2 * exists[1].astype(I32)
    pl.semaphore_wait(barrier, waits)

    inside = ((pl.ds(0, 16), pl.ds(0, WIDTH)), (pl.ds(32, 16), pl.ds(256, WIDTH)))
    send_sib = copy(0, own, sib, sibling)
    send_gx = copy(1, slab, gx_in.at[0], across)
    send_gy = [copy(2 + s, own.at[:, toward[s]], gy_in.at[1 - s, 0], beside[s][0]) for s in range(2)]
    pass_gx = copy(4, gx_in.at[0], gx_in.at[1], sibling)
    pass_gy = [copy(5 + s, gy_in.at[s, 0], gy_in.at[s, 1], sibling) for s in range(2)]
    pass_co = [
        [
            copy(7 + 2 * s + c, gx_in.at[0, *inside[s]], co_in.at[1 - s, c], beside[s][c])
            for c in range(2)
        ]
        for s in range(2)
    ]

    def arrived(number, dst):
        copy(number, dst, dst, sibling).wait_recv()

    both_sides(lambda s: send_gy[s].start())
    load_est[2].wait()
    own[:, parts[2]] = est[:, parts[2]].astype(BF16)
    send_sib.start()

    row = i.astype(F32)
    edge = est[53:64, :] * (1.0 - row) + est[0:HALO, :] * row
    slab[...] = jnp.concatenate(
        [edge[:, q * QUARTER : (q + 1) * QUARTER] for q in range(4)] + [jnp.zeros((4, QUARTER), F32)],
        axis=0,
    ).astype(BF16)

    for side in range(2):

        @pl.when(jnp.logical_not(exists[side]))
        def _(side=side):
            gy_in[side] = jnp.zeros(gy_in.shape[1:], BF16)
            co_in[side] = jnp.zeros(co_in.shape[1:], BF16)
            take_co[side] = jnp.zeros(take_co.shape[1:], BF16)

    def column(row, col):
        col = jnp.minimum(jnp.maximum(col, 0), n_gy - 1)
        codes = [owner[row, k, col] for k in range(PILLAR)]
        found = []
        for code in (g, 1 - g):
            hits = [(codes[k] == code).astype(I32) for k in range(PILLAR)]
            found.append((sum(hits), sum(k * hits[k] for k in range(PILLAR))))
        return found

    home = column(i, j)
    valid, height = home[0]

    def factors(entry, there=None):
        present, level = entry
        live = present * valid
        if there is not None:
            live = live * there.astype(I32)
        at = [(live * (level - height == d).astype(I32)).astype(F32) for d in (0, 1, -1)]
        lane_low = (iota((1, LANES), 1) & 63) < 32
        return at[0], jnp.where(lane_low, at[1], at[2])

    f_sib = factors(home[1])
    f_gx = [factors(e) for e in column(1 - i, j)]
    f_gy = [[factors(e, exists[s]) for e in column(i, j + 2 * s - 1)] for s in range(2)]
    f_co = [[factors(e, exists[s]) for e in column(1 - i, j + 2 * s - 1)] for s in range(2)]
    live = valid.astype(F32)

    build_forward(ps, wb, wc)
    send_gx.start()

    def place(first_row, count, pair, mid, mix):
        mid_f[pl.ds(first_row * STEP_F + pair, count, stride=STEP_F), :] = mid
        mix_f[pl.ds(first_row * STEP_F + pair, count, stride=STEP_F), :] = mix

    def tile(number):
        return pl.ds(pl.multiple_of(number * LANES, LANES), LANES)

    def blend(pieces, factor):
        first, second = pieces[0].astype(F32), pieces[1].astype(F32)
        return (
            first * factor[0][0] + second * factor[1][0],
            first * factor[0][1] + second * factor[1][1],
        )

    for pair in range(44, PAIRS):
        place(0, SPAN_A, pair, jnp.zeros((SPAN_A, LANES), F32), jnp.zeros((SPAN_A, LANES), F32))

    first_pair = (38, 32)

    for side in range(2):

        @pl.when(exists[side])
        def _(side=side):
            arrived(3 - side, gy_in.at[side, 0])
            pass_gy[side].start()

    build_rest(ps, i, wbt, wct, wa, wat_own, wat_far)
    send_sib.wait_recv()

    @pl.loop(0, 32)
    def _(pair):
        place(0, 64, pair, own[:, tile(pair)].astype(F32), sib[:, tile(pair)].astype(F32) * f_sib[1])

    both_sides(lambda s: pass_gy[s].wait_recv())
    for side in range(2):
        for pair in range(6):
            lanes = pl.ds(pair * LANES, LANES)
            mid, mix = blend([gy_in[side, k, :, lanes] for k in range(2)], f_gy[side])
            place(0, 64, first_pair[side] + pair, mid, mix)

    low = iota((PAIRS, LANES), 1) < 64

    def forward_chunk(chunk):
        for two in range(CHUNK // 2):
            parts = []
            for one in range(2):
                start = pl.multiple_of((chunk * CHUNK + two * 2 + one) * STEP_F, 8)
                mid, mix = mid_f[pl.ds(start, PAIRS), :], mix_f[pl.ds(start, PAIRS), :]
                even = jnp.where(low, mid, pltpu.roll(mix, 64, 1))
                odd = jnp.where(low, pltpu.roll(mid, 64, 1), mix)
                parts.append(jnp.concatenate([even, odd], axis=0).astype(BF16))
            first = jnp.dot(wb[...], jnp.concatenate(parts, axis=1), preferred_element_type=F32)
            rows_t[:, two * 256 : two * 256 + 256] = first.astype(BF16)
        for number in range(VIEWS * RANK):
            view, term = number // RANK, number % RANK
            top = number * 64
            block = jnp.concatenate(
                [
                    jnp.concatenate(
                        [
                            rows_t[top : top + 32, a * LANES : (a + 1) * LANES],
                            rows_t[top + 32 : top + 64, a * LANES : (a + 1) * LANES],
                        ],
                        axis=1,
                    )
                    for a in range(CHUNK)
                ],
                axis=0,
            )
            second = jnp.dot(block, wc[number], preferred_element_type=F32)
            for a in range(CHUNK):
                start = view * 32 * STEP_T + term * SPAN_A + chunk * CHUNK + a
                t2[pl.ds(start, 32, stride=STEP_T), :] = second[a * 32 : a * 32 + 32, :]

    pl.loop(0, 2)(forward_chunk)

    arrived(1, gx_in.at[0])
    pass_gx.start()

    def pass_ends(side):
        for core in range(2):
            pass_co[side][core].start()

    both_sides(pass_ends)
    pl.loop(2, 64 // CHUNK)(forward_chunk)

    pass_gx.wait_recv()
    for side in range(2):

        @pl.when(exists[side])
        def _(side=side):
            for core in range(2):
                arrived(7 + 2 * (1 - side) + core, co_in.at[side, core])

    def lengthen(rows):
        return jnp.concatenate([rows, jnp.zeros((16 - HALO, rows.shape[1]), F32)], axis=0)

    for q in range(4):
        rows = [gx_in[k].astype(F32)[HALO * q : HALO * q + HALO] for k in range(2)]
        for number in range(8):
            lanes = slice(number * LANES, (number + 1) * LANES)
            mid, mix = blend([lengthen(rows[k][:, lanes]) for k in range(2)], f_gx)
            place(64, 16, q * 8 + number, mid, mix)

    for side in range(2):
        down = 1 - side
        for pair in range(6):
            lanes = slice(pair * LANES, (pair + 1) * LANES)
            rows = [co_in[side, k, :, lanes].astype(F32)[down : down + HALO] for k in range(2)]
            mid, mix = blend([lengthen(r) for r in rows], f_co[side])
            place(64, 16, first_pair[side] + pair, mid, mix)

    forward_chunk(64 // CHUNK)
    load_data.wait()

    def adjoint_front(view, back, count, first):
        for term in range(RANK):
            rows = back[term * count : (term + 1) * count]
            block = jnp.concatenate([rows[:, k * LANES : (k + 1) * LANES] for k in range(32)], axis=0)
            wide = jnp.dot(block, wct[view * RANK + term], preferred_element_type=F32)
            for k in range(32):
                for odd in range(2):
                    at = first * STEP_V + (view * RANK + term) * 64 + odd * 32 + k
                    v2[pl.ds(at, count, stride=STEP_V), :] = wide[
                        k * count : (k + 1) * count, odd * LANES : (odd + 1) * LANES
                    ]

    def turn_far(view):
        start = pl.multiple_of(view * 32 * STEP_T, 8)
        fields = jnp.concatenate(
            [t2[pl.ds(start + k * STEP_T, 2 * SPAN_A), :].astype(BF16) for k in range(32)], axis=1
        )
        blurred = jnp.dot(wa[view], fields, preferred_element_type=F32)
        ratio = (data[view].astype(F32) / jnp.maximum(blurred, FLOOR) * live).astype(BF16)
        data[view] = ratio
        back = jnp.dot(wat_far[view], ratio, preferred_element_type=F32).astype(BF16)
        adjoint_front(view, back, 16, 64)

    def turn_own(view):
        back = jnp.dot(wat_own[view], data[view], preferred_element_type=F32).astype(BF16)
        adjoint_front(view, back, 64, 0)

    pl.loop(0, VIEWS)(turn_far)

    def adjoint_rows(step):
        start = pl.multiple_of(step * DUO * STEP_V, 8)
        fields = jnp.concatenate(
            [v2[pl.ds(start + k * STEP_V, 512), :].astype(BF16) for k in range(DUO)], axis=1
        )
        spread = jnp.dot(wbt[...], fields, preferred_element_type=F32)
        for k in range(DUO):
            even = spread[0:PAIRS, k * LANES : (k + 1) * LANES]
            odd = spread[PAIRS : 2 * PAIRS, k * LANES : (k + 1) * LANES]
            at = pl.multiple_of((step * DUO + k) * STEP_F, 8)
            mid_f[pl.ds(at, PAIRS), :] = jnp.where(low, even, pltpu.roll(odd, 64, 1))
            mix_f[pl.ds(at, PAIRS), :] = jnp.where(low, pltpu.roll(even, 64, 1), odd)

    def fetch(first_row, count, pair):
        at = pl.ds(first_row * STEP_F + pair, count, stride=STEP_F)
        return mid_f[at, :], mix_f[at, :]

    adjoint_rows(64 // DUO)
    for q in range(4):
        for number in range(8):
            lanes = slice(number * LANES, (number + 1) * LANES)
            mid, mix = fetch(64, 16, q * 8 + number)
            mid, mix = mid[:HALO], mix[:HALO]
            keep_gx[HALO * q : HALO * q + HALO, lanes] = mid * f_gx[0][0] + mix * f_gx[0][1]
            part_gx[HALO * q : HALO * q + HALO, lanes] = mid * f_gx[1][0] + mix * f_gx[1][1]
    keep_gx[44:48, :] = jnp.zeros((4, QUARTER), F32)
    part_gx[44:48, :] = jnp.zeros((4, QUARTER), F32)
    give_gx[...] = part_gx[...].astype(BF16)
    share_gx = copy(11, give_gx, take_gx, sibling)
    share_gx.start()

    for side in range(2):
        down = 1 - side
        for pair in range(6):
            lanes = slice(pair * LANES, (pair + 1) * LANES)
            mid, mix = fetch(64, 16, first_pair[side] + pair)
            for core in range(2):
                factor = f_co[side][core]
                rows = (mid * factor[0] + mix * factor[1])[:HALO]
                parts = [jnp.zeros((down, LANES), F32)] if down else []
                parts += [rows, jnp.zeros((16 - HALO - down, LANES), F32)]
                give_co[side, core, :, lanes] = jnp.concatenate(parts, axis=0).astype(BF16)

    send_co = [
        [
            copy(12 + 2 * s + c, give_co.at[s, c], take_co.at[1 - s, c], beside[s][c])
            for c in range(2)
        ]
        for s in range(2)
    ]

    def send_ends(side):
        for core in range(2):
            send_co[side][core].start()

    both_sides(send_ends)
    final_gx = copy(16, put_gx, get_gx, across)

    def finish_gx():
        share_gx.wait_recv()
        keep_gx[...] = keep_gx[...] + take_gx[...].astype(F32)
        for side in range(2):

            @pl.when(exists[side])
            def _(side=side):
                for core in range(2):
                    arrived(12 + 2 * (1 - side) + core, take_co.at[side, core])

        for side in range(2):
            ends = take_co[side, 0].astype(F32) + take_co[side, 1].astype(F32)
            keep_gx[inside[side]] = keep_gx[inside[side]] + ends
        put_gx[...] = keep_gx[...].astype(BF16)
        final_gx.start()

    pl.loop(0, VIEWS // 2)(turn_own)
    finish_gx()
    pl.loop(VIEWS // 2, VIEWS)(turn_own)

    scale = live / VIEWS
    send_sides = [
        [
            [
                copy(17 + 4 * k + 2 * s + c, give_gy.at[k, s, c], take_gy.at[k, 1 - s, c], beside[s][c])
                for c in range(2)
            ]
            for s in range(2)
        ]
        for k in range(4)
    ]
    share_own = [
        copy(33 + k, give_own.at[pl.ds(16 * k, 16)], take_own.at[pl.ds(16 * k, 16)], sibling)
        for k in range(4)
    ]

    def own_rows(k):
        adjoint_rows(k)
        for side in range(2):
            for pair in range(6):
                lanes = pl.ds(pair * LANES, LANES)
                mid, mix = fetch(16 * k, 16, first_pair[side] + pair)
                for core in range(2):
                    factor = f_gy[side][core]
                    give_gy[k, side, core, :, lanes] = (mid * factor[0] + mix * factor[1]).astype(BF16)

        def send(side):
            for core in range(2):
                send_sides[k][side][core].start()

        both_sides(send)
        for pair in range(32):
            lanes = pl.ds(pair * LANES, LANES)
            mid, mix = fetch(16 * k, 16, pair)
            out[0, 16 * k : 16 * k + 16, lanes] = mid
            give_own[16 * k : 16 * k + 16, lanes] = (mix * f_sib[1]).astype(BF16)
        share_own[k].start()

    def finish_own(k):
        share_own[k].wait_recv()
        rows = slice(16 * k, 16 * k + 16)
        out[0, rows] = (out[0, rows] + take_own[rows].astype(F32)) * (est[rows] * scale)

    own_rows(0)
    for k in range(1, 4):
        own_rows(k)
        finish_own(k - 1)
    finish_own(3)

    final_gx.wait_recv()
    for q in range(4):
        rows = get_gx[...].astype(F32)[HALO * q : HALO * q + HALO]
        gap = jnp.zeros((16 - HALO, QUARTER), F32)
        lanes = pl.ds(q * QUARTER, QUARTER)
        low_rows = jnp.concatenate([rows, gap], axis=0) * (row * scale)
        high_rows = jnp.concatenate([gap, rows], axis=0) * ((1.0 - row) * scale)
        out[0, 0:16, lanes] = out[0, 0:16, lanes] + low_rows * est[0:16, lanes]
        out[0, 48:64, lanes] = out[0, 48:64, lanes] + high_rows * est[48:64, lanes]
    for k in range(4):
        for side in range(2):

            @pl.when(exists[side])
            def _(k=k, side=side):
                for core in range(2):
                    arrived(17 + 4 * k + 2 * (1 - side) + core, take_gy.at[k, side, core])
                rows = slice(16 * k, 16 * k + 16)
                total = take_gy[k, side, 0].astype(F32) + take_gy[k, side, 1].astype(F32)
                out[0, rows, toward[side]] = out[0, rows, toward[side]] + total * (
                    est[rows, toward[side]] * scale
                )

    for item in [send_sib, send_gx, pass_gx, share_gx, final_gx] + share_own:
        item.wait_send()

    def drain(side):
        items = [send_gy[side], pass_gy[side], *pass_co[side], *send_co[side]]
        for item in items + [c for k in range(4) for c in send_sides[k][side]]:
            item.wait_send()

    both_sides(drain)


def solution(mesh):
    n_gy = mesh.shape["gy"]

    def body(estimate, views_data, point_spread, block_owner):
        slab, ends = (48, QUARTER), (2, 2, 16, WIDTH)
        sides = (4, 2, 2, 16, WIDTH)
        scratch = [
            ((64, 4096), F32),
            ((VIEWS, 64, 4096), BF16),
            ((64, 4096), BF16),
            ((64, 4096), BF16),
            (slab, BF16),
            ((2, *slab), BF16),
            ((2, 2, 64, WIDTH), BF16),
            (ends, BF16),
            ((SPAN_A * STEP_F, LANES), F32),
            ((SPAN_A * STEP_F, LANES), F32),
            ((512, CHUNK * LANES), BF16),
            ((VIEWS * 32 * STEP_T, LANES), F32),
            ((SPAN_A * STEP_V, LANES), F32),
            ((512, 96), BF16),
            ((96, 512), BF16),
            ((8, 256, 128), BF16),
            ((8, 128, 256), BF16),
            ((VIEWS, 64, 2 * SPAN_A), BF16),
            ((VIEWS, RANK * 64, 64), BF16),
            ((VIEWS, RANK * 16, 64), BF16),
            (slab, F32),
            (slab, F32),
            ((64, 4096), BF16),
            (slab, BF16),
            (sides, BF16),
            (ends, BF16),
            ((64, 4096), BF16),
            (slab, BF16),
            (sides, BF16),
            (ends, BF16),
            (slab, BF16),
            (slab, BF16),
        ]
        any_spec = pl.BlockSpec(memory_space=pl.ANY)
        smem = pl.BlockSpec(memory_space=pltpu.SMEM)
        return pl.pallas_call(
            functools.partial(kernel, n_gy),
            out_shape=jax.ShapeDtypeStruct((1, 64, 4096), F32),
            in_specs=[any_spec, any_spec, smem, smem],
            out_specs=pl.BlockSpec(memory_space=pltpu.VMEM),
            scratch_shapes=[pltpu.VMEM(shape, kind) for shape, kind in scratch]
            + [
                pltpu.SemaphoreType.DMA((4,)),
                pltpu.SemaphoreType.DMA((37,)),
                pltpu.SemaphoreType.DMA((37,)),
            ],
            compiler_params=pltpu.CompilerParams(
                collective_id=0, has_side_effects=True, vmem_limit_bytes=60 * 2**20
            ),
        )(
            estimate,
            views_data,
            point_spread.transpose(0, 2, 1, 3),
            block_owner.transpose(0, 2, 1),
        )

    placed = (P(("gx", "gy", "gz"), None, None), P(None, ("gx", "gy", "gz"), None, None), P(), P())
    return jax.shard_map(
        body,
        mesh=mesh,
        in_specs=placed,
        out_specs=P(("gx", "gy", "gz"), None, None),
        check_vma=False,
    )
```

```python
import functools

import jax
import jax.numpy as jnp
from jax import lax
from jax.experimental import pallas as pl
from jax.experimental.pallas import tpu as pltpu
from jax.sharding import PartitionSpec as P

MESH = pl.DeviceIdType.MESH
F32, BF16, I32 = jnp.float32, jnp.bfloat16, jnp.int32
BLOCK, TAPS, HALO, RANK, VIEWS, PILLAR = 64, 23, 11, 2, 4, 4
FLOOR = 0.5
SPAN_A = 80
PAIRS = 48
STEP_F, STEP_T, STEP_V = 56, 168, 520
LANES = 128
WIDTH = 768
FACE = 3328
QUARTER = 1024
CHUNK = 16
DUO = 16


def iota(shape, dim):
    return lax.broadcasted_iota(I32, shape, dim)


def band(distance, tap):
    total = jnp.zeros(distance.shape, F32)
    for t in range(TAPS):
        total = jnp.where(distance == t, tap(t), total)
    return total


def ext_c(lane):
    return jnp.where(lane < 96, lane, lane - LANES)


def parity_b(row):
    return jnp.where(row < 32, 2 * row, 2 * row - 63)


def ext_b(row):
    odd = (row >= PAIRS).astype(I32)
    pair = row - PAIRS * odd
    value = 2 * pair + odd - 88 * (pair >= 38).astype(I32)
    return jnp.where(pair >= 44, 1000, value)


def tap_of(ps):
    def tap(number, axis):
        return lambda t: ps[number // RANK, axis, number % RANK, t]

    return tap


def build_forward(ps, wb, wc):
    tap = tap_of(ps)
    d_b = ext_b(iota((64, 96), 1)) - parity_b(iota((64, 96), 0)) + HALO
    lane = iota((LANES, LANES), 1)
    d_c = ext_c(iota((LANES, LANES), 0)) - jnp.where(lane >= 64, lane - 64, lane) + HALO

    @pl.loop(0, VIEWS * RANK)
    def _(number):
        start = pl.multiple_of(number * 64, 64)
        wb[pl.ds(start, 64), :] = band(d_b, tap(number, 1)).astype(BF16)
        base = band(d_c, tap(number, 2))
        wc[number, 0:128, :] = jnp.where(lane < 64, base, 0.0).astype(BF16)
        wc[number, 128:256, :] = jnp.where(lane >= 64, base, 0.0).astype(BF16)


def build_rest(ps, mesh_row, wbt, wct, wa, wat_own, wat_far):
    tap = tap_of(ps)
    d_ct = ext_c(iota((64, LANES), 1)) - iota((64, LANES), 0) + HALO
    wct[...] = jnp.zeros_like(wct)

    @pl.loop(0, VIEWS * RANK)
    def _(number):
        base = band(d_ct, tap(number, 2)).astype(BF16)
        wct[number, 0:64, 0:128] = base
        wct[number, 64:128, 128:256] = base

    col = iota((96, LANES), 1)
    high = col >= 64
    d_bt = ext_b(iota((96, LANES), 0)) - parity_b(jnp.where(high, col - 64, col)) + HALO
    for pair in range(VIEWS * RANK // 2):
        low_tap, high_tap = tap(2 * pair, 1), tap(2 * pair + 1, 1)
        wbt[:, pair * LANES : (pair + 1) * LANES] = band(
            d_bt, lambda t: jnp.where(high, high_tap(t), low_tap(t))
        ).astype(BF16)

    def ext_a(place):
        inside = place - (64 + HALO) * (place >= 64).astype(I32) * mesh_row
        return jnp.where(place >= 64 + HALO, 1000, inside)

    second = iota((64, 2 * SPAN_A), 1) >= SPAN_A
    place = iota((64, 2 * SPAN_A), 1) - SPAN_A * second.astype(I32)
    d_a = ext_a(place) - iota((64, 2 * SPAN_A), 0) + HALO
    d_at = ext_a(iota((SPAN_A, 64), 0)) - iota((SPAN_A, 64), 1) + HALO

    @pl.loop(0, VIEWS)
    def _(view):
        first_tap, second_tap = tap(2 * view, 0), tap(2 * view + 1, 0)
        wa[view] = band(d_a, lambda t: jnp.where(second, second_tap(t), first_tap(t))).astype(BF16)
        for term, taps in enumerate((first_tap, second_tap)):
            base = band(d_at, taps).astype(BF16)
            wat_own[view, term * 64 : term * 64 + 64, :] = base[:64]
            wat_far[view, term * 16 : term * 16 + 16, :] = base[64:]


def kernel(
    n_gy,
    est_hbm,
    data_hbm,
    ps,
    owner,
    out,
    est,
    data,
    own,
    sib,
    slab,
    gx_in,
    gy_in,
    co_in,
    mid_f,
    mix_f,
    rows_t,
    t2,
    v2,
    wb,
    wbt,
    wc,
    wct,
    wa,
    wat_own,
    wat_far,
    keep_gx,
    part_gx,
    give_own,
    give_gx,
    give_gy,
    give_co,
    take_own,
    take_gx,
    take_gy,
    take_co,
    put_gx,
    get_gx,
    load_sem,
    send_sem,
    recv_sem,
):
    i, j, g = lax.axis_index("gx"), lax.axis_index("gy"), lax.axis_index("gz")
    sibling = (i, j, 1 - g)
    across = (1 - i, j, g)
    beside = [[(i, j + 2 * s - 1, g), (i, j + 2 * s - 1, 1 - g)] for s in range(2)]
    exists = (j > 0, j < n_gy - 1)

    toward = (pl.ds(0, WIDTH), pl.ds(FACE, WIDTH))
    parts = (*toward, pl.ds(WIDTH, FACE - WIDTH))
    load_est = [
        pltpu.make_async_copy(est_hbm.at[0, :, p], est.at[:, p], load_sem.at[n])
        for n, p in enumerate(parts)
    ]
    load_data = pltpu.make_async_copy(data_hbm.at[:, 0], data, load_sem.at[3])
    for item in load_est:
        item.start()
    load_data.start()

    def copy(number, src, dst, target):
        return pltpu.make_async_remote_copy(
            src_ref=src,
            dst_ref=dst,
            send_sem=send_sem.at[number],
            recv_sem=recv_sem.at[number],
            device_id=target,
            device_id_type=MESH,
        )

    def both_sides(action):
        for side in range(2):

            @pl.when(exists[side])
            def _(side=side):
                action(side)

    barrier = pltpu.get_barrier_semaphore()
    for target in (sibling, across):
        pl.semaphore_signal(barrier, inc=1, device_id=target, device_id_type=MESH)

    def greet(side):
        for core in range(2):
            pl.semaphore_signal(
                barrier, inc=1, device_id=beside[side][core], device_id_type=MESH
            )

    both_sides(greet)
    for item, lanes in zip(load_est[:2], toward):
        item.wait()
        own[:, lanes] = est[:, lanes].astype(BF16)
    waits = 2 + 2 * exists[0].astype(I32) + 2 * exists[1].astype(I32)
    pl.semaphore_wait(barrier, waits)

    inside = ((pl.ds(0, 16), pl.ds(0, WIDTH)), (pl.ds(32, 16), pl.ds(256, WIDTH)))
    send_sib = copy(0, own, sib, sibling)
    send_gx = copy(1, slab, gx_in.at[0], across)
    send_gy = [copy(2 + s, own.at[:, toward[s]], gy_in.at[1 - s, 0], beside[s][0]) for s in range(2)]
    pass_gx = copy(4, gx_in.at[0], gx_in.at[1], sibling)
    pass_gy = [copy(5 + s, gy_in.at[s, 0], gy_in.at[s, 1], sibling) for s in range(2)]
    pass_co = [
        [
            copy(7 + 2 * s + c, gx_in.at[0, *inside[s]], co_in.at[1 - s, c], beside[s][c])
            for c in range(2)
        ]
        for s in range(2)
    ]

    def arrived(number, dst):
        copy(number, dst, dst, sibling).wait_recv()

    both_sides(lambda s: send_gy[s].start())
    load_est[2].wait()
    own[:, parts[2]] = est[:, parts[2]].astype(BF16)
    send_sib.start()

    row = i.astype(F32)
    edge = est[53:64, :] * (1.0 - row) + est[0:HALO, :] * row
    slab[...] = jnp.concatenate(
        [edge[:, q * QUARTER : (q + 1) * QUARTER] for q in range(4)] + [jnp.zeros((4, QUARTER), F32)],
        axis=0,
    ).astype(BF16)

    for side in range(2):

        @pl.when(jnp.logical_not(exists[side]))
        def _(side=side):
            gy_in[side] = jnp.zeros(gy_in.shape[1:], BF16)
            co_in[side] = jnp.zeros(co_in.shape[1:], BF16)
            take_co[side] = jnp.zeros(take_co.shape[1:], BF16)

    def column(row, col):
        col = jnp.minimum(jnp.maximum(col, 0), n_gy - 1)
        codes = [owner[row, k, col] for k in range(PILLAR)]
        found = []
        for code in (g, 1 - g):
            hits = [(codes[k] == code).astype(I32) for k in range(PILLAR)]
            found.append((sum(hits), sum(k * hits[k] for k in range(PILLAR))))
        return found

    home = column(i, j)
    valid, height = home[0]

    def factors(entry, there=None):
        present, level = entry
        live = present * valid
        if there is not None:
            live = live * there.astype(I32)
        at = [(live * (level - height == d).astype(I32)).astype(F32) for d in (0, 1, -1)]
        lane_low = (iota((1, LANES), 1) & 63) < 32
        return at[0], jnp.where(lane_low, at[1], at[2])

    f_sib = factors(home[1])
    f_gx = [factors(e) for e in column(1 - i, j)]
    f_gy = [[factors(e, exists[s]) for e in column(i, j + 2 * s - 1)] for s in range(2)]
    f_co = [[factors(e, exists[s]) for e in column(1 - i, j + 2 * s - 1)] for s in range(2)]
    live = valid.astype(F32)

    build_forward(ps, wb, wc)
    build_rest(ps, i, wbt, wct, wa, wat_own, wat_far)
    send_gx.start()

    def place(first_row, count, pair, mid, mix):
        mid_f[pl.ds(first_row * STEP_F + pair, count, stride=STEP_F), :] = mid
        mix_f[pl.ds(first_row * STEP_F + pair, count, stride=STEP_F), :] = mix

    def tile(number):
        return pl.ds(pl.multiple_of(number * LANES, LANES), LANES)

    def blend(pieces, factor):
        first, second = pieces[0].astype(F32), pieces[1].astype(F32)
        return (
            first * factor[0][0] + second * factor[1][0],
            first * factor[0][1] + second * factor[1][1],
        )

    for pair in range(44, PAIRS):
        place(0, SPAN_A, pair, jnp.zeros((SPAN_A, LANES), F32), jnp.zeros((SPAN_A, LANES), F32))

    first_pair = (38, 32)

    send_sib.wait_recv()

    @pl.loop(0, 32)
    def _(pair):
        place(0, 64, pair, own[:, tile(pair)].astype(F32), sib[:, tile(pair)].astype(F32) * f_sib[1])

    for side in range(2):

        @pl.when(exists[side])
        def _(side=side):
            arrived(3 - side, gy_in.at[side, 0])
            pass_gy[side].start()


    both_sides(lambda s: pass_gy[s].wait_recv())
    for side in range(2):
        for pair in range(6):
            lanes = pl.ds(pair * LANES, LANES)
            mid, mix = blend([gy_in[side, k, :, lanes] for k in range(2)], f_gy[side])
            place(0, 64, first_pair[side] + pair, mid, mix)

    low = iota((PAIRS, LANES), 1) < 64

    def forward_chunk(chunk):
        for two in range(CHUNK // 2):
            parts = []
            for one in range(2):
                start = pl.multiple_of((chunk * CHUNK + two * 2 + one) * STEP_F, 8)
                mid, mix = mid_f[pl.ds(start, PAIRS), :], mix_f[pl.ds(start, PAIRS), :]
                even = jnp.where(low, mid, pltpu.roll(mix, 64, 1))
                odd = jnp.where(low, pltpu.roll(mid, 64, 1), mix)
                parts.append(jnp.concatenate([even, odd], axis=0).astype(BF16))
            first = jnp.dot(wb[...], jnp.concatenate(parts, axis=1), preferred_element_type=F32)
            rows_t[:, two * 256 : two * 256 + 256] = first.astype(BF16)
        for number in range(VIEWS * RANK):
            view, term = number // RANK, number % RANK
            top = number * 64
            block = jnp.concatenate(
                [
                    jnp.concatenate(
                        [
                            rows_t[top : top + 32, a * LANES : (a + 1) * LANES],
                            rows_t[top + 32 : top + 64, a * LANES : (a + 1) * LANES],
                        ],
                        axis=1,
                    )
                    for a in range(CHUNK)
                ],
                axis=0,
            )
            second = jnp.dot(block, wc[number], preferred_element_type=F32)
            for a in range(CHUNK):
                start = view * 32 * STEP_T + term * SPAN_A + chunk * CHUNK + a
                t2[pl.ds(start, 32, stride=STEP_T), :] = second[a * 32 : a * 32 + 32, :]

    pl.loop(0, 3)(forward_chunk)

    arrived(1, gx_in.at[0])
    pass_gx.start()

    def pass_ends(side):
        for core in range(2):
            pass_co[side][core].start()

    both_sides(pass_ends)
    forward_chunk(3)

    pass_gx.wait_recv()
    for side in range(2):

        @pl.when(exists[side])
        def _(side=side):
            for core in range(2):
                arrived(7 + 2 * (1 - side) + core, co_in.at[side, core])

    def lengthen(rows):
        return jnp.concatenate([rows, jnp.zeros((16 - HALO, rows.shape[1]), F32)], axis=0)

    for q in range(4):
        rows = [gx_in[k].astype(F32)[HALO * q : HALO * q + HALO] for k in range(2)]
        for number in range(8):
            lanes = slice(number * LANES, (number + 1) * LANES)
            mid, mix = blend([lengthen(rows[k][:, lanes]) for k in range(2)], f_gx)
            place(64, 16, q * 8 + number, mid, mix)

    for side in range(2):
        down = 1 - side
        for pair in range(6):
            lanes = slice(pair * LANES, (pair + 1) * LANES)
            rows = [co_in[side, k, :, lanes].astype(F32)[down : down + HALO] for k in range(2)]
            mid, mix = blend([lengthen(r) for r in rows], f_co[side])
            place(64, 16, first_pair[side] + pair, mid, mix)

    forward_chunk(64 // CHUNK)
    load_data.wait()

    def adjoint_front(view, back, count, first):
        for term in range(RANK):
            rows = back[term * count : (term + 1) * count]
            block = jnp.concatenate([rows[:, k * LANES : (k + 1) * LANES] for k in range(32)], axis=0)
            wide = jnp.dot(block, wct[view * RANK + term], preferred_element_type=F32)
            for k in range(32):
                for odd in range(2):
                    at = first * STEP_V + (view * RANK + term) * 64 + odd * 32 + k
                    v2[pl.ds(at, count, stride=STEP_V), :] = wide[
                        k * count : (k + 1) * count, odd * LANES : (odd + 1) * LANES
                    ]

    def turn_far(view):
        start = pl.multiple_of(view * 32 * STEP_T, 8)
        fields = jnp.concatenate(
            [t2[pl.ds(start + k * STEP_T, 2 * SPAN_A), :].astype(BF16) for k in range(32)], axis=1
        )
        blurred = jnp.dot(wa[view], fields, preferred_element_type=F32)
        ratio = (data[view].astype(F32) / jnp.maximum(blurred, FLOOR) * live).astype(BF16)
        data[view] = ratio
        back = jnp.dot(wat_far[view], ratio, preferred_element_type=F32).astype(BF16)
        adjoint_front(view, back, 16, 64)

    def turn_own(view):
        back = jnp.dot(wat_own[view], data[view], preferred_element_type=F32).astype(BF16)
        adjoint_front(view, back, 64, 0)

    pl.loop(0, VIEWS)(turn_far)

    def adjoint_rows(step):
        start = pl.multiple_of(step * DUO * STEP_V, 8)
        fields = jnp.concatenate(
            [v2[pl.ds(start + k * STEP_V, 512), :].astype(BF16) for k in range(DUO)], axis=1
        )
        spread = jnp.dot(wbt[...], fields, preferred_element_type=F32)
        for k in range(DUO):
            even = spread[0:PAIRS, k * LANES : (k + 1) * LANES]
            odd = spread[PAIRS : 2 * PAIRS, k * LANES : (k + 1) * LANES]
            at = pl.multiple_of((step * DUO + k) * STEP_F, 8)
            mid_f[pl.ds(at, PAIRS), :] = jnp.where(low, even, pltpu.roll(odd, 64, 1))
            mix_f[pl.ds(at, PAIRS), :] = jnp.where(low, pltpu.roll(even, 64, 1), odd)

    def fetch(first_row, count, pair):
        at = pl.ds(first_row * STEP_F + pair, count, stride=STEP_F)
        return mid_f[at, :], mix_f[at, :]

    adjoint_rows(64 // DUO)
    for q in range(4):
        for number in range(8):
            lanes = slice(number * LANES, (number + 1) * LANES)
            mid, mix = fetch(64, 16, q * 8 + number)
            mid, mix = mid[:HALO], mix[:HALO]
            keep_gx[HALO * q : HALO * q + HALO, lanes] = mid * f_gx[0][0] + mix * f_gx[0][1]
            part_gx[HALO * q : HALO * q + HALO, lanes] = mid * f_gx[1][0] + mix * f_gx[1][1]
    keep_gx[44:48, :] = jnp.zeros((4, QUARTER), F32)
    part_gx[44:48, :] = jnp.zeros((4, QUARTER), F32)
    give_gx[...] = part_gx[...].astype(BF16)
    share_gx = copy(11, give_gx, take_gx, sibling)
    share_gx.start()

    for side in range(2):
        down = 1 - side
        for pair in range(6):
            lanes = slice(pair * LANES, (pair + 1) * LANES)
            mid, mix = fetch(64, 16, first_pair[side] + pair)
            for core in range(2):
                factor = f_co[side][core]
                rows = (mid * factor[0] + mix * factor[1])[:HALO]
                parts = [jnp.zeros((down, LANES), F32)] if down else []
                parts += [rows, jnp.zeros((16 - HALO - down, LANES), F32)]
                give_co[side, core, :, lanes] = jnp.concatenate(parts, axis=0).astype(BF16)

    send_co = [
        [
            copy(12 + 2 * s + c, give_co.at[s, c], take_co.at[1 - s, c], beside[s][c])
            for c in range(2)
        ]
        for s in range(2)
    ]

    def send_ends(side):
        for core in range(2):
            send_co[side][core].start()

    both_sides(send_ends)
    final_gx = copy(16, put_gx, get_gx, across)

    def finish_gx():
        share_gx.wait_recv()
        keep_gx[...] = keep_gx[...] + take_gx[...].astype(F32)
        for side in range(2):

            @pl.when(exists[side])
            def _(side=side):
                for core in range(2):
                    arrived(12 + 2 * (1 - side) + core, take_co.at[side, core])

        for side in range(2):
            ends = take_co[side, 0].astype(F32) + take_co[side, 1].astype(F32)
            keep_gx[inside[side]] = keep_gx[inside[side]] + ends
        put_gx[...] = keep_gx[...].astype(BF16)
        final_gx.start()

    pl.loop(0, VIEWS - 1)(turn_own)
    finish_gx()
    turn_own(VIEWS - 1)

    scale = live / VIEWS
    send_sides = [
        [
            [
                copy(17 + 4 * k + 2 * s + c, give_gy.at[k, s, c], take_gy.at[k, 1 - s, c], beside[s][c])
                for c in range(2)
            ]
            for s in range(2)
        ]
        for k in range(4)
    ]
    share_own = [
        copy(33 + k, give_own.at[pl.ds(16 * k, 16)], take_own.at[pl.ds(16 * k, 16)], sibling)
        for k in range(4)
    ]

    def own_rows(k):
        adjoint_rows(k)
        for side in range(2):
            for pair in range(6):
                lanes = pl.ds(pair * LANES, LANES)
                mid, mix = fetch(16 * k, 16, first_pair[side] + pair)
                for core in range(2):
                    factor = f_gy[side][core]
                    give_gy[k, side, core, :, lanes] = (mid * factor[0] + mix * factor[1]).astype(BF16)

        def send(side):
            for core in range(2):
                send_sides[k][side][core].start()

        both_sides(send)

    def own_block(k):
        for pair in range(32):
            lanes = pl.ds(pair * LANES, LANES)
            mid, mix = fetch(16 * k, 16, pair)
            out[0, 16 * k : 16 * k + 16, lanes] = mid
            give_own[16 * k : 16 * k + 16, lanes] = (mix * f_sib[1]).astype(BF16)
        share_own[k].start()

    def finish_own(k):
        share_own[k].wait_recv()
        rows = slice(16 * k, 16 * k + 16)
        out[0, rows] = (out[0, rows] + take_own[rows].astype(F32)) * (est[rows] * scale)

    for k in range(4):
        own_rows(k)
    for k in range(4):
        own_block(k)
        if k:
            finish_own(k - 1)
    finish_own(3)

    final_gx.wait_recv()
    for q in range(4):
        rows = get_gx[...].astype(F32)[HALO * q : HALO * q + HALO]
        gap = jnp.zeros((16 - HALO, QUARTER), F32)
        lanes = pl.ds(q * QUARTER, QUARTER)
        low_rows = jnp.concatenate([rows, gap], axis=0) * (row * scale)
        high_rows = jnp.concatenate([gap, rows], axis=0) * ((1.0 - row) * scale)
        out[0, 0:16, lanes] = out[0, 0:16, lanes] + low_rows * est[0:16, lanes]
        out[0, 48:64, lanes] = out[0, 48:64, lanes] + high_rows * est[48:64, lanes]
    for k in range(4):
        for side in range(2):

            @pl.when(exists[side])
            def _(k=k, side=side):
                for core in range(2):
                    arrived(17 + 4 * k + 2 * (1 - side) + core, take_gy.at[k, side, core])
                rows = slice(16 * k, 16 * k + 16)
                total = take_gy[k, side, 0].astype(F32) + take_gy[k, side, 1].astype(F32)
                out[0, rows, toward[side]] = out[0, rows, toward[side]] + total * (
                    est[rows, toward[side]] * scale
                )

    for item in [send_sib, send_gx, pass_gx, share_gx, final_gx] + share_own:
        item.wait_send()

    def drain(side):
        items = [send_gy[side], pass_gy[side], *pass_co[side], *send_co[side]]
        for item in items + [c for k in range(4) for c in send_sides[k][side]]:
            item.wait_send()

    both_sides(drain)


def solution(mesh):
    n_gy = mesh.shape["gy"]

    def body(estimate, views_data, point_spread, block_owner):
        slab, ends = (48, QUARTER), (2, 2, 16, WIDTH)
        sides = (4, 2, 2, 16, WIDTH)
        scratch = [
            ((64, 4096), F32),
            ((VIEWS, 64, 4096), BF16),
            ((64, 4096), BF16),
            ((64, 4096), BF16),
            (slab, BF16),
            ((2, *slab), BF16),
            ((2, 2, 64, WIDTH), BF16),
            (ends, BF16),
            ((SPAN_A * STEP_F, LANES), F32),
            ((SPAN_A * STEP_F, LANES), F32),
            ((512, CHUNK * LANES), BF16),
            ((VIEWS * 32 * STEP_T, LANES), F32),
            ((SPAN_A * STEP_V, LANES), F32),
            ((512, 96), BF16),
            ((96, 512), BF16),
            ((8, 256, 128), BF16),
            ((8, 128, 256), BF16),
            ((VIEWS, 64, 2 * SPAN_A), BF16),
            ((VIEWS, RANK * 64, 64), BF16),
            ((VIEWS, RANK * 16, 64), BF16),
            (slab, F32),
            (slab, F32),
            ((64, 4096), BF16),
            (slab, BF16),
            (sides, BF16),
            (ends, BF16),
            ((64, 4096), BF16),
            (slab, BF16),
            (sides, BF16),
            (ends, BF16),
            (slab, BF16),
            (slab, BF16),
        ]
        any_spec = pl.BlockSpec(memory_space=pl.ANY)
        smem = pl.BlockSpec(memory_space=pltpu.SMEM)
        return pl.pallas_call(
            functools.partial(kernel, n_gy),
            out_shape=jax.ShapeDtypeStruct((1, 64, 4096), F32),
            in_specs=[any_spec, any_spec, smem, smem],
            out_specs=pl.BlockSpec(memory_space=pltpu.VMEM),
            scratch_shapes=[pltpu.VMEM(shape, kind) for shape, kind in scratch]
            + [
                pltpu.SemaphoreType.DMA((4,)),
                pltpu.SemaphoreType.DMA((37,)),
                pltpu.SemaphoreType.DMA((37,)),
            ],
            compiler_params=pltpu.CompilerParams(
                collective_id=0, has_side_effects=True, vmem_limit_bytes=52 * 2**20
            ),
        )(
            estimate,
            views_data,
            point_spread.transpose(0, 2, 1, 3),
            block_owner.transpose(0, 2, 1),
        )

    placed = (P(("gx", "gy", "gz"), None, None), P(None, ("gx", "gy", "gz"), None, None), P(), P())
    return jax.shard_map(
        body,
        mesh=mesh,
        in_specs=placed,
        out_specs=P(("gx", "gy", "gz"), None, None),
        check_vma=False,
    )
```

```python
import functools

import jax
import jax.numpy as jnp
from jax import lax
from jax.experimental import pallas as pl
from jax.experimental.pallas import tpu as pltpu
from jax.sharding import PartitionSpec as P

MESH = pl.DeviceIdType.MESH
F32, BF16, I32 = jnp.float32, jnp.bfloat16, jnp.int32
BLOCK, TAPS, HALO, RANK, VIEWS, PILLAR = 64, 23, 11, 2, 4, 4
FLOOR = 0.5
SPAN_A = 80
PAIRS = 48
STEP_F, STEP_T, STEP_V = 56, 168, 520
LANES = 128
WIDTH = 768
FACE = 3328
QUARTER = 1024
CHUNK = 16
DUO = 16


def iota(shape, dim):
    return lax.broadcasted_iota(I32, shape, dim)


def band(distance, tap):
    total = jnp.zeros(distance.shape, F32)
    for t in range(TAPS):
        total = jnp.where(distance == t, tap(t), total)
    return total


def ext_c(lane):
    return jnp.where(lane < 96, lane, lane - LANES)


def parity_b(row):
    return jnp.where(row < 32, 2 * row, 2 * row - 63)


def ext_b(row):
    odd = (row >= PAIRS).astype(I32)
    pair = row - PAIRS * odd
    value = 2 * pair + odd - 88 * (pair >= 38).astype(I32)
    return jnp.where(pair >= 44, 1000, value)


def tap_of(ps):
    def tap(number, axis):
        return lambda t: ps[number // RANK, axis, number % RANK, t]

    return tap


def build_forward(ps, wb, wc):
    tap = tap_of(ps)
    d_b = ext_b(iota((64, 96), 1)) - parity_b(iota((64, 96), 0)) + HALO
    lane = iota((LANES, LANES), 1)
    d_c = ext_c(iota((LANES, LANES), 0)) - jnp.where(lane >= 64, lane - 64, lane) + HALO

    @pl.loop(0, VIEWS * RANK)
    def _(number):
        start = pl.multiple_of(number * 64, 64)
        wb[pl.ds(start, 64), :] = band(d_b, tap(number, 1)).astype(BF16)
        base = band(d_c, tap(number, 2))
        wc[number, 0:128, :] = jnp.where(lane < 64, base, 0.0).astype(BF16)
        wc[number, 128:256, :] = jnp.where(lane >= 64, base, 0.0).astype(BF16)


def build_rest(ps, mesh_row, wbt, wct, wa, wat_own, wat_far):
    tap = tap_of(ps)
    d_ct = ext_c(iota((64, LANES), 1)) - iota((64, LANES), 0) + HALO
    wct[...] = jnp.zeros_like(wct)

    @pl.loop(0, VIEWS * RANK)
    def _(number):
        base = band(d_ct, tap(number, 2)).astype(BF16)
        wct[number, 0:64, 0:128] = base
        wct[number, 64:128, 128:256] = base

    col = iota((96, LANES), 1)
    high = col >= 64
    d_bt = ext_b(iota((96, LANES), 0)) - parity_b(jnp.where(high, col - 64, col)) + HALO
    for pair in range(VIEWS * RANK // 2):
        low_tap, high_tap = tap(2 * pair, 1), tap(2 * pair + 1, 1)
        wbt[:, pair * LANES : (pair + 1) * LANES] = band(
            d_bt, lambda t: jnp.where(high, high_tap(t), low_tap(t))
        ).astype(BF16)

    def ext_a(place):
        inside = place - (64 + HALO) * (place >= 64).astype(I32) * mesh_row
        return jnp.where(place >= 64 + HALO, 1000, inside)

    second = iota((64, 2 * SPAN_A), 1) >= SPAN_A
    place = iota((64, 2 * SPAN_A), 1) - SPAN_A * second.astype(I32)
    d_a = ext_a(place) - iota((64, 2 * SPAN_A), 0) + HALO
    d_at = ext_a(iota((SPAN_A, 64), 0)) - iota((SPAN_A, 64), 1) + HALO

    @pl.loop(0, VIEWS)
    def _(view):
        first_tap, second_tap = tap(2 * view, 0), tap(2 * view + 1, 0)
        wa[view] = band(d_a, lambda t: jnp.where(second, second_tap(t), first_tap(t))).astype(BF16)
        for term, taps in enumerate((first_tap, second_tap)):
            base = band(d_at, taps).astype(BF16)
            wat_own[view, term * 64 : term * 64 + 64, :] = base[:64]
            wat_far[view, term * 16 : term * 16 + 16, :] = base[64:]


def kernel(
    n_gy,
    est_hbm,
    data_hbm,
    ps,
    owner,
    out,
    est,
    data,
    own,
    sib,
    slab,
    gx_in,
    gy_in,
    co_in,
    mid_f,
    mix_f,
    rows_t,
    t2,
    v2,
    wb,
    wbt,
    wc,
    wct,
    wa,
    wat_own,
    wat_far,
    keep_gx,
    part_gx,
    give_own,
    give_gx,
    give_gy,
    give_co,
    take_own,
    take_gx,
    take_gy,
    take_co,
    put_gx,
    get_gx,
    load_sem,
    send_sem,
    recv_sem,
):
    i, j, g = lax.axis_index("gx"), lax.axis_index("gy"), lax.axis_index("gz")
    sibling = (i, j, 1 - g)
    across = (1 - i, j, g)
    beside = [[(i, j + 2 * s - 1, g), (i, j + 2 * s - 1, 1 - g)] for s in range(2)]
    exists = (j > 0, j < n_gy - 1)

    toward = (pl.ds(0, WIDTH), pl.ds(FACE, WIDTH))
    parts = (*toward, pl.ds(WIDTH, FACE - WIDTH))
    load_est = [
        pltpu.make_async_copy(est_hbm.at[0, :, p], est.at[:, p], load_sem.at[n])
        for n, p in enumerate(parts)
    ]
    load_data = pltpu.make_async_copy(data_hbm.at[:, 0], data, load_sem.at[3])
    for item in load_est:
        item.start()
    load_data.start()

    def copy(number, src, dst, target):
        return pltpu.make_async_remote_copy(
            src_ref=src,
            dst_ref=dst,
            send_sem=send_sem.at[number],
            recv_sem=recv_sem.at[number],
            device_id=target,
            device_id_type=MESH,
        )

    def both_sides(action):
        for side in range(2):

            @pl.when(exists[side])
            def _(side=side):
                action(side)

    barrier = pltpu.get_barrier_semaphore()
    for target in (sibling, across):
        pl.semaphore_signal(barrier, inc=1, device_id=target, device_id_type=MESH)

    def greet(side):
        for core in range(2):
            pl.semaphore_signal(
                barrier, inc=1, device_id=beside[side][core], device_id_type=MESH
            )

    both_sides(greet)
    for item, lanes in zip(load_est[:2], toward):
        item.wait()
        own[:, lanes] = est[:, lanes].astype(BF16)
    waits = 2 + 2 * exists[0].astype(I32) + 2 * exists[1].astype(I32)
    pl.semaphore_wait(barrier, waits)

    inside = ((pl.ds(0, 16), pl.ds(0, WIDTH)), (pl.ds(32, 16), pl.ds(256, WIDTH)))
    send_sib = copy(0, own, sib, sibling)
    send_gx = copy(1, slab, gx_in.at[0], across)
    rows_of = [pl.ds(16 * k, 16) for k in range(4)]
    send_gy = [
        [
            copy(37 + 2 * k + s, own.at[rows_of[k], toward[s]], gy_in.at[1 - s, 0, rows_of[k]], beside[s][0])
            for s in range(2)
        ]
        for k in range(4)
    ]
    pass_gx = copy(4, gx_in.at[0], gx_in.at[1], sibling)
    pass_gy = [
        [
            copy(45 + 2 * k + s, gy_in.at[s, 0, rows_of[k]], gy_in.at[s, 1, rows_of[k]], sibling)
            for s in range(2)
        ]
        for k in range(4)
    ]
    pass_co = [
        [
            copy(7 + 2 * s + c, gx_in.at[0, *inside[s]], co_in.at[1 - s, c], beside[s][c])
            for c in range(2)
        ]
        for s in range(2)
    ]

    def arrived(number, dst):
        copy(number, dst, dst, sibling).wait_recv()


    def send_rows(side):
        for k in range(4):
            send_gy[k][side].start()

    both_sides(send_rows)
    load_est[2].wait()
    own[:, parts[2]] = est[:, parts[2]].astype(BF16)
    send_sib.start()

    row = i.astype(F32)
    edge = est[53:64, :] * (1.0 - row) + est[0:HALO, :] * row
    slab[...] = jnp.concatenate(
        [edge[:, q * QUARTER : (q + 1) * QUARTER] for q in range(4)] + [jnp.zeros((4, QUARTER), F32)],
        axis=0,
    ).astype(BF16)

    for side in range(2):

        @pl.when(jnp.logical_not(exists[side]))
        def _(side=side):
            gy_in[side] = jnp.zeros(gy_in.shape[1:], BF16)
            co_in[side] = jnp.zeros(co_in.shape[1:], BF16)
            take_co[side] = jnp.zeros(take_co.shape[1:], BF16)

    def column(row, col):
        col = jnp.minimum(jnp.maximum(col, 0), n_gy - 1)
        codes = [owner[row, k, col] for k in range(PILLAR)]
        found = []
        for code in (g, 1 - g):
            hits = [(codes[k] == code).astype(I32) for k in range(PILLAR)]
            found.append((sum(hits), sum(k * hits[k] for k in range(PILLAR))))
        return found

    home = column(i, j)
    valid, height = home[0]

    def factors(entry, there=None):
        present, level = entry
        live = present * valid
        if there is not None:
            live = live * there.astype(I32)
        at = [(live * (level - height == d).astype(I32)).astype(F32) for d in (0, 1, -1)]
        lane_low = (iota((1, LANES), 1) & 63) < 32
        return at[0], jnp.where(lane_low, at[1], at[2])

    f_sib = factors(home[1])
    f_gx = [factors(e) for e in column(1 - i, j)]
    f_gy = [[factors(e, exists[s]) for e in column(i, j + 2 * s - 1)] for s in range(2)]
    f_co = [[factors(e, exists[s]) for e in column(1 - i, j + 2 * s - 1)] for s in range(2)]
    live = valid.astype(F32)

    build_forward(ps, wb, wc)
    send_gx.start()
    build_rest(ps, i, wbt, wct, wa, wat_own, wat_far)

    def place(first_row, count, pair, mid, mix):
        mid_f[pl.ds(first_row * STEP_F + pair, count, stride=STEP_F), :] = mid
        mix_f[pl.ds(first_row * STEP_F + pair, count, stride=STEP_F), :] = mix

    def tile(number):
        return pl.ds(pl.multiple_of(number * LANES, LANES), LANES)

    def blend(pieces, factor):
        first, second = pieces[0].astype(F32), pieces[1].astype(F32)
        return (
            first * factor[0][0] + second * factor[1][0],
            first * factor[0][1] + second * factor[1][1],
        )

    for pair in range(44, PAIRS):
        place(0, SPAN_A, pair, jnp.zeros((SPAN_A, LANES), F32), jnp.zeros((SPAN_A, LANES), F32))

    first_pair = (38, 32)

    send_sib.wait_recv()

    @pl.loop(0, 32)
    def _(pair):
        place(0, 64, pair, own[:, tile(pair)].astype(F32), sib[:, tile(pair)].astype(F32) * f_sib[1])

    def hand_on(k):
        for side in range(2):

            @pl.when(exists[side])
            def _(side=side):
                arrived(37 + 2 * k + 1 - side, gy_in.at[side, 0, rows_of[k]])
                pass_gy[k][side].start()

    def select_rows(k):
        both_sides(lambda s: pass_gy[k][s].wait_recv())
        for side in range(2):
            for pair in range(6):
                lanes = pl.ds(pair * LANES, LANES)
                mid, mix = blend([gy_in[side, c, rows_of[k], lanes] for c in range(2)], f_gy[side])
                place(16 * k, 16, first_pair[side] + pair, mid, mix)

    low = iota((PAIRS, LANES), 1) < 64

    def forward_chunk(chunk):
        for two in range(CHUNK // 2):
            parts = []
            for one in range(2):
                start = pl.multiple_of((chunk * CHUNK + two * 2 + one) * STEP_F, 8)
                mid, mix = mid_f[pl.ds(start, PAIRS), :], mix_f[pl.ds(start, PAIRS), :]
                even = jnp.where(low, mid, pltpu.roll(mix, 64, 1))
                odd = jnp.where(low, pltpu.roll(mid, 64, 1), mix)
                parts.append(jnp.concatenate([even, odd], axis=0).astype(BF16))
            first = jnp.dot(wb[...], jnp.concatenate(parts, axis=1), preferred_element_type=F32)
            rows_t[:, two * 256 : two * 256 + 256] = first.astype(BF16)
        for number in range(VIEWS * RANK):
            view, term = number // RANK, number % RANK
            top = number * 64
            block = jnp.concatenate(
                [
                    jnp.concatenate(
                        [
                            rows_t[top : top + 32, a * LANES : (a + 1) * LANES],
                            rows_t[top + 32 : top + 64, a * LANES : (a + 1) * LANES],
                        ],
                        axis=1,
                    )
                    for a in range(CHUNK)
                ],
                axis=0,
            )
            second = jnp.dot(block, wc[number], preferred_element_type=F32)
            for a in range(CHUNK):
                start = view * 32 * STEP_T + term * SPAN_A + chunk * CHUNK + a
                t2[pl.ds(start, 32, stride=STEP_T), :] = second[a * 32 : a * 32 + 32, :]

    hand_on(0)
    for k in range(3):
        hand_on(k + 1)
        select_rows(k)
        forward_chunk(k)

    arrived(1, gx_in.at[0])
    pass_gx.start()

    def pass_ends(side):
        for core in range(2):
            pass_co[side][core].start()

    both_sides(pass_ends)
    select_rows(3)
    forward_chunk(3)

    pass_gx.wait_recv()
    for side in range(2):

        @pl.when(exists[side])
        def _(side=side):
            for core in range(2):
                arrived(7 + 2 * (1 - side) + core, co_in.at[side, core])

    def lengthen(rows):
        return jnp.concatenate([rows, jnp.zeros((16 - HALO, rows.shape[1]), F32)], axis=0)

    for q in range(4):
        rows = [gx_in[k].astype(F32)[HALO * q : HALO * q + HALO] for k in range(2)]
        for number in range(8):
            lanes = slice(number * LANES, (number + 1) * LANES)
            mid, mix = blend([lengthen(rows[k][:, lanes]) for k in range(2)], f_gx)
            place(64, 16, q * 8 + number, mid, mix)

    for side in range(2):
        down = 1 - side
        for pair in range(6):
            lanes = slice(pair * LANES, (pair + 1) * LANES)
            rows = [co_in[side, k, :, lanes].astype(F32)[down : down + HALO] for k in range(2)]
            mid, mix = blend([lengthen(r) for r in rows], f_co[side])
            place(64, 16, first_pair[side] + pair, mid, mix)

    forward_chunk(64 // CHUNK)
    load_data.wait()

    def adjoint_front(view, back, count, first):
        for term in range(RANK):
            rows = back[term * count : (term + 1) * count]
            block = jnp.concatenate([rows[:, k * LANES : (k + 1) * LANES] for k in range(32)], axis=0)
            wide = jnp.dot(block, wct[view * RANK + term], preferred_element_type=F32)
            for k in range(32):
                for odd in range(2):
                    at = first * STEP_V + (view * RANK + term) * 64 + odd * 32 + k
                    v2[pl.ds(at, count, stride=STEP_V), :] = wide[
                        k * count : (k + 1) * count, odd * LANES : (odd + 1) * LANES
                    ]

    def turn_far(view):
        start = pl.multiple_of(view * 32 * STEP_T, 8)
        fields = jnp.concatenate(
            [t2[pl.ds(start + k * STEP_T, 2 * SPAN_A), :].astype(BF16) for k in range(32)], axis=1
        )
        blurred = jnp.dot(wa[view], fields, preferred_element_type=F32)
        ratio = (data[view].astype(F32) / jnp.maximum(blurred, FLOOR) * live).astype(BF16)
        data[view] = ratio
        back = jnp.dot(wat_far[view], ratio, preferred_element_type=F32).astype(BF16)
        adjoint_front(view, back, 16, 64)

    def turn_own(view):
        back = jnp.dot(wat_own[view], data[view], preferred_element_type=F32).astype(BF16)
        adjoint_front(view, back, 64, 0)

    pl.loop(0, VIEWS)(turn_far)

    def adjoint_rows(step):
        start = pl.multiple_of(step * DUO * STEP_V, 8)
        fields = jnp.concatenate(
            [v2[pl.ds(start + k * STEP_V, 512), :].astype(BF16) for k in range(DUO)], axis=1
        )
        spread = jnp.dot(wbt[...], fields, preferred_element_type=F32)
        for k in range(DUO):
            even = spread[0:PAIRS, k * LANES : (k + 1) * LANES]
            odd = spread[PAIRS : 2 * PAIRS, k * LANES : (k + 1) * LANES]
            at = pl.multiple_of((step * DUO + k) * STEP_F, 8)
            mid_f[pl.ds(at, PAIRS), :] = jnp.where(low, even, pltpu.roll(odd, 64, 1))
            mix_f[pl.ds(at, PAIRS), :] = jnp.where(low, pltpu.roll(even, 64, 1), odd)

    def fetch(first_row, count, pair):
        at = pl.ds(first_row * STEP_F + pair, count, stride=STEP_F)
        return mid_f[at, :], mix_f[at, :]

    adjoint_rows(64 // DUO)
    for q in range(4):
        for number in range(8):
            lanes = slice(number * LANES, (number + 1) * LANES)
            mid, mix = fetch(64, 16, q * 8 + number)
            mid, mix = mid[:HALO], mix[:HALO]
            keep_gx[HALO * q : HALO * q + HALO, lanes] = mid * f_gx[0][0] + mix * f_gx[0][1]
            part_gx[HALO * q : HALO * q + HALO, lanes] = mid * f_gx[1][0] + mix * f_gx[1][1]
    keep_gx[44:48, :] = jnp.zeros((4, QUARTER), F32)
    part_gx[44:48, :] = jnp.zeros((4, QUARTER), F32)
    give_gx[...] = part_gx[...].astype(BF16)
    share_gx = copy(11, give_gx, take_gx, sibling)
    share_gx.start()

    for side in range(2):
        down = 1 - side
        for pair in range(6):
            lanes = slice(pair * LANES, (pair + 1) * LANES)
            mid, mix = fetch(64, 16, first_pair[side] + pair)
            for core in range(2):
                factor = f_co[side][core]
                rows = (mid * factor[0] + mix * factor[1])[:HALO]
                parts = [jnp.zeros((down, LANES), F32)] if down else []
                parts += [rows, jnp.zeros((16 - HALO - down, LANES), F32)]
                give_co[side, core, :, lanes] = jnp.concatenate(parts, axis=0).astype(BF16)

    send_co = [
        [
            copy(12 + 2 * s + c, give_co.at[s, c], take_co.at[1 - s, c], beside[s][c])
            for c in range(2)
        ]
        for s in range(2)
    ]

    def send_ends(side):
        for core in range(2):
            send_co[side][core].start()

    both_sides(send_ends)
    final_gx = copy(16, put_gx, get_gx, across)

    def finish_gx():
        share_gx.wait_recv()
        keep_gx[...] = keep_gx[...] + take_gx[...].astype(F32)
        for side in range(2):

            @pl.when(exists[side])
            def _(side=side):
                for core in range(2):
                    arrived(12 + 2 * (1 - side) + core, take_co.at[side, core])

        for side in range(2):
            ends = take_co[side, 0].astype(F32) + take_co[side, 1].astype(F32)
            keep_gx[inside[side]] = keep_gx[inside[side]] + ends
        put_gx[...] = keep_gx[...].astype(BF16)
        final_gx.start()

    pl.loop(0, VIEWS - 1)(turn_own)
    finish_gx()
    turn_own(VIEWS - 1)

    scale = live / VIEWS
    send_sides = [
        [
            [
                copy(17 + 4 * k + 2 * s + c, give_gy.at[k, s, c], take_gy.at[k, 1 - s, c], beside[s][c])
                for c in range(2)
            ]
            for s in range(2)
        ]
        for k in range(4)
    ]
    share_own = [
        copy(33 + k, give_own.at[pl.ds(16 * k, 16)], take_own.at[pl.ds(16 * k, 16)], sibling)
        for k in range(4)
    ]

    def own_rows(k):
        adjoint_rows(k)
        for side in range(2):
            for pair in range(6):
                lanes = pl.ds(pair * LANES, LANES)
                mid, mix = fetch(16 * k, 16, first_pair[side] + pair)
                for core in range(2):
                    factor = f_gy[side][core]
                    give_gy[k, side, core, :, lanes] = (mid * factor[0] + mix * factor[1]).astype(BF16)

        def send(side):
            for core in range(2):
                send_sides[k][side][core].start()

        both_sides(send)

    def own_block(k):
        for pair in range(32):
            lanes = pl.ds(pair * LANES, LANES)
            mid, mix = fetch(16 * k, 16, pair)
            out[0, 16 * k : 16 * k + 16, lanes] = mid
            give_own[16 * k : 16 * k + 16, lanes] = (mix * f_sib[1]).astype(BF16)
        share_own[k].start()

    def finish_own(k):
        share_own[k].wait_recv()
        rows = slice(16 * k, 16 * k + 16)
        out[0, rows] = (out[0, rows] + take_own[rows].astype(F32)) * (est[rows] * scale)

    for k in range(4):
        own_rows(k)
    for k in range(4):
        own_block(k)
        if k:
            finish_own(k - 1)
    finish_own(3)

    final_gx.wait_recv()
    for q in range(4):
        rows = get_gx[...].astype(F32)[HALO * q : HALO * q + HALO]
        gap = jnp.zeros((16 - HALO, QUARTER), F32)
        lanes = pl.ds(q * QUARTER, QUARTER)
        low_rows = jnp.concatenate([rows, gap], axis=0) * (row * scale)
        high_rows = jnp.concatenate([gap, rows], axis=0) * ((1.0 - row) * scale)
        out[0, 0:16, lanes] = out[0, 0:16, lanes] + low_rows * est[0:16, lanes]
        out[0, 48:64, lanes] = out[0, 48:64, lanes] + high_rows * est[48:64, lanes]
    for k in range(4):
        for side in range(2):

            @pl.when(exists[side])
            def _(k=k, side=side):
                for core in range(2):
                    arrived(17 + 4 * k + 2 * (1 - side) + core, take_gy.at[k, side, core])
                rows = slice(16 * k, 16 * k + 16)
                total = take_gy[k, side, 0].astype(F32) + take_gy[k, side, 1].astype(F32)
                out[0, rows, toward[side]] = out[0, rows, toward[side]] + total * (
                    est[rows, toward[side]] * scale
                )

    for item in [send_sib, send_gx, pass_gx, share_gx, final_gx] + share_own:
        item.wait_send()

    def drain(side):
        items = [*pass_co[side], *send_co[side]]
        for k in range(4):
            items += [send_gy[k][side], pass_gy[k][side], *send_sides[k][side]]
        for item in items:
            item.wait_send()

    both_sides(drain)


def solution(mesh):
    n_gy = mesh.shape["gy"]

    def body(estimate, views_data, point_spread, block_owner):
        slab, ends = (48, QUARTER), (2, 2, 16, WIDTH)
        sides = (4, 2, 2, 16, WIDTH)
        scratch = [
            ((64, 4096), F32),
            ((VIEWS, 64, 4096), BF16),
            ((64, 4096), BF16),
            ((64, 4096), BF16),
            (slab, BF16),
            ((2, *slab), BF16),
            ((2, 2, 64, WIDTH), BF16),
            (ends, BF16),
            ((SPAN_A * STEP_F, LANES), F32),
            ((SPAN_A * STEP_F, LANES), F32),
            ((512, CHUNK * LANES), BF16),
            ((VIEWS * 32 * STEP_T, LANES), F32),
            ((SPAN_A * STEP_V, LANES), F32),
            ((512, 96), BF16),
            ((96, 512), BF16),
            ((8, 256, 128), BF16),
            ((8, 128, 256), BF16),
            ((VIEWS, 64, 2 * SPAN_A), BF16),
            ((VIEWS, RANK * 64, 64), BF16),
            ((VIEWS, RANK * 16, 64), BF16),
            (slab, F32),
            (slab, F32),
            ((64, 4096), BF16),
            (slab, BF16),
            (sides, BF16),
            (ends, BF16),
            ((64, 4096), BF16),
            (slab, BF16),
            (sides, BF16),
            (ends, BF16),
            (slab, BF16),
            (slab, BF16),
        ]
        far_spec = pl.BlockSpec(memory_space=pltpu.HBM)
        smem = pl.BlockSpec(memory_space=pltpu.SMEM)
        return pl.pallas_call(
            functools.partial(kernel, n_gy),
            out_shape=jax.ShapeDtypeStruct((1, 64, 4096), F32),
            in_specs=[far_spec, far_spec, smem, smem],
            out_specs=pl.BlockSpec(memory_space=pltpu.VMEM),
            scratch_shapes=[pltpu.VMEM(shape, kind) for shape, kind in scratch]
            + [
                pltpu.SemaphoreType.DMA((4,)),
                pltpu.SemaphoreType.DMA((53,)),
                pltpu.SemaphoreType.DMA((53,)),
            ],
            compiler_params=pltpu.CompilerParams(
                collective_id=0, has_side_effects=True, vmem_limit_bytes=52 * 2**20
            ),
        )(
            estimate,
            views_data,
            point_spread.transpose(0, 2, 1, 3),
            block_owner.transpose(0, 2, 1),
        )

    placed = (P(("gx", "gy", "gz"), None, None), P(None, ("gx", "gy", "gz"), None, None), P(), P())
    return jax.shard_map(
        body,
        mesh=mesh,
        in_specs=placed,
        out_specs=P(("gx", "gy", "gz"), None, None),
        check_vma=False,
    )
```

```python
import functools

import jax
import jax.numpy as jnp
from jax import lax
from jax.experimental import pallas as pl
from jax.experimental.pallas import tpu as pltpu
from jax.sharding import PartitionSpec as P

MESH = pl.DeviceIdType.MESH
F32, BF16, I32 = jnp.float32, jnp.bfloat16, jnp.int32
BLOCK, TAPS, HALO, RANK, VIEWS, PILLAR = 64, 23, 11, 2, 4, 4
FLOOR = 0.5
SPAN_A = 80
PAIRS = 48
STEP_F, STEP_T, STEP_V = 56, 168, 520
LANES = 128
WIDTH = 768
FACE = 3328
QUARTER = 1024
CHUNK = 16
DUO = 16


def iota(shape, dim):
    return lax.broadcasted_iota(I32, shape, dim)


def band(distance, tap):
    total = jnp.zeros(distance.shape, F32)
    for t in range(TAPS):
        total = jnp.where(distance == t, tap(t), total)
    return total


def ext_c(lane):
    return jnp.where(lane < 96, lane, lane - LANES)


def parity_b(row):
    return jnp.where(row < 32, 2 * row, 2 * row - 63)


def ext_b(row):
    odd = (row >= PAIRS).astype(I32)
    pair = row - PAIRS * odd
    value = 2 * pair + odd - 88 * (pair >= 38).astype(I32)
    return jnp.where(pair >= 44, 1000, value)


def tap_of(ps):
    def tap(number, axis):
        return lambda t: ps[number // RANK, axis, number % RANK, t]

    return tap


def build_forward(ps, wb, wc):
    tap = tap_of(ps)
    d_b = ext_b(iota((64, 96), 1)) - parity_b(iota((64, 96), 0)) + HALO
    lane = iota((LANES, LANES), 1)
    d_c = ext_c(iota((LANES, LANES), 0)) - jnp.where(lane >= 64, lane - 64, lane) + HALO

    @pl.loop(0, VIEWS * RANK)
    def _(number):
        start = pl.multiple_of(number * 64, 64)
        wb[pl.ds(start, 64), :] = band(d_b, tap(number, 1)).astype(BF16)
        base = band(d_c, tap(number, 2))
        wc[number, 0:128, :] = jnp.where(lane < 64, base, 0.0).astype(BF16)
        wc[number, 128:256, :] = jnp.where(lane >= 64, base, 0.0).astype(BF16)


def build_rest(ps, mesh_row, wbt, wct, wa, wat_own, wat_far):
    tap = tap_of(ps)
    d_ct = ext_c(iota((64, LANES), 1)) - iota((64, LANES), 0) + HALO
    wct[...] = jnp.zeros_like(wct)

    @pl.loop(0, VIEWS * RANK)
    def _(number):
        base = band(d_ct, tap(number, 2)).astype(BF16)
        wct[number, 0:64, 0:128] = base
        wct[number, 64:128, 128:256] = base

    col = iota((96, LANES), 1)
    high = col >= 64
    d_bt = ext_b(iota((96, LANES), 0)) - parity_b(jnp.where(high, col - 64, col)) + HALO
    for pair in range(VIEWS * RANK // 2):
        low_tap, high_tap = tap(2 * pair, 1), tap(2 * pair + 1, 1)
        wbt[:, pair * LANES : (pair + 1) * LANES] = band(
            d_bt, lambda t: jnp.where(high, high_tap(t), low_tap(t))
        ).astype(BF16)

    def ext_a(place):
        inside = place - (64 + HALO) * (place >= 64).astype(I32) * mesh_row
        return jnp.where(place >= 64 + HALO, 1000, inside)

    second = iota((64, 2 * SPAN_A), 1) >= SPAN_A
    place = iota((64, 2 * SPAN_A), 1) - SPAN_A * second.astype(I32)
    d_a = ext_a(place) - iota((64, 2 * SPAN_A), 0) + HALO
    d_at = ext_a(iota((SPAN_A, 64), 0)) - iota((SPAN_A, 64), 1) + HALO

    @pl.loop(0, VIEWS)
    def _(view):
        first_tap, second_tap = tap(2 * view, 0), tap(2 * view + 1, 0)
        wa[view] = band(d_a, lambda t: jnp.where(second, second_tap(t), first_tap(t))).astype(BF16)
        for term, taps in enumerate((first_tap, second_tap)):
            base = band(d_at, taps).astype(BF16)
            wat_own[view, term * 64 : term * 64 + 64, :] = base[:64]
            wat_far[view, term * 16 : term * 16 + 16, :] = base[64:]


def kernel(
    n_gy,
    est_hbm,
    data_hbm,
    ps_hbm,
    owner_hbm,
    out,
    est,
    data,
    own,
    sib,
    slab,
    gx_in,
    gy_in,
    co_in,
    mid_f,
    mix_f,
    rows_t,
    t2,
    v2,
    wb,
    wbt,
    wc,
    wct,
    wa,
    wat_own,
    wat_far,
    keep_gx,
    part_gx,
    keep_co,
    give_own,
    give_gx,
    give_gy,
    give_co,
    take_own,
    take_gx,
    take_gy,
    take_co,
    put_gx,
    put_co,
    get_gx,
    get_co,
    ps,
    owner,
    load_sem,
    send_sem,
    recv_sem,
):
    i, j, g = lax.axis_index("gx"), lax.axis_index("gy"), lax.axis_index("gz")
    sibling = (i, j, 1 - g)
    across = (1 - i, j, g)
    beside = [[(i, j + 2 * s - 1, g), (i, j + 2 * s - 1, 1 - g)] for s in range(2)]
    corner = [(1 - i, j + 2 * s - 1, g) for s in range(2)]
    exists = (j > 0, j < n_gy - 1)

    toward = (pl.ds(0, WIDTH), pl.ds(FACE, WIDTH))
    parts = (*toward, pl.ds(WIDTH, FACE - WIDTH))
    load_est = [
        pltpu.make_async_copy(est_hbm.at[0, :, p], est.at[:, p], load_sem.at[n])
        for n, p in enumerate(parts)
    ]
    load_data = pltpu.make_async_copy(data_hbm.at[:, 0], data, load_sem.at[3])
    load_owner = pltpu.make_async_copy(owner_hbm, owner, load_sem.at[4])
    load_ps = pltpu.make_async_copy(ps_hbm, ps, load_sem.at[5])
    for item in [*load_est, load_owner, load_ps, load_data]:
        item.start()

    def copy(number, src, dst, target):
        return pltpu.make_async_remote_copy(
            src_ref=src,
            dst_ref=dst,
            send_sem=send_sem.at[number],
            recv_sem=recv_sem.at[number],
            device_id=target,
            device_id_type=MESH,
        )

    def both_sides(action):
        for side in range(2):

            @pl.when(exists[side])
            def _(side=side):
                action(side)

    barrier = pltpu.get_barrier_semaphore()
    for target in (sibling, across):
        pl.semaphore_signal(barrier, inc=1, device_id=target, device_id_type=MESH)

    def greet(side):
        for target in (*beside[side], corner[side]):
            pl.semaphore_signal(barrier, inc=1, device_id=target, device_id_type=MESH)

    both_sides(greet)
    for item, lanes in zip(load_est[:2], toward):
        item.wait()
        own[:, lanes] = est[:, lanes].astype(BF16)
    waits = 2 + 3 * exists[0].astype(I32) + 3 * exists[1].astype(I32)
    pl.semaphore_wait(barrier, waits)

    inside = ((pl.ds(0, 16), pl.ds(0, WIDTH)), (pl.ds(32, 16), pl.ds(256, WIDTH)))
    send_sib = copy(0, own, sib, sibling)
    send_gx = copy(1, slab, gx_in.at[0], across)
    rows_of = [pl.ds(16 * k, 16) for k in range(4)]
    send_gy = [
        [
            copy(37 + 2 * k + s, own.at[rows_of[k], toward[s]], gy_in.at[1 - s, 0, rows_of[k]], beside[s][0])
            for s in range(2)
        ]
        for k in range(4)
    ]
    pass_gx = copy(4, gx_in.at[0], gx_in.at[1], sibling)
    pass_gy = [
        [
            copy(45 + 2 * k + s, gy_in.at[s, 0, rows_of[k]], gy_in.at[s, 1, rows_of[k]], sibling)
            for s in range(2)
        ]
        for k in range(4)
    ]
    send_co = [copy(7 + s, slab.at[*inside[s]], co_in.at[1 - s, 0], corner[s]) for s in range(2)]
    pass_co = [copy(9 + s, co_in.at[s, 0], co_in.at[s, 1], sibling) for s in range(2)]

    def arrived(number, dst):
        copy(number, dst, dst, sibling).wait_recv()


    def send_rows(side):
        for k in range(4):
            send_gy[k][side].start()

    both_sides(send_rows)
    load_est[2].wait()
    own[:, parts[2]] = est[:, parts[2]].astype(BF16)
    send_sib.start()

    row = i.astype(F32)
    edge = est[53:64, :] * (1.0 - row) + est[0:HALO, :] * row
    slab[...] = jnp.concatenate(
        [edge[:, q * QUARTER : (q + 1) * QUARTER] for q in range(4)] + [jnp.zeros((4, QUARTER), F32)],
        axis=0,
    ).astype(BF16)

    for side in range(2):

        @pl.when(jnp.logical_not(exists[side]))
        def _(side=side):
            gy_in[side] = jnp.zeros(gy_in.shape[1:], BF16)
            co_in[side] = jnp.zeros(co_in.shape[1:], BF16)

    load_owner.wait()
    load_ps.wait()

    def column(row, col):
        col = jnp.minimum(jnp.maximum(col, 0), n_gy - 1)
        codes = [owner[row, k, col] for k in range(PILLAR)]
        found = []
        for code in (g, 1 - g):
            hits = [(codes[k] == code).astype(I32) for k in range(PILLAR)]
            found.append((sum(hits), sum(k * hits[k] for k in range(PILLAR))))
        return found

    home = column(i, j)
    valid, height = home[0]

    def factors(entry, there=None):
        present, level = entry
        live = present * valid
        if there is not None:
            live = live * there.astype(I32)
        at = [(live * (level - height == d).astype(I32)).astype(F32) for d in (0, 1, -1)]
        lane_low = (iota((1, LANES), 1) & 63) < 32
        return at[0], jnp.where(lane_low, at[1], at[2])

    f_sib = factors(home[1])
    f_gx = [factors(e) for e in column(1 - i, j)]
    f_gy = [[factors(e, exists[s]) for e in column(i, j + 2 * s - 1)] for s in range(2)]
    f_co = [[factors(e, exists[s]) for e in column(1 - i, j + 2 * s - 1)] for s in range(2)]
    live = valid.astype(F32)

    build_forward(ps, wb, wc)
    send_gx.start()
    both_sides(lambda s: send_co[s].start())
    build_rest(ps, i, wbt, wct, wa, wat_own, wat_far)

    def place(first_row, count, pair, mid, mix):
        mid_f[pl.ds(first_row * STEP_F + pair, count, stride=STEP_F), :] = mid
        mix_f[pl.ds(first_row * STEP_F + pair, count, stride=STEP_F), :] = mix

    def tile(number):
        return pl.ds(pl.multiple_of(number * LANES, LANES), LANES)

    def blend(pieces, factor):
        first, second = pieces[0].astype(F32), pieces[1].astype(F32)
        return (
            first * factor[0][0] + second * factor[1][0],
            first * factor[0][1] + second * factor[1][1],
        )

    for pair in range(44, PAIRS):
        place(0, SPAN_A, pair, jnp.zeros((SPAN_A, LANES), F32), jnp.zeros((SPAN_A, LANES), F32))

    first_pair = (38, 32)

    send_sib.wait_recv()

    @pl.loop(0, 32)
    def _(pair):
        place(0, 64, pair, own[:, tile(pair)].astype(F32), sib[:, tile(pair)].astype(F32) * f_sib[1])

    def hand_on(k):
        for side in range(2):

            @pl.when(exists[side])
            def _(side=side):
                arrived(37 + 2 * k + 1 - side, gy_in.at[side, 0, rows_of[k]])
                pass_gy[k][side].start()

    def select_rows(k):
        both_sides(lambda s: pass_gy[k][s].wait_recv())
        for side in range(2):
            for pair in range(6):
                lanes = pl.ds(pair * LANES, LANES)
                mid, mix = blend([gy_in[side, c, rows_of[k], lanes] for c in range(2)], f_gy[side])
                place(16 * k, 16, first_pair[side] + pair, mid, mix)

    low = iota((PAIRS, LANES), 1) < 64

    def forward_chunk(chunk):
        for two in range(CHUNK // 2):
            parts = []
            for one in range(2):
                start = pl.multiple_of((chunk * CHUNK + two * 2 + one) * STEP_F, 8)
                mid, mix = mid_f[pl.ds(start, PAIRS), :], mix_f[pl.ds(start, PAIRS), :]
                even = jnp.where(low, mid, pltpu.roll(mix, 64, 1))
                odd = jnp.where(low, pltpu.roll(mid, 64, 1), mix)
                parts.append(jnp.concatenate([even, odd], axis=0).astype(BF16))
            first = jnp.dot(wb[...], jnp.concatenate(parts, axis=1), preferred_element_type=F32)
            rows_t[:, two * 256 : two * 256 + 256] = first.astype(BF16)
        for number in range(VIEWS * RANK):
            view, term = number // RANK, number % RANK
            top = number * 64
            block = jnp.concatenate(
                [
                    jnp.concatenate(
                        [
                            rows_t[top : top + 32, a * LANES : (a + 1) * LANES],
                            rows_t[top + 32 : top + 64, a * LANES : (a + 1) * LANES],
                        ],
                        axis=1,
                    )
                    for a in range(CHUNK)
                ],
                axis=0,
            )
            second = jnp.dot(block, wc[number], preferred_element_type=F32)
            for a in range(CHUNK):
                start = view * 32 * STEP_T + term * SPAN_A + chunk * CHUNK + a
                t2[pl.ds(start, 32, stride=STEP_T), :] = second[a * 32 : a * 32 + 32, :]

    hand_on(0)
    for k in range(3):
        hand_on(k + 1)
        select_rows(k)
        forward_chunk(k)

    arrived(1, gx_in.at[0])
    pass_gx.start()

    for side in range(2):

        @pl.when(exists[side])
        def _(side=side):
            arrived(7 + 1 - side, co_in.at[side, 0])
            pass_co[side].start()

    select_rows(3)
    forward_chunk(3)

    pass_gx.wait_recv()
    both_sides(lambda s: pass_co[s].wait_recv())

    def lengthen(rows):
        return jnp.concatenate([rows, jnp.zeros((16 - HALO, rows.shape[1]), F32)], axis=0)

    for q in range(4):
        rows = [gx_in[k].astype(F32)[HALO * q : HALO * q + HALO] for k in range(2)]
        for number in range(8):
            lanes = slice(number * LANES, (number + 1) * LANES)
            mid, mix = blend([lengthen(rows[k][:, lanes]) for k in range(2)], f_gx)
            place(64, 16, q * 8 + number, mid, mix)

    for side in range(2):
        down = 1 - side
        for pair in range(6):
            lanes = slice(pair * LANES, (pair + 1) * LANES)
            rows = [co_in[side, k, :, lanes].astype(F32)[down : down + HALO] for k in range(2)]
            mid, mix = blend([lengthen(r) for r in rows], f_co[side])
            place(64, 16, first_pair[side] + pair, mid, mix)

    forward_chunk(64 // CHUNK)
    load_data.wait()

    def adjoint_front(view, back, count, first):
        for term in range(RANK):
            rows = back[term * count : (term + 1) * count]
            block = jnp.concatenate([rows[:, k * LANES : (k + 1) * LANES] for k in range(32)], axis=0)
            wide = jnp.dot(block, wct[view * RANK + term], preferred_element_type=F32)
            for k in range(32):
                for odd in range(2):
                    at = first * STEP_V + (view * RANK + term) * 64 + odd * 32 + k
                    v2[pl.ds(at, count, stride=STEP_V), :] = wide[
                        k * count : (k + 1) * count, odd * LANES : (odd + 1) * LANES
                    ]

    def turn_far(view):
        start = pl.multiple_of(view * 32 * STEP_T, 8)
        fields = jnp.concatenate(
            [t2[pl.ds(start + k * STEP_T, 2 * SPAN_A), :].astype(BF16) for k in range(32)], axis=1
        )
        blurred = jnp.dot(wa[view], fields, preferred_element_type=F32)
        ratio = (data[view].astype(F32) / jnp.maximum(blurred, FLOOR) * live).astype(BF16)
        data[view] = ratio
        back = jnp.dot(wat_far[view], ratio, preferred_element_type=F32).astype(BF16)
        adjoint_front(view, back, 16, 64)

    def turn_own(view):
        back = jnp.dot(wat_own[view], data[view], preferred_element_type=F32).astype(BF16)
        adjoint_front(view, back, 64, 0)

    pl.loop(0, VIEWS)(turn_far)

    def adjoint_rows(step):
        start = pl.multiple_of(step * DUO * STEP_V, 8)
        fields = jnp.concatenate(
            [v2[pl.ds(start + k * STEP_V, 512), :].astype(BF16) for k in range(DUO)], axis=1
        )
        spread = jnp.dot(wbt[...], fields, preferred_element_type=F32)
        for k in range(DUO):
            even = spread[0:PAIRS, k * LANES : (k + 1) * LANES]
            odd = spread[PAIRS : 2 * PAIRS, k * LANES : (k + 1) * LANES]
            at = pl.multiple_of((step * DUO + k) * STEP_F, 8)
            mid_f[pl.ds(at, PAIRS), :] = jnp.where(low, even, pltpu.roll(odd, 64, 1))
            mix_f[pl.ds(at, PAIRS), :] = jnp.where(low, pltpu.roll(even, 64, 1), odd)

    def fetch(first_row, count, pair):
        at = pl.ds(first_row * STEP_F + pair, count, stride=STEP_F)
        return mid_f[at, :], mix_f[at, :]

    adjoint_rows(64 // DUO)
    for q in range(4):
        for number in range(8):
            lanes = slice(number * LANES, (number + 1) * LANES)
            mid, mix = fetch(64, 16, q * 8 + number)
            mid, mix = mid[:HALO], mix[:HALO]
            keep_gx[HALO * q : HALO * q + HALO, lanes] = mid * f_gx[0][0] + mix * f_gx[0][1]
            part_gx[HALO * q : HALO * q + HALO, lanes] = mid * f_gx[1][0] + mix * f_gx[1][1]
    keep_gx[44:48, :] = jnp.zeros((4, QUARTER), F32)
    part_gx[44:48, :] = jnp.zeros((4, QUARTER), F32)
    give_gx[...] = part_gx[...].astype(BF16)
    share_gx = copy(11, give_gx, take_gx, sibling)
    share_gx.start()

    for side in range(2):
        for pair in range(6):
            lanes = slice(pair * LANES, (pair + 1) * LANES)
            mid, mix = fetch(64, 16, first_pair[side] + pair)
            one, two = f_co[side]
            keep_co[side, :, lanes] = mid * one[0] + mix * one[1]
            give_co[side, :, lanes] = (mid * two[0] + mix * two[1]).astype(BF16)
    share_co = copy(12, give_co, take_co, sibling)
    share_co.start()
    final_gx = copy(16, put_gx, get_gx, across)
    final_co = [copy(13 + s, put_co.at[s], get_co.at[1 - s], corner[s]) for s in range(2)]

    def finish_gx():
        share_gx.wait_recv()
        put_gx[...] = (keep_gx[...] + take_gx[...].astype(F32)).astype(BF16)
        final_gx.start()
        share_co.wait_recv()
        put_co[...] = (keep_co[...] + take_co[...].astype(F32)).astype(BF16)
        both_sides(lambda s: final_co[s].start())

    turn_own(0)
    finish_gx()
    pl.loop(1, VIEWS)(turn_own)

    scale = live / VIEWS
    send_sides = [
        [
            [
                copy(17 + 4 * k + 2 * s + c, give_gy.at[k, s, c], take_gy.at[k, 1 - s, c], beside[s][c])
                for c in range(2)
            ]
            for s in range(2)
        ]
        for k in range(4)
    ]
    share_own = [
        copy(33 + k, give_own.at[pl.ds(16 * k, 16)], take_own.at[pl.ds(16 * k, 16)], sibling)
        for k in range(4)
    ]

    def own_rows(k):
        adjoint_rows(k)
        for side in range(2):
            for pair in range(6):
                lanes = pl.ds(pair * LANES, LANES)
                mid, mix = fetch(16 * k, 16, first_pair[side] + pair)
                for core in range(2):
                    factor = f_gy[side][core]
                    give_gy[k, side, core, :, lanes] = (mid * factor[0] + mix * factor[1]).astype(BF16)

        def send(side):
            for core in range(2):
                send_sides[k][side][core].start()

        both_sides(send)

    def own_block(k):
        for pair in range(32):
            lanes = pl.ds(pair * LANES, LANES)
            mid, mix = fetch(16 * k, 16, pair)
            out[0, 16 * k : 16 * k + 16, lanes] = mid
            give_own[16 * k : 16 * k + 16, lanes] = (mix * f_sib[1]).astype(BF16)
        share_own[k].start()

    def finish_own(k):
        share_own[k].wait_recv()
        rows = slice(16 * k, 16 * k + 16)
        out[0, rows] = (out[0, rows] + take_own[rows].astype(F32)) * (est[rows] * scale)

    for k in range(4):
        own_rows(k)
    for k in range(4):
        own_block(k)
        if k:
            finish_own(k - 1)
    finish_own(3)

    def add_rows(rows, lanes):
        gap = jnp.zeros((16 - HALO, rows.shape[1]), F32)
        low_rows = jnp.concatenate([rows, gap], axis=0) * (row * scale)
        high_rows = jnp.concatenate([gap, rows], axis=0) * ((1.0 - row) * scale)
        out[0, 0:16, lanes] = out[0, 0:16, lanes] + low_rows * est[0:16, lanes]
        out[0, 48:64, lanes] = out[0, 48:64, lanes] + high_rows * est[48:64, lanes]

    final_gx.wait_recv()
    for q in range(4):
        add_rows(get_gx[...].astype(F32)[HALO * q : HALO * q + HALO], pl.ds(q * QUARTER, QUARTER))
    for side in range(2):

        @pl.when(exists[side])
        def _(side=side):
            arrived(13 + 1 - side, get_co.at[side])
            add_rows(get_co[side].astype(F32)[:HALO], toward[side])

    for k in range(4):
        for side in range(2):

            @pl.when(exists[side])
            def _(k=k, side=side):
                for core in range(2):
                    arrived(17 + 4 * k + 2 * (1 - side) + core, take_gy.at[k, side, core])
                rows = slice(16 * k, 16 * k + 16)
                total = take_gy[k, side, 0].astype(F32) + take_gy[k, side, 1].astype(F32)
                out[0, rows, toward[side]] = out[0, rows, toward[side]] + total * (
                    est[rows, toward[side]] * scale
                )

    for item in [send_sib, send_gx, pass_gx, share_gx, share_co, final_gx] + share_own:
        item.wait_send()

    def drain(side):
        items = [send_co[side], pass_co[side], final_co[side]]
        for k in range(4):
            items += [send_gy[k][side], pass_gy[k][side], *send_sides[k][side]]
        for item in items:
            item.wait_send()

    both_sides(drain)


def solution(mesh):
    n_gy = mesh.shape["gy"]

    def body(estimate, views_data, point_spread, block_owner):
        slab, ends = (48, QUARTER), (2, 16, WIDTH)
        sides = (4, 2, 2, 16, WIDTH)
        scratch = [
            ((64, 4096), F32),
            ((VIEWS, 64, 4096), BF16),
            ((64, 4096), BF16),
            ((64, 4096), BF16),
            (slab, BF16),
            ((2, *slab), BF16),
            ((2, 2, 64, WIDTH), BF16),
            ((2, *ends), BF16),
            ((SPAN_A * STEP_F, LANES), F32),
            ((SPAN_A * STEP_F, LANES), F32),
            ((512, CHUNK * LANES), BF16),
            ((VIEWS * 32 * STEP_T, LANES), F32),
            ((SPAN_A * STEP_V, LANES), F32),
            ((512, 96), BF16),
            ((96, 512), BF16),
            ((8, 256, 128), BF16),
            ((8, 128, 256), BF16),
            ((VIEWS, 64, 2 * SPAN_A), BF16),
            ((VIEWS, RANK * 64, 64), BF16),
            ((VIEWS, RANK * 16, 64), BF16),
            (slab, F32),
            (slab, F32),
            (ends, F32),
            ((64, 4096), BF16),
            (slab, BF16),
            (sides, BF16),
            (ends, BF16),
            ((64, 4096), BF16),
            (slab, BF16),
            (sides, BF16),
            (ends, BF16),
            (slab, BF16),
            (ends, BF16),
            (slab, BF16),
            (ends, BF16),
        ]
        far_spec = pl.BlockSpec(memory_space=pltpu.HBM)
        return pl.pallas_call(
            functools.partial(kernel, n_gy),
            out_shape=jax.ShapeDtypeStruct((1, 64, 4096), F32),
            in_specs=[far_spec] * 4,
            out_specs=pl.BlockSpec(memory_space=pltpu.VMEM),
            scratch_shapes=[pltpu.VMEM(shape, kind) for shape, kind in scratch]
            + [
                pltpu.SMEM((VIEWS, 3, RANK, TAPS), F32),
                pltpu.SMEM((2, PILLAR, n_gy), I32),
                pltpu.SemaphoreType.DMA((6,)),
                pltpu.SemaphoreType.DMA((53,)),
                pltpu.SemaphoreType.DMA((53,)),
            ],
            compiler_params=pltpu.CompilerParams(
                collective_id=0, has_side_effects=True, vmem_limit_bytes=52 * 2**20
            ),
        )(
            estimate,
            views_data,
            point_spread.transpose(0, 2, 1, 3),
            block_owner.transpose(0, 2, 1),
        )

    placed = (P(("gx", "gy", "gz"), None, None), P(None, ("gx", "gy", "gz"), None, None), P(), P())
    return jax.shard_map(
        body,
        mesh=mesh,
        in_specs=placed,
        out_specs=P(("gx", "gy", "gz"), None, None),
        check_vma=False,
    )
```

```python
import functools

import jax
import jax.numpy as jnp
from jax import lax
from jax.experimental import pallas as pl
from jax.experimental.pallas import tpu as pltpu
from jax.sharding import PartitionSpec as P

MESH = pl.DeviceIdType.MESH
F32, BF16, I32 = jnp.float32, jnp.bfloat16, jnp.int32
BLOCK, TAPS, HALO, RANK, VIEWS, PILLAR = 64, 23, 11, 2, 4, 4
FLOOR = 0.5
SPAN_A = 80
PAIRS = 48
STEP_F, STEP_T, STEP_V = 56, 168, 520
LANES = 128
WIDTH = 768
FACE = 3328
QUARTER = 1024
CHUNK = 16
DUO = 16


def iota(shape, dim):
    return lax.broadcasted_iota(I32, shape, dim)


def band(distance, tap):
    total = jnp.zeros(distance.shape, F32)
    for t in range(TAPS):
        total = jnp.where(distance == t, tap(t), total)
    return total


def ext_c(lane):
    return jnp.where(lane < 96, lane, lane - LANES)


def parity_b(row):
    return jnp.where(row < 32, 2 * row, 2 * row - 63)


def ext_b(row):
    odd = (row >= PAIRS).astype(I32)
    pair = row - PAIRS * odd
    value = 2 * pair + odd - 88 * (pair >= 38).astype(I32)
    return jnp.where(pair >= 44, 1000, value)


def tap_of(ps):
    def tap(number, axis):
        return lambda t: ps[number // RANK, axis, number % RANK, t]

    return tap


def build_forward(ps, wb, wc):
    tap = tap_of(ps)
    d_b = ext_b(iota((64, 96), 1)) - parity_b(iota((64, 96), 0)) + HALO
    lane = iota((LANES, LANES), 1)
    d_c = ext_c(iota((LANES, LANES), 0)) - jnp.where(lane >= 64, lane - 64, lane) + HALO

    @pl.loop(0, VIEWS * RANK)
    def _(number):
        start = pl.multiple_of(number * 64, 64)
        wb[pl.ds(start, 64), :] = band(d_b, tap(number, 1)).astype(BF16)
        base = band(d_c, tap(number, 2))
        wc[number, 0:128, :] = jnp.where(lane < 64, base, 0.0).astype(BF16)
        wc[number, 128:256, :] = jnp.where(lane >= 64, base, 0.0).astype(BF16)


def build_rest(ps, mesh_row, wbt, wown, wside, wct, wa, wat_own, wat_far):
    tap = tap_of(ps)
    d_ct = ext_c(iota((64, LANES), 1)) - iota((64, LANES), 0) + HALO
    wct[...] = jnp.zeros_like(wct)

    @pl.loop(0, VIEWS * RANK)
    def _(number):
        base = band(d_ct, tap(number, 2)).astype(BF16)
        wct[number, 0:64, 0:128] = base
        wct[number, 64:128, 128:256] = base

    col = iota((96, LANES), 1)
    high = col >= 64
    d_bt = ext_b(iota((96, LANES), 0)) - parity_b(jnp.where(high, col - 64, col)) + HALO
    for pair in range(VIEWS * RANK // 2):
        low_tap, high_tap = tap(2 * pair, 1), tap(2 * pair + 1, 1)
        wbt[:, pair * LANES : (pair + 1) * LANES] = band(
            d_bt, lambda t: jnp.where(high, high_tap(t), low_tap(t))
        ).astype(BF16)

    wown[0:32, :] = wbt[0:32, :]
    wown[32:64, :] = wbt[PAIRS : PAIRS + 32, :]

    line, col = iota((32, LANES), 0), iota((32, LANES), 1)
    line = jnp.where(line >= 16, line + PAIRS + 16, line + 32)
    odd, entry = (col & 31) >> 4, col & 15
    d_side = ext_b(line) - (2 * jnp.where(entry >= 8, entry + 16, entry) + odd) + HALO
    group = col >> 5
    for half in range(2):
        taps = [tap(4 * half + n, 1) for n in range(4)]
        wside[:, half * LANES : (half + 1) * LANES] = band(
            d_side,
            lambda t: jnp.where(
                group < 2,
                jnp.where(group == 0, taps[0](t), taps[1](t)),
                jnp.where(group == 2, taps[2](t), taps[3](t)),
            ),
        ).astype(BF16)

    def ext_a(place):
        inside = place - (64 + HALO) * (place >= 64).astype(I32) * mesh_row
        return jnp.where(place >= 64 + HALO, 1000, inside)

    second = iota((64, 2 * SPAN_A), 1) >= SPAN_A
    place = iota((64, 2 * SPAN_A), 1) - SPAN_A * second.astype(I32)
    d_a = ext_a(place) - iota((64, 2 * SPAN_A), 0) + HALO
    d_at = ext_a(iota((SPAN_A, 64), 0)) - iota((SPAN_A, 64), 1) + HALO

    @pl.loop(0, VIEWS)
    def _(view):
        first_tap, second_tap = tap(2 * view, 0), tap(2 * view + 1, 0)
        wa[view] = band(d_a, lambda t: jnp.where(second, second_tap(t), first_tap(t))).astype(BF16)
        for term, taps in enumerate((first_tap, second_tap)):
            base = band(d_at, taps).astype(BF16)
            wat_own[view, term * 64 : term * 64 + 64, :] = base[:64]
            wat_far[view, term * 16 : term * 16 + 16, :] = base[64:]


def kernel(
    n_gy,
    est_hbm,
    data_hbm,
    ps_hbm,
    owner_hbm,
    out,
    est,
    data,
    own,
    sib,
    slab,
    gx_in,
    gy_in,
    co_in,
    mid_f,
    mix_f,
    rows_t,
    t2,
    v2,
    wb,
    wbt,
    wown,
    wside,
    wc,
    wct,
    wa,
    wat_own,
    wat_far,
    keep_gx,
    part_gx,
    keep_co,
    give_own,
    give_gx,
    give_gy,
    give_co,
    take_own,
    take_gx,
    take_gy,
    take_co,
    put_gx,
    put_co,
    get_gx,
    get_co,
    ps,
    owner,
    load_sem,
    send_sem,
    recv_sem,
):
    i, j, g = lax.axis_index("gx"), lax.axis_index("gy"), lax.axis_index("gz")
    sibling = (i, j, 1 - g)
    across = (1 - i, j, g)
    beside = [[(i, j + 2 * s - 1, g), (i, j + 2 * s - 1, 1 - g)] for s in range(2)]
    corner = [(1 - i, j + 2 * s - 1, g) for s in range(2)]
    exists = (j > 0, j < n_gy - 1)

    toward = (pl.ds(0, WIDTH), pl.ds(FACE, WIDTH))
    parts = (*toward, pl.ds(WIDTH, FACE - WIDTH))
    load_est = [
        pltpu.make_async_copy(est_hbm.at[0, :, p], est.at[:, p], load_sem.at[n])
        for n, p in enumerate(parts)
    ]
    load_data = pltpu.make_async_copy(data_hbm.at[:, 0], data, load_sem.at[3])
    load_owner = pltpu.make_async_copy(owner_hbm, owner, load_sem.at[4])
    load_ps = pltpu.make_async_copy(ps_hbm, ps, load_sem.at[5])
    for item in [*load_est, load_owner, load_ps, load_data]:
        item.start()

    def copy(number, src, dst, target):
        return pltpu.make_async_remote_copy(
            src_ref=src,
            dst_ref=dst,
            send_sem=send_sem.at[number],
            recv_sem=recv_sem.at[number],
            device_id=target,
            device_id_type=MESH,
        )

    def both_sides(action):
        for side in range(2):

            @pl.when(exists[side])
            def _(side=side):
                action(side)

    barrier = pltpu.get_barrier_semaphore()
    for target in (sibling, across):
        pl.semaphore_signal(barrier, inc=1, device_id=target, device_id_type=MESH)

    def greet(side):
        for target in (*beside[side], corner[side]):
            pl.semaphore_signal(barrier, inc=1, device_id=target, device_id_type=MESH)

    both_sides(greet)
    for item, lanes in zip(load_est[:2], toward):
        item.wait()
        own[:, lanes] = est[:, lanes].astype(BF16)
    waits = 2 + 3 * exists[0].astype(I32) + 3 * exists[1].astype(I32)
    pl.semaphore_wait(barrier, waits)

    inside = ((pl.ds(0, 16), pl.ds(0, WIDTH)), (pl.ds(32, 16), pl.ds(256, WIDTH)))
    send_sib = copy(0, own, sib, sibling)
    send_gx = copy(1, slab, gx_in.at[0], across)
    rows_of = [pl.ds(16 * k, 16) for k in range(4)]
    send_gy = [
        [
            copy(37 + 2 * k + s, own.at[rows_of[k], toward[s]], gy_in.at[1 - s, 0, rows_of[k]], beside[s][0])
            for s in range(2)
        ]
        for k in range(4)
    ]
    pass_gx = copy(4, gx_in.at[0], gx_in.at[1], sibling)
    pass_gy = [
        [
            copy(45 + 2 * k + s, gy_in.at[s, 0, rows_of[k]], gy_in.at[s, 1, rows_of[k]], sibling)
            for s in range(2)
        ]
        for k in range(4)
    ]
    send_co = [copy(7 + s, slab.at[*inside[s]], co_in.at[1 - s, 0], corner[s]) for s in range(2)]
    pass_co = [copy(9 + s, co_in.at[s, 0], co_in.at[s, 1], sibling) for s in range(2)]

    def arrived(number, dst):
        copy(number, dst, dst, sibling).wait_recv()


    def send_rows(side):
        for k in range(4):
            send_gy[k][side].start()

    both_sides(send_rows)
    load_est[2].wait()
    own[:, parts[2]] = est[:, parts[2]].astype(BF16)
    send_sib.start()

    row = i.astype(F32)
    edge = est[53:64, :] * (1.0 - row) + est[0:HALO, :] * row
    slab[...] = jnp.concatenate(
        [edge[:, q * QUARTER : (q + 1) * QUARTER] for q in range(4)] + [jnp.zeros((4, QUARTER), F32)],
        axis=0,
    ).astype(BF16)

    for side in range(2):

        @pl.when(jnp.logical_not(exists[side]))
        def _(side=side):
            gy_in[side] = jnp.zeros(gy_in.shape[1:], BF16)
            co_in[side] = jnp.zeros(co_in.shape[1:], BF16)

    load_owner.wait()
    load_ps.wait()

    def column(row, col):
        col = jnp.minimum(jnp.maximum(col, 0), n_gy - 1)
        codes = [owner[row, k, col] for k in range(PILLAR)]
        found = []
        for code in (g, 1 - g):
            hits = [(codes[k] == code).astype(I32) for k in range(PILLAR)]
            found.append((sum(hits), sum(k * hits[k] for k in range(PILLAR))))
        return found

    home = column(i, j)
    valid, height = home[0]

    def factors(entry, there=None):
        present, level = entry
        live = present * valid
        if there is not None:
            live = live * there.astype(I32)
        at = [(live * (level - height == d).astype(I32)).astype(F32) for d in (0, 1, -1)]
        lane_low = (iota((1, LANES), 1) & 63) < 32
        return at[0], jnp.where(lane_low, at[1], at[2])

    f_sib = factors(home[1])
    f_gx = [factors(e) for e in column(1 - i, j)]
    f_gy = [[factors(e, exists[s]) for e in column(i, j + 2 * s - 1)] for s in range(2)]
    f_co = [[factors(e, exists[s]) for e in column(1 - i, j + 2 * s - 1)] for s in range(2)]
    live = valid.astype(F32)

    build_forward(ps, wb, wc)
    send_gx.start()
    both_sides(lambda s: send_co[s].start())
    build_rest(ps, i, wbt, wown, wside, wct, wa, wat_own, wat_far)

    def place(first_row, count, pair, mid, mix):
        mid_f[pl.ds(first_row * STEP_F + pair, count, stride=STEP_F), :] = mid
        mix_f[pl.ds(first_row * STEP_F + pair, count, stride=STEP_F), :] = mix

    def tile(number):
        return pl.ds(pl.multiple_of(number * LANES, LANES), LANES)

    def blend(pieces, factor):
        first, second = pieces[0].astype(F32), pieces[1].astype(F32)
        return (
            first * factor[0][0] + second * factor[1][0],
            first * factor[0][1] + second * factor[1][1],
        )

    for pair in range(44, PAIRS):
        place(0, SPAN_A, pair, jnp.zeros((SPAN_A, LANES), F32), jnp.zeros((SPAN_A, LANES), F32))

    first_pair = (38, 32)

    send_sib.wait_recv()

    @pl.loop(0, 32)
    def _(pair):
        place(0, 64, pair, own[:, tile(pair)].astype(F32), sib[:, tile(pair)].astype(F32) * f_sib[1])

    def hand_on(k):
        for side in range(2):

            @pl.when(exists[side])
            def _(side=side):
                arrived(37 + 2 * k + 1 - side, gy_in.at[side, 0, rows_of[k]])
                pass_gy[k][side].start()

    def select_rows(k):
        both_sides(lambda s: pass_gy[k][s].wait_recv())
        for side in range(2):
            for pair in range(6):
                lanes = pl.ds(pair * LANES, LANES)
                mid, mix = blend([gy_in[side, c, rows_of[k], lanes] for c in range(2)], f_gy[side])
                place(16 * k, 16, first_pair[side] + pair, mid, mix)

    low = iota((PAIRS, LANES), 1) < 64

    def forward_chunk(chunk):
        for two in range(CHUNK // 2):
            parts = []
            for one in range(2):
                start = pl.multiple_of((chunk * CHUNK + two * 2 + one) * STEP_F, 8)
                mid, mix = mid_f[pl.ds(start, PAIRS), :], mix_f[pl.ds(start, PAIRS), :]
                even = jnp.where(low, mid, pltpu.roll(mix, 64, 1))
                odd = jnp.where(low, pltpu.roll(mid, 64, 1), mix)
                parts.append(jnp.concatenate([even, odd], axis=0).astype(BF16))
            first = jnp.dot(wb[...], jnp.concatenate(parts, axis=1), preferred_element_type=F32)
            rows_t[:, two * 256 : two * 256 + 256] = first.astype(BF16)
        for number in range(VIEWS * RANK):
            view, term = number // RANK, number % RANK
            top = number * 64
            block = jnp.concatenate(
                [
                    jnp.concatenate(
                        [
                            rows_t[top : top + 32, a * LANES : (a + 1) * LANES],
                            rows_t[top + 32 : top + 64, a * LANES : (a + 1) * LANES],
                        ],
                        axis=1,
                    )
                    for a in range(CHUNK)
                ],
                axis=0,
            )
            second = jnp.dot(block, wc[number], preferred_element_type=F32)
            for a in range(CHUNK):
                start = view * 32 * STEP_T + term * SPAN_A + chunk * CHUNK + a
                t2[pl.ds(start, 32, stride=STEP_T), :] = second[a * 32 : a * 32 + 32, :]

    hand_on(0)
    for k in range(3):
        hand_on(k + 1)
        select_rows(k)
        forward_chunk(k)

    arrived(1, gx_in.at[0])
    pass_gx.start()

    for side in range(2):

        @pl.when(exists[side])
        def _(side=side):
            arrived(7 + 1 - side, co_in.at[side, 0])
            pass_co[side].start()

    select_rows(3)
    forward_chunk(3)

    pass_gx.wait_recv()
    both_sides(lambda s: pass_co[s].wait_recv())

    def lengthen(rows):
        return jnp.concatenate([rows, jnp.zeros((16 - HALO, rows.shape[1]), F32)], axis=0)

    for q in range(4):
        rows = [gx_in[k].astype(F32)[HALO * q : HALO * q + HALO] for k in range(2)]
        for number in range(8):
            lanes = slice(number * LANES, (number + 1) * LANES)
            mid, mix = blend([lengthen(rows[k][:, lanes]) for k in range(2)], f_gx)
            place(64, 16, q * 8 + number, mid, mix)

    for side in range(2):
        down = 1 - side
        for pair in range(6):
            lanes = slice(pair * LANES, (pair + 1) * LANES)
            rows = [co_in[side, k, :, lanes].astype(F32)[down : down + HALO] for k in range(2)]
            mid, mix = blend([lengthen(r) for r in rows], f_co[side])
            place(64, 16, first_pair[side] + pair, mid, mix)

    forward_chunk(64 // CHUNK)
    load_data.wait()

    def adjoint_front(view, back, count, first, tiles):
        for term in range(RANK):
            rows = back[term * count : (term + 1) * count]
            block = jnp.concatenate(
                [rows[:, n * LANES : (n + 1) * LANES] for n in range(len(tiles))], axis=0
            )
            wide = jnp.dot(block, wct[view * RANK + term], preferred_element_type=F32)
            for n, k in enumerate(tiles):
                for odd in range(2):
                    at = first * STEP_V + (view * RANK + term) * 64 + odd * 32 + k
                    v2[pl.ds(at, count, stride=STEP_V), :] = wide[
                        n * count : (n + 1) * count, odd * LANES : (odd + 1) * LANES
                    ]

    def turn_far(view):
        start = pl.multiple_of(view * 32 * STEP_T, 8)
        fields = jnp.concatenate(
            [t2[pl.ds(start + k * STEP_T, 2 * SPAN_A), :].astype(BF16) for k in range(32)], axis=1
        )
        blurred = jnp.dot(wa[view], fields, preferred_element_type=F32)
        ratio = (data[view].astype(F32) / jnp.maximum(blurred, FLOOR) * live).astype(BF16)
        data[view] = ratio
        back = jnp.dot(wat_far[view], ratio, preferred_element_type=F32).astype(BF16)
        adjoint_front(view, back, 16, 64, range(32))

    def turn_near(view):
        ratio = jnp.concatenate([data[view, :, 0:1024], data[view, :, 3072:4096]], axis=1)
        back = jnp.dot(wat_own[view], ratio, preferred_element_type=F32).astype(BF16)
        adjoint_front(view, back, 64, 0, [*range(8), *range(24, 32)])

    def turn_inner(view):
        back = jnp.dot(wat_own[view], data[view, :, 1024:3072], preferred_element_type=F32)
        adjoint_front(view, back.astype(BF16), 64, 0, range(8, 24))

    pl.loop(0, VIEWS)(turn_far)

    def last_pass(step, weights, pieces, count, first):
        start = step * DUO * STEP_V
        columns = []
        for k in range(DUO):
            rows = [v2[pl.ds(start + k * STEP_V + at, size), :] for at, size in pieces]
            columns.append(jnp.concatenate(rows, axis=0).astype(BF16))
        spread = jnp.dot(
            weights[...], jnp.concatenate(columns, axis=1), preferred_element_type=F32
        )
        for k in range(DUO):
            even = spread[0:count, k * LANES : (k + 1) * LANES]
            odd = spread[count : 2 * count, k * LANES : (k + 1) * LANES]
            near = iota((count, LANES), 1) < 64
            at = (step * DUO + k) * STEP_F + first
            mid_f[pl.ds(at, count), :] = jnp.where(near, even, pltpu.roll(odd, 64, 1))
            mix_f[pl.ds(at, count), :] = jnp.where(near, pltpu.roll(even, 64, 1), odd)

    whole = [(0, 512)]
    sides_only = [(at + edge, 8) for at in range(0, 512, 32) for edge in (0, 24)]

    def fetch(first_row, count, pair):
        at = pl.ds(first_row * STEP_F + pair, count, stride=STEP_F)
        return mid_f[at, :], mix_f[at, :]

    last_pass(64 // DUO, wbt, whole, PAIRS, 0)
    for q in range(4):
        for number in range(8):
            lanes = slice(number * LANES, (number + 1) * LANES)
            mid, mix = fetch(64, 16, q * 8 + number)
            mid, mix = mid[:HALO], mix[:HALO]
            keep_gx[HALO * q : HALO * q + HALO, lanes] = mid * f_gx[0][0] + mix * f_gx[0][1]
            part_gx[HALO * q : HALO * q + HALO, lanes] = mid * f_gx[1][0] + mix * f_gx[1][1]
    keep_gx[44:48, :] = jnp.zeros((4, QUARTER), F32)
    part_gx[44:48, :] = jnp.zeros((4, QUARTER), F32)
    give_gx[...] = part_gx[...].astype(BF16)
    share_gx = copy(11, give_gx, take_gx, sibling)
    share_gx.start()

    for side in range(2):
        for pair in range(6):
            lanes = slice(pair * LANES, (pair + 1) * LANES)
            mid, mix = fetch(64, 16, first_pair[side] + pair)
            one, two = f_co[side]
            keep_co[side, :, lanes] = mid * one[0] + mix * one[1]
            give_co[side, :, lanes] = (mid * two[0] + mix * two[1]).astype(BF16)
    share_co = copy(12, give_co, take_co, sibling)
    share_co.start()
    final_gx = copy(16, put_gx, get_gx, across)
    final_co = [copy(13 + s, put_co.at[s], get_co.at[1 - s], corner[s]) for s in range(2)]

    def finish_gx():
        share_gx.wait_recv()
        put_gx[...] = (keep_gx[...] + take_gx[...].astype(F32)).astype(BF16)
        final_gx.start()
        share_co.wait_recv()
        put_co[...] = (keep_co[...] + take_co[...].astype(F32)).astype(BF16)
        both_sides(lambda s: final_co[s].start())

    pl.loop(0, 2)(turn_near)
    finish_gx()
    pl.loop(2, VIEWS)(turn_near)

    scale = live / VIEWS
    send_sides = [
        [
            [
                copy(17 + 4 * k + 2 * s + c, give_gy.at[k, s, c], take_gy.at[k, 1 - s, c], beside[s][c])
                for c in range(2)
            ]
            for s in range(2)
        ]
        for k in range(4)
    ]
    share_own = [
        copy(33 + k, give_own.at[pl.ds(16 * k, 16)], take_own.at[pl.ds(16 * k, 16)], sibling)
        for k in range(4)
    ]

    def own_rows(k):
        last_pass(k, wside, sides_only, 16, 32)
        for side in range(2):
            for pair in range(6):
                lanes = pl.ds(pair * LANES, LANES)
                mid, mix = fetch(16 * k, 16, first_pair[side] + pair)
                for core in range(2):
                    factor = f_gy[side][core]
                    give_gy[k, side, core, :, lanes] = (mid * factor[0] + mix * factor[1]).astype(BF16)

        def send(side):
            for core in range(2):
                send_sides[k][side][core].start()

        both_sides(send)

    def own_block(k):
        last_pass(k, wown, whole, 32, 0)
        for pair in range(32):
            lanes = pl.ds(pair * LANES, LANES)
            mid, mix = fetch(16 * k, 16, pair)
            out[0, 16 * k : 16 * k + 16, lanes] = mid
            give_own[16 * k : 16 * k + 16, lanes] = (mix * f_sib[1]).astype(BF16)
        share_own[k].start()

    def finish_own(k):
        share_own[k].wait_recv()
        rows = slice(16 * k, 16 * k + 16)
        out[0, rows] = (out[0, rows] + take_own[rows].astype(F32)) * (est[rows] * scale)

    for k in range(4):
        own_rows(k)
    pl.loop(0, VIEWS)(turn_inner)
    for k in range(4):
        own_block(k)
        if k:
            finish_own(k - 1)
    finish_own(3)

    def add_rows(rows, lanes):
        gap = jnp.zeros((16 - HALO, rows.shape[1]), F32)
        low_rows = jnp.concatenate([rows, gap], axis=0) * (row * scale)
        high_rows = jnp.concatenate([gap, rows], axis=0) * ((1.0 - row) * scale)
        out[0, 0:16, lanes] = out[0, 0:16, lanes] + low_rows * est[0:16, lanes]
        out[0, 48:64, lanes] = out[0, 48:64, lanes] + high_rows * est[48:64, lanes]

    final_gx.wait_recv()
    for q in range(4):
        add_rows(get_gx[...].astype(F32)[HALO * q : HALO * q + HALO], pl.ds(q * QUARTER, QUARTER))
    for side in range(2):

        @pl.when(exists[side])
        def _(side=side):
            arrived(13 + 1 - side, get_co.at[side])
            add_rows(get_co[side].astype(F32)[:HALO], toward[side])

    for k in range(4):
        for side in range(2):

            @pl.when(exists[side])
            def _(k=k, side=side):
                for core in range(2):
                    arrived(17 + 4 * k + 2 * (1 - side) + core, take_gy.at[k, side, core])
                rows = slice(16 * k, 16 * k + 16)
                total = take_gy[k, side, 0].astype(F32) + take_gy[k, side, 1].astype(F32)
                out[0, rows, toward[side]] = out[0, rows, toward[side]] + total * (
                    est[rows, toward[side]] * scale
                )

    for item in [send_sib, send_gx, pass_gx, share_gx, share_co, final_gx] + share_own:
        item.wait_send()

    def drain(side):
        items = [send_co[side], pass_co[side], final_co[side]]
        for k in range(4):
            items += [send_gy[k][side], pass_gy[k][side], *send_sides[k][side]]
        for item in items:
            item.wait_send()

    both_sides(drain)


def solution(mesh):
    n_gy = mesh.shape["gy"]

    def body(estimate, views_data, point_spread, block_owner):
        slab, ends = (48, QUARTER), (2, 16, WIDTH)
        sides = (4, 2, 2, 16, WIDTH)
        scratch = [
            ((64, 4096), F32),
            ((VIEWS, 64, 4096), BF16),
            ((64, 4096), BF16),
            ((64, 4096), BF16),
            (slab, BF16),
            ((2, *slab), BF16),
            ((2, 2, 64, WIDTH), BF16),
            ((2, *ends), BF16),
            ((SPAN_A * STEP_F, LANES), F32),
            ((SPAN_A * STEP_F, LANES), F32),
            ((512, CHUNK * LANES), BF16),
            ((VIEWS * 32 * STEP_T, LANES), F32),
            ((SPAN_A * STEP_V, LANES), F32),
            ((512, 96), BF16),
            ((96, 512), BF16),
            ((64, 512), BF16),
            ((32, 256), BF16),
            ((8, 256, 128), BF16),
            ((8, 128, 256), BF16),
            ((VIEWS, 64, 2 * SPAN_A), BF16),
            ((VIEWS, RANK * 64, 64), BF16),
            ((VIEWS, RANK * 16, 64), BF16),
            (slab, F32),
            (slab, F32),
            (ends, F32),
            ((64, 4096), BF16),
            (slab, BF16),
            (sides, BF16),
            (ends, BF16),
            ((64, 4096), BF16),
            (slab, BF16),
            (sides, BF16),
            (ends, BF16),
            (slab, BF16),
            (ends, BF16),
            (slab, BF16),
            (ends, BF16),
        ]
        far_spec = pl.BlockSpec(memory_space=pltpu.HBM)
        return pl.pallas_call(
            functools.partial(kernel, n_gy),
            out_shape=jax.ShapeDtypeStruct((1, 64, 4096), F32),
            in_specs=[far_spec] * 4,
            out_specs=pl.BlockSpec(memory_space=pltpu.VMEM),
            scratch_shapes=[pltpu.VMEM(shape, kind) for shape, kind in scratch]
            + [
                pltpu.SMEM((VIEWS, 3, RANK, TAPS), F32),
                pltpu.SMEM((2, PILLAR, n_gy), I32),
                pltpu.SemaphoreType.DMA((6,)),
                pltpu.SemaphoreType.DMA((53,)),
                pltpu.SemaphoreType.DMA((53,)),
            ],
            compiler_params=pltpu.CompilerParams(
                collective_id=0, has_side_effects=True, vmem_limit_bytes=52 * 2**20
            ),
        )(
            estimate,
            views_data,
            pltpu.with_memory_space_constraint(point_spread.transpose(0, 2, 1, 3), pltpu.HBM),
            pltpu.with_memory_space_constraint(block_owner.transpose(0, 2, 1), pltpu.HBM),
        )

    placed = (P(("gx", "gy", "gz"), None, None), P(None, ("gx", "gy", "gz"), None, None), P(), P())
    return jax.shard_map(
        body,
        mesh=mesh,
        in_specs=placed,
        out_specs=P(("gx", "gy", "gz"), None, None),
        check_vma=False,
    )
```

```python
import functools

import jax
import jax.numpy as jnp
from jax import lax
from jax.experimental import pallas as pl
from jax.experimental.pallas import tpu as pltpu
from jax.sharding import PartitionSpec as P

MESH = pl.DeviceIdType.MESH
F32, BF16, I32 = jnp.float32, jnp.bfloat16, jnp.int32
BLOCK, TAPS, HALO, RANK, VIEWS, PILLAR = 64, 23, 11, 2, 4, 4
FLOOR = 0.5
SPAN_A = 80
PAIRS = 48
STEP_F, STEP_T, STEP_V = 56, 168, 520
LANES = 128
WIDTH = 768
FACE = 3328
QUARTER = 1024
CHUNK = 16
DUO = 16


def iota(shape, dim):
    return lax.broadcasted_iota(I32, shape, dim)


def band(distance, tap):
    total = jnp.zeros(distance.shape, F32)
    for t in range(TAPS):
        total = jnp.where(distance == t, tap(t), total)
    return total


def ext_c(lane):
    return jnp.where(lane < 96, lane, lane - LANES)


def parity_b(row):
    return jnp.where(row < 32, 2 * row, 2 * row - 63)


def ext_b(row):
    odd = (row >= PAIRS).astype(I32)
    pair = row - PAIRS * odd
    value = 2 * pair + odd - 88 * (pair >= 38).astype(I32)
    return jnp.where(pair >= 44, 1000, value)


def tap_of(ps):
    def tap(number, axis):
        return lambda t: ps[number // RANK, axis, number % RANK, t]

    return tap


def build_forward(ps, wb, wct):
    tap = tap_of(ps)
    d_b = ext_b(iota((64, 96), 1)) - parity_b(iota((64, 96), 0)) + HALO
    d_ct = ext_c(iota((64, LANES), 1)) - iota((64, LANES), 0) + HALO
    wct[...] = jnp.zeros_like(wct)

    @pl.loop(0, VIEWS * RANK)
    def _(number):
        start = pl.multiple_of(number * 64, 64)
        wb[pl.ds(start, 64), :] = band(d_b, tap(number, 1)).astype(BF16)
        base = band(d_ct, tap(number, 2)).astype(BF16)
        wct[number, 0:64, 0:128] = base
        wct[number, 64:128, 128:256] = base


def build_rest(ps, mesh_row, wbt, wown, wside, wa, wat_own, wat_far):
    tap = tap_of(ps)
    col = iota((96, LANES), 1)
    high = col >= 64
    d_bt = ext_b(iota((96, LANES), 0)) - parity_b(jnp.where(high, col - 64, col)) + HALO
    for pair in range(VIEWS * RANK // 2):
        low_tap, high_tap = tap(2 * pair, 1), tap(2 * pair + 1, 1)
        wbt[:, pair * LANES : (pair + 1) * LANES] = band(
            d_bt, lambda t: jnp.where(high, high_tap(t), low_tap(t))
        ).astype(BF16)

    wown[0:32, :] = wbt[0:32, :]
    wown[32:64, :] = wbt[PAIRS : PAIRS + 32, :]

    line, col = iota((32, LANES), 0), iota((32, LANES), 1)
    line = jnp.where(line >= 16, line + PAIRS + 16, line + 32)
    odd, entry = (col & 31) >> 4, col & 15
    d_side = ext_b(line) - (2 * jnp.where(entry >= 8, entry + 16, entry) + odd) + HALO
    group = col >> 5
    for half in range(2):
        taps = [tap(4 * half + n, 1) for n in range(4)]
        wside[:, half * LANES : (half + 1) * LANES] = band(
            d_side,
            lambda t: jnp.where(
                group < 2,
                jnp.where(group == 0, taps[0](t), taps[1](t)),
                jnp.where(group == 2, taps[2](t), taps[3](t)),
            ),
        ).astype(BF16)

    def ext_a(place):
        inside = place - (64 + HALO) * (place >= 64).astype(I32) * mesh_row
        return jnp.where(place >= 64 + HALO, 1000, inside)

    second = iota((64, 2 * SPAN_A), 1) >= SPAN_A
    place = iota((64, 2 * SPAN_A), 1) - SPAN_A * second.astype(I32)
    d_a = ext_a(place) - iota((64, 2 * SPAN_A), 0) + HALO
    d_at = ext_a(iota((SPAN_A, 64), 0)) - iota((SPAN_A, 64), 1) + HALO

    @pl.loop(0, VIEWS)
    def _(view):
        first_tap, second_tap = tap(2 * view, 0), tap(2 * view + 1, 0)
        wa[view] = band(d_a, lambda t: jnp.where(second, second_tap(t), first_tap(t))).astype(BF16)
        for term, taps in enumerate((first_tap, second_tap)):
            base = band(d_at, taps).astype(BF16)
            wat_own[view, term * 64 : term * 64 + 64, :] = base[:64]
            wat_far[view, term * 16 : term * 16 + 16, :] = base[64:]


def kernel(
    n_gy,
    est_hbm,
    data_hbm,
    ps_hbm,
    owner_hbm,
    out,
    est,
    data,
    own,
    sib,
    slab,
    gx_in,
    gy_in,
    co_in,
    mid_f,
    mix_f,
    rows_t,
    t2,
    v2,
    wb,
    wbt,
    wown,
    wside,
    wct,
    wa,
    wat_own,
    wat_far,
    keep_gx,
    part_gx,
    keep_co,
    give_own,
    give_gx,
    give_gy,
    give_co,
    take_own,
    take_gx,
    take_gy,
    take_co,
    put_gx,
    put_co,
    get_gx,
    get_co,
    ps,
    owner,
    load_sem,
    send_sem,
    recv_sem,
):
    i, j, g = lax.axis_index("gx"), lax.axis_index("gy"), lax.axis_index("gz")
    sibling = (i, j, 1 - g)
    across = (1 - i, j, g)
    beside = [[(i, j + 2 * s - 1, g), (i, j + 2 * s - 1, 1 - g)] for s in range(2)]
    corner = [(1 - i, j + 2 * s - 1, g) for s in range(2)]
    exists = (j > 0, j < n_gy - 1)

    toward = (pl.ds(0, WIDTH), pl.ds(FACE, WIDTH))
    parts = (*toward, pl.ds(WIDTH, FACE - WIDTH))
    load_est = [
        pltpu.make_async_copy(est_hbm.at[0, :, p], est.at[:, p], load_sem.at[n])
        for n, p in enumerate(parts)
    ]
    load_data = pltpu.make_async_copy(data_hbm.at[:, 0], data, load_sem.at[3])
    load_owner = pltpu.make_async_copy(owner_hbm, owner, load_sem.at[4])
    load_ps = pltpu.make_async_copy(ps_hbm, ps, load_sem.at[5])
    for item in [*load_est, load_owner, load_ps, load_data]:
        item.start()

    def copy(number, src, dst, target):
        return pltpu.make_async_remote_copy(
            src_ref=src,
            dst_ref=dst,
            send_sem=send_sem.at[number],
            recv_sem=recv_sem.at[number],
            device_id=target,
            device_id_type=MESH,
        )

    def both_sides(action):
        for side in range(2):

            @pl.when(exists[side])
            def _(side=side):
                action(side)

    barrier = pltpu.get_barrier_semaphore()
    for target in (sibling, across):
        pl.semaphore_signal(barrier, inc=1, device_id=target, device_id_type=MESH)

    def greet(side):
        for target in (*beside[side], corner[side]):
            pl.semaphore_signal(barrier, inc=1, device_id=target, device_id_type=MESH)

    both_sides(greet)
    for item, lanes in zip(load_est[:2], toward):
        item.wait()
        own[:, lanes] = est[:, lanes].astype(BF16)
    waits = 2 + 3 * exists[0].astype(I32) + 3 * exists[1].astype(I32)
    pl.semaphore_wait(barrier, waits)

    inside = ((pl.ds(0, 16), pl.ds(0, WIDTH)), (pl.ds(32, 16), pl.ds(256, WIDTH)))
    send_sib = copy(0, own, sib, sibling)
    send_gx = copy(1, slab, gx_in.at[0], across)
    rows_of = [pl.ds(16 * k, 16) for k in range(4)]
    send_gy = [
        [
            copy(37 + 2 * k + s, own.at[rows_of[k], toward[s]], gy_in.at[1 - s, 0, rows_of[k]], beside[s][0])
            for s in range(2)
        ]
        for k in range(4)
    ]
    pass_gx = copy(4, gx_in.at[0], gx_in.at[1], sibling)
    pass_gy = [
        [
            copy(45 + 2 * k + s, gy_in.at[s, 0, rows_of[k]], gy_in.at[s, 1, rows_of[k]], sibling)
            for s in range(2)
        ]
        for k in range(4)
    ]
    send_co = [copy(7 + s, slab.at[*inside[s]], co_in.at[1 - s, 0], corner[s]) for s in range(2)]
    pass_co = [copy(9 + s, co_in.at[s, 0], co_in.at[s, 1], sibling) for s in range(2)]

    def arrived(number, dst):
        copy(number, dst, dst, sibling).wait_recv()


    def send_rows(side):
        for k in range(4):
            send_gy[k][side].start()

    both_sides(send_rows)
    load_est[2].wait()
    own[:, parts[2]] = est[:, parts[2]].astype(BF16)
    send_sib.start()

    row = i.astype(F32)
    edge = est[53:64, :] * (1.0 - row) + est[0:HALO, :] * row
    slab[...] = jnp.concatenate(
        [edge[:, q * QUARTER : (q + 1) * QUARTER] for q in range(4)] + [jnp.zeros((4, QUARTER), F32)],
        axis=0,
    ).astype(BF16)

    for side in range(2):

        @pl.when(jnp.logical_not(exists[side]))
        def _(side=side):
            gy_in[side] = jnp.zeros(gy_in.shape[1:], BF16)
            co_in[side] = jnp.zeros(co_in.shape[1:], BF16)

    load_owner.wait()
    load_ps.wait()

    def column(row, col):
        col = jnp.minimum(jnp.maximum(col, 0), n_gy - 1)
        codes = [owner[row, k, col] for k in range(PILLAR)]
        found = []
        for code in (g, 1 - g):
            hits = [(codes[k] == code).astype(I32) for k in range(PILLAR)]
            found.append((sum(hits), sum(k * hits[k] for k in range(PILLAR))))
        return found

    home = column(i, j)
    valid, height = home[0]

    def factors(entry, there=None):
        present, level = entry
        live = present * valid
        if there is not None:
            live = live * there.astype(I32)
        at = [(live * (level - height == d).astype(I32)).astype(F32) for d in (0, 1, -1)]
        lane_low = (iota((1, LANES), 1) & 63) < 32
        return at[0], jnp.where(lane_low, at[1], at[2])

    f_sib = factors(home[1])
    f_gx = [factors(e) for e in column(1 - i, j)]
    f_gy = [[factors(e, exists[s]) for e in column(i, j + 2 * s - 1)] for s in range(2)]
    f_co = [[factors(e, exists[s]) for e in column(1 - i, j + 2 * s - 1)] for s in range(2)]
    live = valid.astype(F32)

    build_forward(ps, wb, wct)
    send_gx.start()
    both_sides(lambda s: send_co[s].start())
    build_rest(ps, i, wbt, wown, wside, wa, wat_own, wat_far)

    def place(first_row, count, pair, mid, mix):
        mid_f[pl.ds(first_row * STEP_F + pair, count, stride=STEP_F), :] = mid
        mix_f[pl.ds(first_row * STEP_F + pair, count, stride=STEP_F), :] = mix

    def tile(number):
        return pl.ds(pl.multiple_of(number * LANES, LANES), LANES)

    def blend(pieces, factor):
        first, second = pieces[0].astype(F32), pieces[1].astype(F32)
        return (
            first * factor[0][0] + second * factor[1][0],
            first * factor[0][1] + second * factor[1][1],
        )

    for term in range(RANK):
        for unused in range(76, SPAN_A):
            start = term * SPAN_A + unused
            t2[pl.ds(start, VIEWS * 32, stride=STEP_T), :] = jnp.zeros((VIEWS * 32, LANES), F32)

    for pair in range(44, PAIRS):
        place(0, SPAN_A, pair, jnp.zeros((SPAN_A, LANES), F32), jnp.zeros((SPAN_A, LANES), F32))

    first_pair = (38, 32)

    send_sib.wait_recv()

    @pl.loop(0, 32)
    def _(pair):
        place(0, 64, pair, own[:, tile(pair)].astype(F32), sib[:, tile(pair)].astype(F32) * f_sib[1])

    def hand_on(k):
        for side in range(2):

            @pl.when(exists[side])
            def _(side=side):
                arrived(37 + 2 * k + 1 - side, gy_in.at[side, 0, rows_of[k]])
                pass_gy[k][side].start()

    def select_rows(k):
        both_sides(lambda s: pass_gy[k][s].wait_recv())
        for side in range(2):
            for pair in range(6):
                lanes = pl.ds(pair * LANES, LANES)
                mid, mix = blend([gy_in[side, c, rows_of[k], lanes] for c in range(2)], f_gy[side])
                place(16 * k, 16, first_pair[side] + pair, mid, mix)

    low = iota((PAIRS, LANES), 1) < 64

    def forward_chunk(chunk, count=CHUNK):
        for two in range(count // 2):
            parts = []
            for one in range(2):
                start = pl.multiple_of((chunk * CHUNK + two * 2 + one) * STEP_F, 8)
                mid, mix = mid_f[pl.ds(start, PAIRS), :], mix_f[pl.ds(start, PAIRS), :]
                even = jnp.where(low, mid, pltpu.roll(mix, 64, 1))
                odd = jnp.where(low, pltpu.roll(mid, 64, 1), mix)
                parts.append(jnp.concatenate([even, odd], axis=0).astype(BF16))
            first = jnp.dot(wb[...], jnp.concatenate(parts, axis=1), preferred_element_type=F32)
            rows_t[:, two * 256 : two * 256 + 256] = first.astype(BF16)
        for number in range(VIEWS * RANK):
            view, term = number // RANK, number % RANK
            top = number * 64
            block = jnp.concatenate(
                [
                    jnp.concatenate(
                        [
                            rows_t[top : top + 32, a * LANES : (a + 1) * LANES],
                            rows_t[top + 32 : top + 64, a * LANES : (a + 1) * LANES],
                        ],
                        axis=1,
                    )
                    for a in range(count)
                ],
                axis=0,
            )
            second = lax.dot_general(
                block, wct[number], (((1,), (1,)), ((), ())), preferred_element_type=F32
            )
            for a in range(count):
                start = view * 32 * STEP_T + term * SPAN_A + chunk * CHUNK + a
                t2[pl.ds(start, 32, stride=STEP_T), :] = second[a * 32 : a * 32 + 32, :]

    hand_on(0)
    for k in range(3):
        hand_on(k + 1)
        select_rows(k)
        forward_chunk(k)

    arrived(1, gx_in.at[0])
    pass_gx.start()

    for side in range(2):

        @pl.when(exists[side])
        def _(side=side):
            arrived(7 + 1 - side, co_in.at[side, 0])
            pass_co[side].start()

    select_rows(3)
    forward_chunk(3)

    pass_gx.wait_recv()
    both_sides(lambda s: pass_co[s].wait_recv())

    def lengthen(rows):
        return jnp.concatenate([rows, jnp.zeros((16 - HALO, rows.shape[1]), F32)], axis=0)

    for q in range(4):
        rows = [gx_in[k].astype(F32)[HALO * q : HALO * q + HALO] for k in range(2)]
        for number in range(8):
            lanes = slice(number * LANES, (number + 1) * LANES)
            mid, mix = blend([lengthen(rows[k][:, lanes]) for k in range(2)], f_gx)
            place(64, 16, q * 8 + number, mid, mix)

    for side in range(2):
        down = 1 - side
        for pair in range(6):
            lanes = slice(pair * LANES, (pair + 1) * LANES)
            rows = [co_in[side, k, :, lanes].astype(F32)[down : down + HALO] for k in range(2)]
            mid, mix = blend([lengthen(r) for r in rows], f_co[side])
            place(64, 16, first_pair[side] + pair, mid, mix)

    forward_chunk(64 // CHUNK, 12)
    load_data.wait()

    def adjoint_front(view, back, count, first, tiles):
        for term in range(RANK):
            rows = back[term * count : (term + 1) * count]
            block = jnp.concatenate(
                [rows[:, n * LANES : (n + 1) * LANES] for n in range(len(tiles))], axis=0
            )
            wide = jnp.dot(block, wct[view * RANK + term], preferred_element_type=F32)
            for n, k in enumerate(tiles):
                for odd in range(2):
                    at = first * STEP_V + (view * RANK + term) * 64 + odd * 32 + k
                    v2[pl.ds(at, count, stride=STEP_V), :] = wide[
                        n * count : (n + 1) * count, odd * LANES : (odd + 1) * LANES
                    ]

    def turn_far(view):
        start = pl.multiple_of(view * 32 * STEP_T, 8)
        fields = jnp.concatenate(
            [t2[pl.ds(start + k * STEP_T, 2 * SPAN_A), :].astype(BF16) for k in range(32)], axis=1
        )
        blurred = jnp.dot(wa[view], fields, preferred_element_type=F32)
        ratio = (data[view].astype(F32) / jnp.maximum(blurred, FLOOR)).astype(BF16)
        data[view] = ratio
        back = jnp.dot(wat_far[view], ratio, preferred_element_type=F32).astype(BF16)
        adjoint_front(view, back, 16, 64, range(32))

    def turn_near(view):
        ratio = jnp.concatenate([data[view, :, 0:1024], data[view, :, 3072:4096]], axis=1)
        back = jnp.dot(wat_own[view], ratio, preferred_element_type=F32).astype(BF16)
        adjoint_front(view, back, 64, 0, [*range(8), *range(24, 32)])

    def turn_inner(view):
        back = jnp.dot(wat_own[view], data[view, :, 1024:3072], preferred_element_type=F32)
        adjoint_front(view, back.astype(BF16), 64, 0, range(8, 24))

    pl.loop(0, VIEWS)(turn_far)

    def last_pass(step, weights, pieces, count, first, rows_done=DUO):
        start = step * DUO * STEP_V
        columns = []
        for k in range(rows_done):
            rows = [v2[pl.ds(start + k * STEP_V + at, size), :] for at, size in pieces]
            columns.append(jnp.concatenate(rows, axis=0).astype(BF16))
        spread = jnp.dot(
            weights[...], jnp.concatenate(columns, axis=1), preferred_element_type=F32
        )
        for k in range(rows_done):
            even = spread[0:count, k * LANES : (k + 1) * LANES]
            odd = spread[count : 2 * count, k * LANES : (k + 1) * LANES]
            near = iota((count, LANES), 1) < 64
            at = (step * DUO + k) * STEP_F + first
            mid_f[pl.ds(at, count), :] = jnp.where(near, even, pltpu.roll(odd, 64, 1))
            mix_f[pl.ds(at, count), :] = jnp.where(near, pltpu.roll(even, 64, 1), odd)

    whole = [(0, 512)]
    sides_only = [(at + edge, 8) for at in range(0, 512, 32) for edge in (0, 24)]

    def fetch(first_row, count, pair):
        at = pl.ds(first_row * STEP_F + pair, count, stride=STEP_F)
        return mid_f[at, :], mix_f[at, :]

    last_pass(64 // DUO, wbt, whole, PAIRS, 0, 12)
    for q in range(4):
        for number in range(8):
            lanes = slice(number * LANES, (number + 1) * LANES)
            mid, mix = fetch(64, 16, q * 8 + number)
            mid, mix = mid[:HALO], mix[:HALO]
            keep_gx[HALO * q : HALO * q + HALO, lanes] = mid * f_gx[0][0] + mix * f_gx[0][1]
            part_gx[HALO * q : HALO * q + HALO, lanes] = mid * f_gx[1][0] + mix * f_gx[1][1]
    keep_gx[44:48, :] = jnp.zeros((4, QUARTER), F32)
    part_gx[44:48, :] = jnp.zeros((4, QUARTER), F32)
    give_gx[...] = part_gx[...].astype(BF16)
    share_gx = copy(11, give_gx, take_gx, sibling)
    share_gx.start()

    for side in range(2):
        for pair in range(6):
            lanes = slice(pair * LANES, (pair + 1) * LANES)
            mid, mix = fetch(64, 16, first_pair[side] + pair)
            one, two = f_co[side]
            keep_co[side, :, lanes] = mid * one[0] + mix * one[1]
            give_co[side, :, lanes] = (mid * two[0] + mix * two[1]).astype(BF16)
    share_co = copy(12, give_co, take_co, sibling)
    share_co.start()
    final_gx = copy(16, put_gx, get_gx, across)
    final_co = [copy(13 + s, put_co.at[s], get_co.at[1 - s], corner[s]) for s in range(2)]

    def finish_gx():
        share_gx.wait_recv()
        put_gx[...] = (keep_gx[...] + take_gx[...].astype(F32)).astype(BF16)
        final_gx.start()
        share_co.wait_recv()
        put_co[...] = (keep_co[...] + take_co[...].astype(F32)).astype(BF16)
        both_sides(lambda s: final_co[s].start())

    pl.loop(0, 2)(turn_near)
    finish_gx()
    pl.loop(2, VIEWS)(turn_near)

    scale = live / VIEWS
    send_sides = [
        [
            [
                copy(17 + 4 * k + 2 * s + c, give_gy.at[k, s, c], take_gy.at[k, 1 - s, c], beside[s][c])
                for c in range(2)
            ]
            for s in range(2)
        ]
        for k in range(4)
    ]
    share_own = [
        copy(33 + k, give_own.at[pl.ds(16 * k, 16)], take_own.at[pl.ds(16 * k, 16)], sibling)
        for k in range(4)
    ]

    def own_rows(k):
        last_pass(k, wside, sides_only, 16, 32)
        for side in range(2):
            for pair in range(6):
                lanes = pl.ds(pair * LANES, LANES)
                mid, mix = fetch(16 * k, 16, first_pair[side] + pair)
                for core in range(2):
                    factor = f_gy[side][core]
                    give_gy[k, side, core, :, lanes] = (mid * factor[0] + mix * factor[1]).astype(BF16)

        def send(side):
            for core in range(2):
                send_sides[k][side][core].start()

        both_sides(send)

    def own_block(k):
        last_pass(k, wown, whole, 32, 0)
        for pair in range(32):
            lanes = pl.ds(pair * LANES, LANES)
            mid, mix = fetch(16 * k, 16, pair)
            out[0, 16 * k : 16 * k + 16, lanes] = mid * (est[16 * k : 16 * k + 16, lanes] * scale)
            give_own[16 * k : 16 * k + 16, lanes] = (mix * f_sib[1]).astype(BF16)
        share_own[k].start()

    def finish_own(k):
        share_own[k].wait_recv()
        rows = slice(16 * k, 16 * k + 16)
        out[0, rows] = out[0, rows] + take_own[rows].astype(F32) * (est[rows] * scale)

    for k in range(4):
        own_rows(k)
    pl.loop(0, VIEWS)(turn_inner)
    for k in range(4):
        own_block(k)
        if k:
            finish_own(k - 1)

    def add_rows(rows, lanes):
        gap = jnp.zeros((16 - HALO, rows.shape[1]), F32)
        low_rows = jnp.concatenate([rows, gap], axis=0) * (row * scale)
        high_rows = jnp.concatenate([gap, rows], axis=0) * ((1.0 - row) * scale)
        out[0, 0:16, lanes] = out[0, 0:16, lanes] + low_rows * est[0:16, lanes]
        out[0, 48:64, lanes] = out[0, 48:64, lanes] + high_rows * est[48:64, lanes]

    final_gx.wait_recv()
    for q in range(4):
        add_rows(get_gx[...].astype(F32)[HALO * q : HALO * q + HALO], pl.ds(q * QUARTER, QUARTER))
    for side in range(2):

        @pl.when(exists[side])
        def _(side=side):
            arrived(13 + 1 - side, get_co.at[side])
            add_rows(get_co[side].astype(F32)[:HALO], toward[side])

    for k in range(4):
        for side in range(2):

            @pl.when(exists[side])
            def _(k=k, side=side):
                for core in range(2):
                    arrived(17 + 4 * k + 2 * (1 - side) + core, take_gy.at[k, side, core])
                rows = slice(16 * k, 16 * k + 16)
                total = take_gy[k, side, 0].astype(F32) + take_gy[k, side, 1].astype(F32)
                out[0, rows, toward[side]] = out[0, rows, toward[side]] + total * (
                    est[rows, toward[side]] * scale
                )

    finish_own(3)

    for item in [send_sib, send_gx, pass_gx, share_gx, share_co, final_gx] + share_own:
        item.wait_send()

    def drain(side):
        items = [send_co[side], pass_co[side], final_co[side]]
        for k in range(4):
            items += [send_gy[k][side], pass_gy[k][side], *send_sides[k][side]]
        for item in items:
            item.wait_send()

    both_sides(drain)


def solution(mesh):
    n_gy = mesh.shape["gy"]

    def body(estimate, views_data, point_spread, block_owner):
        slab, ends = (48, QUARTER), (2, 16, WIDTH)
        sides = (4, 2, 2, 16, WIDTH)
        scratch = [
            ((64, 4096), F32),
            ((VIEWS, 64, 4096), BF16),
            ((64, 4096), BF16),
            ((64, 4096), BF16),
            (slab, BF16),
            ((2, *slab), BF16),
            ((2, 2, 64, WIDTH), BF16),
            ((2, *ends), BF16),
            ((SPAN_A * STEP_F, LANES), F32),
            ((SPAN_A * STEP_F, LANES), F32),
            ((512, CHUNK * LANES), BF16),
            ((VIEWS * 32 * STEP_T, LANES), F32),
            ((SPAN_A * STEP_V, LANES), F32),
            ((512, 96), BF16),
            ((96, 512), BF16),
            ((64, 512), BF16),
            ((32, 256), BF16),
            ((8, 128, 256), BF16),
            ((VIEWS, 64, 2 * SPAN_A), BF16),
            ((VIEWS, RANK * 64, 64), BF16),
            ((VIEWS, RANK * 16, 64), BF16),
            (slab, F32),
            (slab, F32),
            (ends, F32),
            ((64, 4096), BF16),
            (slab, BF16),
            (sides, BF16),
            (ends, BF16),
            ((64, 4096), BF16),
            (slab, BF16),
            (sides, BF16),
            (ends, BF16),
            (slab, BF16),
            (ends, BF16),
            (slab, BF16),
            (ends, BF16),
        ]
        far_spec = pl.BlockSpec(memory_space=pltpu.HBM)
        return pl.pallas_call(
            functools.partial(kernel, n_gy),
            out_shape=jax.ShapeDtypeStruct((1, 64, 4096), F32),
            in_specs=[far_spec] * 4,
            out_specs=pl.BlockSpec(memory_space=pltpu.VMEM),
            scratch_shapes=[pltpu.VMEM(shape, kind) for shape, kind in scratch]
            + [
                pltpu.SMEM((VIEWS, 3, RANK, TAPS), F32),
                pltpu.SMEM((2, PILLAR, n_gy), I32),
                pltpu.SemaphoreType.DMA((6,)),
                pltpu.SemaphoreType.DMA((53,)),
                pltpu.SemaphoreType.DMA((53,)),
            ],
            compiler_params=pltpu.CompilerParams(
                collective_id=0, has_side_effects=True, vmem_limit_bytes=52 * 2**20
            ),
        )(
            estimate,
            views_data,
            pltpu.with_memory_space_constraint(point_spread.transpose(0, 2, 1, 3), pltpu.HBM),
            pltpu.with_memory_space_constraint(block_owner.transpose(0, 2, 1), pltpu.HBM),
        )

    placed = (P(("gx", "gy", "gz"), None, None), P(None, ("gx", "gy", "gz"), None, None), P(), P())
    return jax.shard_map(
        body,
        mesh=mesh,
        in_specs=placed,
        out_specs=P(("gx", "gy", "gz"), None, None),
        check_vma=False,
    )
```

```python
import functools

import jax
import jax.numpy as jnp
from jax import lax
from jax.experimental import pallas as pl
from jax.experimental.pallas import tpu as pltpu
from jax.sharding import PartitionSpec as P

MESH = pl.DeviceIdType.MESH
F32, BF16, I32 = jnp.float32, jnp.bfloat16, jnp.int32
BLOCK, TAPS, HALO, RANK, VIEWS, PILLAR = 64, 23, 11, 2, 4, 4
FLOOR = 0.5
SPAN_A = 80
PAIRS = 48
STEP_F, STEP_T, STEP_V = 56, 168, 520
LANES = 128
WIDTH = 768
FACE = 3328
QUARTER = 1024
CHUNK = 16
DUO = 16


def iota(shape, dim):
    return lax.broadcasted_iota(I32, shape, dim)


def band(distance, tap):
    total = jnp.zeros(distance.shape, F32)
    for t in range(TAPS):
        total = jnp.where(distance == t, tap(t), total)
    return total


def ext_c(lane):
    return jnp.where(lane < 96, lane, lane - LANES)


def parity_b(row):
    return jnp.where(row < 32, 2 * row, 2 * row - 63)


def ext_b(row):
    odd = (row >= PAIRS).astype(I32)
    pair = row - PAIRS * odd
    value = 2 * pair + odd - 88 * (pair >= 38).astype(I32)
    return jnp.where(pair >= 44, 1000, value)


def tap_of(ps):
    def tap(number, axis):
        return lambda t: ps[number // RANK, axis, number % RANK, t]

    return tap


def build_forward(ps, wb, wct):
    tap = tap_of(ps)
    d_b = ext_b(iota((64, 96), 1)) - parity_b(iota((64, 96), 0)) + HALO
    d_ct = ext_c(iota((64, LANES), 1)) - iota((64, LANES), 0) + HALO
    wct[...] = jnp.zeros_like(wct)

    @pl.loop(0, VIEWS * RANK)
    def _(number):
        start = pl.multiple_of(number * 64, 64)
        wb[pl.ds(start, 64), :] = band(d_b, tap(number, 1)).astype(BF16)
        base = band(d_ct, tap(number, 2)).astype(BF16)
        wct[number, 0:64, 0:128] = base
        wct[number, 64:128, 128:256] = base


def build_rest(ps, mesh_row, wbt, wown, wside, wa, wat_own, wat_far):
    tap = tap_of(ps)
    col = iota((96, LANES), 1)
    high = col >= 64
    d_bt = ext_b(iota((96, LANES), 0)) - parity_b(jnp.where(high, col - 64, col)) + HALO
    for pair in range(VIEWS * RANK // 2):
        low_tap, high_tap = tap(2 * pair, 1), tap(2 * pair + 1, 1)
        wbt[:, pair * LANES : (pair + 1) * LANES] = band(
            d_bt, lambda t: jnp.where(high, high_tap(t), low_tap(t))
        ).astype(BF16)

    wown[0:32, :] = wbt[0:32, :]
    wown[32:64, :] = wbt[PAIRS : PAIRS + 32, :]

    line, col = iota((32, LANES), 0), iota((32, LANES), 1)
    line = jnp.where(line >= 16, line + PAIRS + 16, line + 32)
    odd, entry = (col & 31) >> 4, col & 15
    d_side = ext_b(line) - (2 * jnp.where(entry >= 8, entry + 16, entry) + odd) + HALO
    group = col >> 5
    for half in range(2):
        taps = [tap(4 * half + n, 1) for n in range(4)]
        wside[:, half * LANES : (half + 1) * LANES] = band(
            d_side,
            lambda t: jnp.where(
                group < 2,
                jnp.where(group == 0, taps[0](t), taps[1](t)),
                jnp.where(group == 2, taps[2](t), taps[3](t)),
            ),
        ).astype(BF16)

    def ext_a(place):
        inside = place - (64 + HALO) * (place >= 64).astype(I32) * mesh_row
        return jnp.where(place >= 64 + HALO, 1000, inside)

    second = iota((64, 2 * SPAN_A), 1) >= SPAN_A
    place = iota((64, 2 * SPAN_A), 1) - SPAN_A * second.astype(I32)
    d_a = ext_a(place) - iota((64, 2 * SPAN_A), 0) + HALO
    d_at = ext_a(iota((SPAN_A, 64), 0)) - iota((SPAN_A, 64), 1) + HALO

    @pl.loop(0, VIEWS)
    def _(view):
        first_tap, second_tap = tap(2 * view, 0), tap(2 * view + 1, 0)
        wa[view] = band(d_a, lambda t: jnp.where(second, second_tap(t), first_tap(t))).astype(BF16)
        for term, taps in enumerate((first_tap, second_tap)):
            base = band(d_at, taps).astype(BF16)
            wat_own[view, term * 64 : term * 64 + 64, :] = base[:64]
            wat_far[view, term * 16 : term * 16 + 16, :] = base[64:]


def kernel(
    n_gy,
    est_hbm,
    data_hbm,
    ps_hbm,
    owner_hbm,
    out,
    est,
    data,
    own,
    sib,
    slab,
    gx_in,
    gy_in,
    co_in,
    mid_f,
    mix_f,
    rows_t,
    t2,
    v2,
    wb,
    wbt,
    wown,
    wside,
    wct,
    wa,
    wat_own,
    wat_far,
    keep_gx,
    part_gx,
    keep_co,
    give_own,
    give_gx,
    give_gy,
    give_co,
    take_own,
    take_gx,
    take_gy,
    take_co,
    put_gx,
    put_co,
    get_gx,
    get_co,
    ps,
    owner,
    load_sem,
    send_sem,
    recv_sem,
):
    i, j, g = lax.axis_index("gx"), lax.axis_index("gy"), lax.axis_index("gz")
    sibling = (i, j, 1 - g)
    across = (1 - i, j, g)
    beside = [[(i, j + 2 * s - 1, g), (i, j + 2 * s - 1, 1 - g)] for s in range(2)]
    corner = [(1 - i, j + 2 * s - 1, g) for s in range(2)]
    exists = (j > 0, j < n_gy - 1)

    toward = (pl.ds(0, WIDTH), pl.ds(FACE, WIDTH))
    parts = (*toward, pl.ds(WIDTH, FACE - WIDTH))
    load_est = [
        pltpu.make_async_copy(est_hbm.at[0, :, p], est.at[:, p], load_sem.at[n])
        for n, p in enumerate(parts)
    ]
    load_data = pltpu.make_async_copy(data_hbm.at[:, 0], data, load_sem.at[3])
    load_owner = pltpu.make_async_copy(owner_hbm, owner, load_sem.at[4])
    load_ps = pltpu.make_async_copy(ps_hbm, ps, load_sem.at[5])
    for item in [*load_est, load_owner, load_ps, load_data]:
        item.start()

    def copy(number, src, dst, target):
        return pltpu.make_async_remote_copy(
            src_ref=src,
            dst_ref=dst,
            send_sem=send_sem.at[number],
            recv_sem=recv_sem.at[number],
            device_id=target,
            device_id_type=MESH,
        )

    def both_sides(action):
        for side in range(2):

            @pl.when(exists[side])
            def _(side=side):
                action(side)

    barrier = pltpu.get_barrier_semaphore()
    for target in (sibling, across):
        pl.semaphore_signal(barrier, inc=1, device_id=target, device_id_type=MESH)

    def greet(side):
        for target in (*beside[side], corner[side]):
            pl.semaphore_signal(barrier, inc=1, device_id=target, device_id_type=MESH)

    both_sides(greet)
    for item, lanes in zip(load_est[:2], toward):
        item.wait()
        own[:, lanes] = est[:, lanes].astype(BF16)
    waits = 2 + 3 * exists[0].astype(I32) + 3 * exists[1].astype(I32)
    pl.semaphore_wait(barrier, waits)

    inside = ((pl.ds(0, 16), pl.ds(0, WIDTH)), (pl.ds(32, 16), pl.ds(256, WIDTH)))
    send_sib = copy(0, own, sib, sibling)
    send_gx = copy(1, slab, gx_in.at[0], across)
    rows_of = [pl.ds(16 * k, 16) for k in range(4)]
    send_gy = [
        [
            copy(37 + 2 * k + s, own.at[rows_of[k], toward[s]], gy_in.at[1 - s, 0, rows_of[k]], beside[s][0])
            for s in range(2)
        ]
        for k in range(4)
    ]
    pass_gx = copy(4, gx_in.at[0], gx_in.at[1], sibling)
    pass_gy = [
        [
            copy(45 + 2 * k + s, gy_in.at[s, 0, rows_of[k]], gy_in.at[s, 1, rows_of[k]], sibling)
            for s in range(2)
        ]
        for k in range(4)
    ]
    send_co = [copy(7 + s, slab.at[*inside[s]], co_in.at[1 - s, 0], corner[s]) for s in range(2)]
    pass_co = [copy(9 + s, co_in.at[s, 0], co_in.at[s, 1], sibling) for s in range(2)]

    def arrived(number, dst):
        copy(number, dst, dst, sibling).wait_recv()


    def send_rows(side):
        for k in range(4):
            send_gy[k][side].start()

    both_sides(send_rows)
    load_est[2].wait()
    own[:, parts[2]] = est[:, parts[2]].astype(BF16)
    send_sib.start()

    row = i.astype(F32)
    edge = est[53:64, :] * (1.0 - row) + est[0:HALO, :] * row
    slab[...] = jnp.concatenate(
        [edge[:, q * QUARTER : (q + 1) * QUARTER] for q in range(4)] + [jnp.zeros((4, QUARTER), F32)],
        axis=0,
    ).astype(BF16)

    for side in range(2):

        @pl.when(jnp.logical_not(exists[side]))
        def _(side=side):
            gy_in[side] = jnp.zeros(gy_in.shape[1:], BF16)
            co_in[side] = jnp.zeros(co_in.shape[1:], BF16)

    load_owner.wait()
    load_ps.wait()

    def column(row, col):
        col = jnp.minimum(jnp.maximum(col, 0), n_gy - 1)
        codes = [owner[row, k, col] for k in range(PILLAR)]
        found = []
        for code in (g, 1 - g):
            hits = [(codes[k] == code).astype(I32) for k in range(PILLAR)]
            found.append((sum(hits), sum(k * hits[k] for k in range(PILLAR))))
        return found

    home = column(i, j)
    valid, height = home[0]

    def factors(entry, there=None):
        present, level = entry
        live = present * valid
        if there is not None:
            live = live * there.astype(I32)
        at = [(live * (level - height == d).astype(I32)).astype(F32) for d in (0, 1, -1)]
        lane_low = (iota((1, LANES), 1) & 63) < 32
        return at[0], jnp.where(lane_low, at[1], at[2])

    f_sib = factors(home[1])
    f_gx = [factors(e) for e in column(1 - i, j)]
    f_gy = [[factors(e, exists[s]) for e in column(i, j + 2 * s - 1)] for s in range(2)]
    f_co = [[factors(e, exists[s]) for e in column(1 - i, j + 2 * s - 1)] for s in range(2)]
    live = valid.astype(F32)

    build_forward(ps, wb, wct)
    build_rest(ps, i, wbt, wown, wside, wa, wat_own, wat_far)
    send_gx.start()
    both_sides(lambda s: send_co[s].start())

    def place(first_row, count, pair, mid, mix):
        mid_f[pl.ds(first_row * STEP_F + pair, count, stride=STEP_F), :] = mid
        mix_f[pl.ds(first_row * STEP_F + pair, count, stride=STEP_F), :] = mix

    def tile(number):
        return pl.ds(pl.multiple_of(number * LANES, LANES), LANES)

    def blend(pieces, factor):
        first, second = pieces[0].astype(F32), pieces[1].astype(F32)
        return (
            first * factor[0][0] + second * factor[1][0],
            first * factor[0][1] + second * factor[1][1],
        )

    for term in range(RANK):
        for unused in range(76, SPAN_A):
            start = term * SPAN_A + unused
            t2[pl.ds(start, VIEWS * 32, stride=STEP_T), :] = jnp.zeros((VIEWS * 32, LANES), F32)

    for pair in range(44, PAIRS):
        place(0, SPAN_A, pair, jnp.zeros((SPAN_A, LANES), F32), jnp.zeros((SPAN_A, LANES), F32))

    first_pair = (38, 32)

    send_sib.wait_recv()

    @pl.loop(0, 32)
    def _(pair):
        place(0, 64, pair, own[:, tile(pair)].astype(F32), sib[:, tile(pair)].astype(F32) * f_sib[1])

    def hand_on(k):
        for side in range(2):

            @pl.when(exists[side])
            def _(side=side):
                arrived(37 + 2 * k + 1 - side, gy_in.at[side, 0, rows_of[k]])
                pass_gy[k][side].start()

    def select_rows(k):
        both_sides(lambda s: pass_gy[k][s].wait_recv())
        for side in range(2):
            for pair in range(6):
                lanes = pl.ds(pair * LANES, LANES)
                mid, mix = blend([gy_in[side, c, rows_of[k], lanes] for c in range(2)], f_gy[side])
                place(16 * k, 16, first_pair[side] + pair, mid, mix)

    low = iota((PAIRS, LANES), 1) < 64

    def forward_chunk(chunk, count=CHUNK):
        for two in range(count // 2):
            parts = []
            for one in range(2):
                start = pl.multiple_of((chunk * CHUNK + two * 2 + one) * STEP_F, 8)
                mid, mix = mid_f[pl.ds(start, PAIRS), :], mix_f[pl.ds(start, PAIRS), :]
                even = jnp.where(low, mid, pltpu.roll(mix, 64, 1))
                odd = jnp.where(low, pltpu.roll(mid, 64, 1), mix)
                parts.append(jnp.concatenate([even, odd], axis=0).astype(BF16))
            first = jnp.dot(wb[...], jnp.concatenate(parts, axis=1), preferred_element_type=F32)
            rows_t[:, two * 256 : two * 256 + 256] = first.astype(BF16)
        for number in range(VIEWS * RANK):
            view, term = number // RANK, number % RANK
            top = number * 64
            block = jnp.concatenate(
                [
                    jnp.concatenate(
                        [
                            rows_t[top : top + 32, a * LANES : (a + 1) * LANES],
                            rows_t[top + 32 : top + 64, a * LANES : (a + 1) * LANES],
                        ],
                        axis=1,
                    )
                    for a in range(count)
                ],
                axis=0,
            )
            second = lax.dot_general(
                block, wct[number], (((1,), (1,)), ((), ())), preferred_element_type=F32
            )
            for a in range(count):
                start = view * 32 * STEP_T + term * SPAN_A + chunk * CHUNK + a
                t2[pl.ds(start, 32, stride=STEP_T), :] = second[a * 32 : a * 32 + 32, :]

    hand_on(0)
    for k in range(3):
        hand_on(k + 1)
        select_rows(k)
        forward_chunk(k)

    arrived(1, gx_in.at[0])
    pass_gx.start()

    for side in range(2):

        @pl.when(exists[side])
        def _(side=side):
            arrived(7 + 1 - side, co_in.at[side, 0])
            pass_co[side].start()

    select_rows(3)
    forward_chunk(3)

    pass_gx.wait_recv()
    both_sides(lambda s: pass_co[s].wait_recv())

    def lengthen(rows):
        return jnp.concatenate([rows, jnp.zeros((16 - HALO, rows.shape[1]), F32)], axis=0)

    for q in range(4):
        rows = [gx_in[k].astype(F32)[HALO * q : HALO * q + HALO] for k in range(2)]
        for number in range(8):
            lanes = slice(number * LANES, (number + 1) * LANES)
            mid, mix = blend([lengthen(rows[k][:, lanes]) for k in range(2)], f_gx)
            place(64, 16, q * 8 + number, mid, mix)

    for side in range(2):
        down = 1 - side
        for pair in range(6):
            lanes = slice(pair * LANES, (pair + 1) * LANES)
            rows = [co_in[side, k, :, lanes].astype(F32)[down : down + HALO] for k in range(2)]
            mid, mix = blend([lengthen(r) for r in rows], f_co[side])
            place(64, 16, first_pair[side] + pair, mid, mix)

    forward_chunk(64 // CHUNK, 12)
    load_data.wait()

    def adjoint_front(view, back, count, first, tiles):
        for term in range(RANK):
            rows = back[term * count : (term + 1) * count]
            block = jnp.concatenate(
                [rows[:, n * LANES : (n + 1) * LANES] for n in range(len(tiles))], axis=0
            )
            wide = jnp.dot(block, wct[view * RANK + term], preferred_element_type=F32)
            for n, k in enumerate(tiles):
                for odd in range(2):
                    at = first * STEP_V + (view * RANK + term) * 64 + odd * 32 + k
                    v2[pl.ds(at, count, stride=STEP_V), :] = wide[
                        n * count : (n + 1) * count, odd * LANES : (odd + 1) * LANES
                    ]

    def turn_far(view):
        start = pl.multiple_of(view * 32 * STEP_T, 8)
        fields = jnp.concatenate(
            [t2[pl.ds(start + k * STEP_T, 2 * SPAN_A), :].astype(BF16) for k in range(32)], axis=1
        )
        blurred = jnp.dot(wa[view], fields, preferred_element_type=F32)
        ratio = (data[view].astype(F32) / jnp.maximum(blurred, FLOOR)).astype(BF16)
        data[view] = ratio
        back = jnp.dot(wat_far[view], ratio, preferred_element_type=F32).astype(BF16)
        adjoint_front(view, back, 16, 64, range(32))

    def turn_near(view):
        ratio = jnp.concatenate([data[view, :, 0:1024], data[view, :, 3072:4096]], axis=1)
        back = jnp.dot(wat_own[view], ratio, preferred_element_type=F32).astype(BF16)
        adjoint_front(view, back, 64, 0, [*range(8), *range(24, 32)])

    def turn_inner(view):
        back = jnp.dot(wat_own[view], data[view, :, 1024:3072], preferred_element_type=F32)
        adjoint_front(view, back.astype(BF16), 64, 0, range(8, 24))

    pl.loop(0, VIEWS)(turn_far)

    def last_pass(step, weights, pieces, count, first, rows_done=DUO):
        start = step * DUO * STEP_V
        columns = []
        for k in range(rows_done):
            rows = [v2[pl.ds(start + k * STEP_V + at, size), :] for at, size in pieces]
            columns.append(jnp.concatenate(rows, axis=0).astype(BF16))
        spread = jnp.dot(
            weights[...], jnp.concatenate(columns, axis=1), preferred_element_type=F32
        )
        for k in range(rows_done):
            even = spread[0:count, k * LANES : (k + 1) * LANES]
            odd = spread[count : 2 * count, k * LANES : (k + 1) * LANES]
            near = iota((count, LANES), 1) < 64
            at = (step * DUO + k) * STEP_F + first
            mid_f[pl.ds(at, count), :] = jnp.where(near, even, pltpu.roll(odd, 64, 1))
            mix_f[pl.ds(at, count), :] = jnp.where(near, pltpu.roll(even, 64, 1), odd)

    whole = [(0, 512)]
    sides_only = [(at + edge, 8) for at in range(0, 512, 32) for edge in (0, 24)]

    def fetch(first_row, count, pair):
        at = pl.ds(first_row * STEP_F + pair, count, stride=STEP_F)
        return mid_f[at, :], mix_f[at, :]

    last_pass(64 // DUO, wbt, whole, PAIRS, 0, 12)
    for q in range(4):
        for number in range(8):
            lanes = slice(number * LANES, (number + 1) * LANES)
            mid, mix = fetch(64, 16, q * 8 + number)
            mid, mix = mid[:HALO], mix[:HALO]
            keep_gx[HALO * q : HALO * q + HALO, lanes] = mid * f_gx[0][0] + mix * f_gx[0][1]
            part_gx[HALO * q : HALO * q + HALO, lanes] = mid * f_gx[1][0] + mix * f_gx[1][1]
    keep_gx[44:48, :] = jnp.zeros((4, QUARTER), F32)
    part_gx[44:48, :] = jnp.zeros((4, QUARTER), F32)
    give_gx[...] = part_gx[...].astype(BF16)
    share_gx = copy(11, give_gx, take_gx, sibling)
    share_gx.start()

    for side in range(2):
        for pair in range(6):
            lanes = slice(pair * LANES, (pair + 1) * LANES)
            mid, mix = fetch(64, 16, first_pair[side] + pair)
            one, two = f_co[side]
            keep_co[side, :, lanes] = mid * one[0] + mix * one[1]
            give_co[side, :, lanes] = (mid * two[0] + mix * two[1]).astype(BF16)
    share_co = copy(12, give_co, take_co, sibling)
    share_co.start()
    final_gx = copy(16, put_gx, get_gx, across)
    final_co = [copy(13 + s, put_co.at[s], get_co.at[1 - s], corner[s]) for s in range(2)]

    def finish_gx():
        share_gx.wait_recv()
        put_gx[...] = (keep_gx[...] + take_gx[...].astype(F32)).astype(BF16)
        final_gx.start()
        share_co.wait_recv()
        put_co[...] = (keep_co[...] + take_co[...].astype(F32)).astype(BF16)
        both_sides(lambda s: final_co[s].start())

    pl.loop(0, 2)(turn_near)
    finish_gx()
    pl.loop(2, VIEWS)(turn_near)

    scale = live / VIEWS
    send_sides = [
        [
            [
                copy(17 + 4 * k + 2 * s + c, give_gy.at[k, s, c], take_gy.at[k, 1 - s, c], beside[s][c])
                for c in range(2)
            ]
            for s in range(2)
        ]
        for k in range(4)
    ]
    share_own = [
        copy(33 + k, give_own.at[pl.ds(16 * k, 16)], take_own.at[pl.ds(16 * k, 16)], sibling)
        for k in range(4)
    ]

    def own_rows(k):
        last_pass(k, wside, sides_only, 16, 32)
        for side in range(2):
            for pair in range(6):
                lanes = pl.ds(pair * LANES, LANES)
                mid, mix = fetch(16 * k, 16, first_pair[side] + pair)
                for core in range(2):
                    factor = f_gy[side][core]
                    give_gy[k, side, core, :, lanes] = (mid * factor[0] + mix * factor[1]).astype(BF16)

        def send(side):
            for core in range(2):
                send_sides[k][side][core].start()

        both_sides(send)

    def own_block(k):
        last_pass(k, wown, whole, 32, 0)
        for pair in range(32):
            lanes = pl.ds(pair * LANES, LANES)
            mid, mix = fetch(16 * k, 16, pair)
            out[0, 16 * k : 16 * k + 16, lanes] = mid * (est[16 * k : 16 * k + 16, lanes] * scale)
            give_own[16 * k : 16 * k + 16, lanes] = (mix * f_sib[1]).astype(BF16)
        share_own[k].start()

    def finish_own(k):
        share_own[k].wait_recv()
        rows = slice(16 * k, 16 * k + 16)
        out[0, rows] = out[0, rows] + take_own[rows].astype(F32) * (est[rows] * scale)

    for k in range(4):
        own_rows(k)
    pl.loop(0, VIEWS)(turn_inner)
    for k in range(4):
        own_block(k)
        if k:
            finish_own(k - 1)

    def add_rows(rows, lanes):
        gap = jnp.zeros((16 - HALO, rows.shape[1]), F32)
        low_rows = jnp.concatenate([rows, gap], axis=0) * (row * scale)
        high_rows = jnp.concatenate([gap, rows], axis=0) * ((1.0 - row) * scale)
        out[0, 0:16, lanes] = out[0, 0:16, lanes] + low_rows * est[0:16, lanes]
        out[0, 48:64, lanes] = out[0, 48:64, lanes] + high_rows * est[48:64, lanes]

    final_gx.wait_recv()
    for q in range(4):
        add_rows(get_gx[...].astype(F32)[HALO * q : HALO * q + HALO], pl.ds(q * QUARTER, QUARTER))
    for side in range(2):

        @pl.when(exists[side])
        def _(side=side):
            arrived(13 + 1 - side, get_co.at[side])
            add_rows(get_co[side].astype(F32)[:HALO], toward[side])

    for k in range(4):
        for side in range(2):

            @pl.when(exists[side])
            def _(k=k, side=side):
                for core in range(2):
                    arrived(17 + 4 * k + 2 * (1 - side) + core, take_gy.at[k, side, core])
                rows = slice(16 * k, 16 * k + 16)
                total = take_gy[k, side, 0].astype(F32) + take_gy[k, side, 1].astype(F32)
                out[0, rows, toward[side]] = out[0, rows, toward[side]] + total * (
                    est[rows, toward[side]] * scale
                )

    finish_own(3)

    for item in [send_sib, send_gx, pass_gx, share_gx, share_co, final_gx] + share_own:
        item.wait_send()

    def drain(side):
        items = [send_co[side], pass_co[side], final_co[side]]
        for k in range(4):
            items += [send_gy[k][side], pass_gy[k][side], *send_sides[k][side]]
        for item in items:
            item.wait_send()

    both_sides(drain)


def solution(mesh):
    n_gy = mesh.shape["gy"]

    def body(estimate, views_data, point_spread, block_owner):
        slab, ends = (48, QUARTER), (2, 16, WIDTH)
        sides = (4, 2, 2, 16, WIDTH)
        scratch = [
            ((64, 4096), F32),
            ((VIEWS, 64, 4096), BF16),
            ((64, 4096), BF16),
            ((64, 4096), BF16),
            (slab, BF16),
            ((2, *slab), BF16),
            ((2, 2, 64, WIDTH), BF16),
            ((2, *ends), BF16),
            ((SPAN_A * STEP_F, LANES), F32),
            ((SPAN_A * STEP_F, LANES), F32),
            ((512, CHUNK * LANES), BF16),
            ((VIEWS * 32 * STEP_T, LANES), F32),
            ((SPAN_A * STEP_V, LANES), F32),
            ((512, 96), BF16),
            ((96, 512), BF16),
            ((64, 512), BF16),
            ((32, 256), BF16),
            ((8, 128, 256), BF16),
            ((VIEWS, 64, 2 * SPAN_A), BF16),
            ((VIEWS, RANK * 64, 64), BF16),
            ((VIEWS, RANK * 16, 64), BF16),
            (slab, F32),
            (slab, F32),
            (ends, F32),
            ((64, 4096), BF16),
            (slab, BF16),
            (sides, BF16),
            (ends, BF16),
            ((64, 4096), BF16),
            (slab, BF16),
            (sides, BF16),
            (ends, BF16),
            (slab, BF16),
            (ends, BF16),
            (slab, BF16),
            (ends, BF16),
        ]
        far_spec = pl.BlockSpec(memory_space=pltpu.HBM)
        return pl.pallas_call(
            functools.partial(kernel, n_gy),
            out_shape=jax.ShapeDtypeStruct((1, 64, 4096), F32),
            in_specs=[far_spec] * 4,
            out_specs=pl.BlockSpec(memory_space=pltpu.VMEM),
            scratch_shapes=[pltpu.VMEM(shape, kind) for shape, kind in scratch]
            + [
                pltpu.SMEM((VIEWS, 3, RANK, TAPS), F32),
                pltpu.SMEM((2, PILLAR, n_gy), I32),
                pltpu.SemaphoreType.DMA((6,)),
                pltpu.SemaphoreType.DMA((53,)),
                pltpu.SemaphoreType.DMA((53,)),
            ],
            compiler_params=pltpu.CompilerParams(
                collective_id=0, has_side_effects=True, vmem_limit_bytes=52 * 2**20
            ),
        )(
            estimate,
            views_data,
            pltpu.with_memory_space_constraint(point_spread.transpose(0, 2, 1, 3), pltpu.HBM),
            pltpu.with_memory_space_constraint(block_owner.transpose(0, 2, 1), pltpu.HBM),
        )

    placed = (P(("gx", "gy", "gz"), None, None), P(None, ("gx", "gy", "gz"), None, None), P(), P())
    return jax.shard_map(
        body,
        mesh=mesh,
        in_specs=placed,
        out_specs=P(("gx", "gy", "gz"), None, None),
        check_vma=False,
    )
```
